32 devices in a mesh: fsdp: 8 (over y, x, core), rep: 4 (over z).
Axes of the slice: x: 2, y: 2, z: 4, core: 2. Of those that a mesh axis runs over, the one named last changes fastest.
Arguments:
- tokens: bfloat16 [65536, 768], P(('fsdp', 'rep')), may hold values from -6 to 6
- segment_ids: int32 [65536], P(('fsdp', 'rep')), may hold values from -1 to 8, as said below
- cotangent: bfloat16 [65536, 768], P(('fsdp', 'rep')), may hold values from -8 to 8
- norm_params: bfloat16 [4, 768], P(None, 'fsdp')
- qkv_weight: bfloat16 [768, 2304], P(None, 'fsdp'), may hold values from -0.21875 to 0.21875
- proj_weight: bfloat16 [768, 768], P(None, 'fsdp'), may hold values from -1.25 to 1.25
- up_weight: bfloat16 [768, 3072], P(None, 'fsdp'), may hold values from -0.21875 to 0.21875
- down_weight: bfloat16 [3072, 768], P(None, 'fsdp'), may hold values from -0.109375 to 0.109375
- target_norms: float32 [4, 768], P(None, 'fsdp'), may hold values from -3 to 3
- target_qkv: float32 [768, 2304], P(None, 'fsdp'), may hold values from -0.21875 to 0.21875
- target_proj: float32 [768, 768], P(None, 'fsdp'), may hold values from -1.25 to 1.25
- target_up: float32 [768, 3072], P(None, 'fsdp'), may hold values from -0.21875 to 0.21875
- target_down: float32 [3072, 768], P(None, 'fsdp'), may hold values from -0.109375 to 0.109375
Outputs:
- block_output: bfloat16 [65536, 768], P(('fsdp', 'rep'))
- input_grad: bfloat16 [65536, 768], P(('fsdp', 'rep'))
- norm_grad: float32 [4, 768], P(None, 'fsdp')
- qkv_grad: float32 [768, 2304], P(None, 'fsdp')
- proj_grad: float32 [768, 768], P(None, 'fsdp')
- up_grad: float32 [768, 3072], P(None, 'fsdp')
- down_grad: float32 [3072, 768], P(None, 'fsdp')
- new_target_norms: float32 [4, 768], P(None, 'fsdp')
- new_target_qkv: float32 [768, 2304], P(None, 'fsdp')
- new_target_proj: float32 [768, 768], P(None, 'fsdp')
- new_target_up: float32 [768, 3072], P(None, 'fsdp')
- new_target_down: float32 [3072, 768], P(None, 'fsdp')
The draws below stay inside these ranges and needn't reach their ends.
Inputs may be any that keep to these rules, and one draw needn't show every extreme that they name: `segment_ids`: in each packed row of 1024 slots, images fill consecutive slots from the row's start with ids 0, 1, 2, ... in order; each image has 98 to 196 slots and one image of each row has exactly 196; the remaining slots at the row's end are -1. In the first packed row all images except the one of 196 slots have exactly 98 slots.
All inputs are finite; a program needn't handle non-finite values.
Results may differ from the reference program's by a relative error of at most 0.014.
Values may be sent and summed in bfloat16 or wider, within the bound.
No kernel may reach another device: no remote copies, remote signals or barrier semaphores. Data moves between devices by JAX's collectives and lax.ppermute only.
A program may use at most 256 MiB of HBM per device.

```python
import jax
import jax.numpy as jnp
from jax import lax

D = 768
HEAD = 64
FF = 3072
ROW_LEN = 1024
MAXLEN = 196
TOKENS = 65536


def draw_segment_ids(key, part):
    rows = TOKENS // ROW_LEN
    count = ROW_LEN // (MAXLEN // 2) + 1
    key_len = jax.random.fold_in(key, 11)
    key_pick = jax.random.fold_in(key, 12)
    sizes = jax.random.randint(key_len, (rows, count), MAXLEN // 2, MAXLEN + 1).astype(jnp.int32)
    row_index = jnp.arange(rows, dtype=jnp.int32)[:, None]
    sizes = jnp.where(row_index == 0, MAXLEN // 2, sizes).astype(jnp.int32)
    pick = jax.random.randint(key_pick, (rows, 1), 0, 2).astype(jnp.int32)
    place = jnp.arange(count, dtype=jnp.int32)[None, :]
    sizes = jnp.where(place == pick, MAXLEN, sizes).astype(jnp.int32)
    ends = jnp.cumsum(sizes, axis=1).astype(jnp.int32)
    slots = jnp.arange(ROW_LEN, dtype=jnp.int32)[None, :, None]
    ident = jnp.sum((slots >= ends[:, None, :]).astype(jnp.int32), axis=2).astype(jnp.int32)
    closing = jnp.take_along_axis(ends, jnp.minimum(ident, count - 1), axis=1)
    fits = closing <= ROW_LEN
    return jnp.where(fits, ident, -1).reshape(-1).astype(jnp.int32)


def draw_norm_params(key, part):
    key_gain = jax.random.fold_in(key, 21)
    key_shift = jax.random.fold_in(key, 22)
    gains = jax.random.uniform(key_gain, (2, D), jnp.float32, 0.5, 1.5)
    shifts = 0.5 * jax.random.normal(key_shift, (2, D), jnp.float32)
    stacked = jnp.stack([gains[0], shifts[0], gains[1], shifts[1]])
    return stacked.astype(jnp.bfloat16)


def spiked(values, own_key, source, target, blocks, factor):
    def block_of(position):
        return (jnp.arange(values.shape[position]) // (values.shape[position] // blocks)).reshape((-1,) + (1,) * (values.ndim - 1 - position))

    first = jax.random.permutation(own_key, blocks)[block_of(target)]
    far = (block_of(target) + blocks // 2) % blocks
    return jnp.where((block_of(source) == first) | (block_of(source) == far), factor * values, values)


def block_levels(own_key, dims, pieces, smallest, largest):
    level = 1.0
    for dim, shards_of in pieces:
        heights = jax.random.uniform(jax.random.fold_in(jax.random.fold_in(own_key, 6), dim), (shards_of,), jnp.float32, smallest / len(pieces), largest / len(pieces))
        level = level * jnp.repeat(jnp.exp(heights), dims[dim] // shards_of).reshape((-1,) + (1,) * (len(dims) - 1 - dim))
    return level


def centred(rng, extent, scale, reach, shards=(), kind=jnp.bfloat16):
    values = scale * jax.random.normal(rng, extent, jnp.float32)
    if shards:
        values = values * block_levels(rng, extent, shards, -0.22, 0.18)
    return jnp.clip(values, -reach, reach).astype(kind)


def bell_draw_with(rng, shape, scale, most, split, heavy, held_as=jnp.bfloat16):
    values = scale * jax.random.normal(rng, shape, jnp.float32)
    if split:
        values = values * block_levels(rng, shape, split, -0.22, 0.18)
    return jnp.clip(spiked(values, jax.random.fold_in(rng, 3), *heavy), -most, most).astype(held_as)


def setup_inputs(seed: int = 0) -> dict:
    key_of = jax.random.split(jax.random.key(seed), 14)
    return {
        "tokens": centred(key_of[0], (TOKENS, D), 1.0, 6.0, ((0, 32),)),
        "segment_ids": draw_segment_ids(jax.random.fold_in(key_of[13], 71), 0),
        "cotangent": bell_draw_with(key_of[2], (TOKENS, D), 1.0, 8.0, ((0, 32),), (0, 1, 32, 2.75)),
        "norm_params": draw_norm_params(jax.random.fold_in(key_of[13], 71), 0),
        "qkv_weight": centred(key_of[4], (D, 3 * D), D ** -0.5, 0.21875, ((1, 8),)),
        "proj_weight": centred(key_of[5], (D, D), (D // 32) ** -0.5, 1.25, ((1, 8),)),
        "up_weight": centred(key_of[6], (D, FF), D ** -0.5, 0.21875, ((1, 8),)),
        "down_weight": centred(key_of[7], (FF, D), FF ** -0.5, 0.109375, ((1, 8),)),
        "target_norms": centred(key_of[8], (4, D), 0.5, 3.0, ((1, 8),), jnp.float32),
        "target_qkv": centred(key_of[9], (D, 3 * D), D ** -0.5, 0.21875, ((1, 8),), jnp.float32),
        "target_proj": centred(key_of[10], (D, D), (D // 32) ** -0.5, 1.25, ((1, 8),), jnp.float32),
        "target_up": centred(key_of[11], (D, FF), D ** -0.5, 0.21875, ((1, 8),), jnp.float32),
        "target_down": centred(key_of[12], (FF, D), FF ** -0.5, 0.109375, ((1, 8),), jnp.float32),
    }


@jax.custom_vjp
def low(v):
    return lax.optimization_barrier(v.astype(jnp.bfloat16)).astype(jnp.float32)

@jax.custom_vjp
def low_back(v):
    return v

def low_keep(v):
    return (low(v), None)

def low_pass(kept, grad):
    return (grad,)

def back_keep(v):
    return (v, None)

def back_low(kept, grad):
    return (low(grad),)
low.defvjp(low_keep, low_pass)
low_back.defvjp(back_keep, back_low)
layer_eps = 1e-06
ema_rate = 0.75

def layer_norm(values, gain, shift):
    center = values - lax.optimization_barrier(jnp.mean(values, axis=-1, keepdims=True))
    spread = lax.optimization_barrier(jnp.mean(center * center, axis=-1, keepdims=True))
    return center * lax.rsqrt(spread + layer_eps) * gain + shift

def mixed(left, right):
    return jnp.dot(left, right, precision=lax.Precision.HIGHEST)

def row_forward(x_row, seg_row, params):
    norms, w_qkv, w_proj, w_up, w_down = params
    length, width = x_row.shape
    heads = width // HEAD
    valid = (seg_row >= 0).astype(x_row.dtype)[:, None]
    first = low(layer_norm(x_row, norms[0], norms[1]))
    qkv = low_back(low(mixed(first, w_qkv)))
    query = qkv[:, :width].reshape(length, heads, HEAD)
    keyset = qkv[:, width:2 * width].reshape(length, heads, HEAD)
    value = qkv[:, 2 * width:].reshape(length, heads, HEAD)
    scores = low_back(jnp.einsum('qhd,khd->hqk', query, keyset, precision=lax.Precision.HIGHEST) * 0.125)
    same = seg_row[:, None] == seg_row[None, :]
    scores = jnp.where(same[None], scores, -1e+30)
    top = lax.optimization_barrier(jnp.max(scores, axis=-1, keepdims=True))
    expo = jnp.exp(scores - top)
    probs = expo / lax.optimization_barrier(jnp.sum(expo, axis=-1, keepdims=True))
    attended = jnp.einsum('hqk,khd->qhd', low(probs), value, precision=lax.Precision.HIGHEST).reshape(length, width)
    attended = low_back(low(attended))
    middle = x_row + low_back(mixed(attended, w_proj))
    second = low(layer_norm(middle, norms[2], norms[3]))
    upper = low_back(mixed(second, w_up))
    activated = low(jax.nn.gelu(upper, approximate=False))
    return (middle + mixed(activated, w_down)) * valid

def forward(inputs, params, segments):
    rows = inputs.reshape(-1, ROW_LEN, inputs.shape[1])
    segs = segments.reshape(-1, ROW_LEN)
    step = jax.checkpoint(lambda x_row, seg_row: row_forward(x_row, seg_row, params))

    def scan_step(carry, item):
        return (carry, step(item[0], item[1]))
    _, outs = lax.scan(scan_step, None, (rows, segs))
    return outs.reshape(inputs.shape)

def reference(tokens, segment_ids, cotangent, norm_params, qkv_weight, proj_weight, up_weight, down_weight, target_norms, target_qkv, target_proj, target_up, target_down):
    inputs = tokens.astype(jnp.float32)
    params = (norm_params.astype(jnp.float32), qkv_weight.astype(jnp.float32), proj_weight.astype(jnp.float32), up_weight.astype(jnp.float32), down_weight.astype(jnp.float32))
    result, pull = jax.vjp(lambda a, b: forward(a, b, segment_ids), inputs, params)
    grad_inputs, grad_params = pull(cotangent.astype(jnp.float32))
    targets = (target_norms, target_qkv, target_proj, target_up, target_down)
    fresh = [ema_rate * t + (1.0 - ema_rate) * w for t, w in zip(targets, params)]
    return (result.astype(jnp.bfloat16), grad_inputs.astype(jnp.bfloat16), grad_params[0], grad_params[1], grad_params[2], grad_params[3], grad_params[4], fresh[0], fresh[1], fresh[2], fresh[3], fresh[4])
```

```python
import math
from functools import partial

import jax
import jax.numpy as jnp
from jax import lax
from jax.experimental import pallas as pl
from jax.experimental.pallas import tpu as pltpu
from jax.sharding import PartitionSpec as P

HEAD = 64
ROW_LEN = 1024
layer_eps = 1e-06
ema_rate = 0.75

BF = jnp.bfloat16
F32 = jnp.float32
NN = (((1,), (0,)), ((), ()))
NT = (((1,), (1,)), ((), ()))
TN = (((0,), (0,)), ((), ()))
VMEM_LIMIT = 66_000_000

QW = 256
KW = 224
FIT = KW - 15
KB = 128
STRIDE = 35


def mm(left, right, dims):
    return lax.dot_general(left, right, dims, preferred_element_type=F32)


def cost(flops, moved, exps=0):
    return pl.CostEstimate(flops=int(flops), bytes_accessed=int(moved), transcendentals=int(exps))


def job_table(segment_ids, rows, device):
    seg = segment_ids.reshape(rows, 1, ROW_LEN)
    ident = jnp.arange(16, dtype=jnp.int32)[None, :, None]
    real = seg >= 0
    starts = jnp.sum((real & (seg < ident)).astype(jnp.int32), axis=2)
    after = jnp.sum((real & (seg < ident + 1)).astype(jnp.int32), axis=2)
    images = jnp.max(seg, axis=2) + 1
    ends = jnp.where(jnp.arange(16, dtype=jnp.int32)[None, :] < images, after, ROW_LEN)
    valid = jnp.sum(real.astype(jnp.int32), axis=2)
    pad = ROW_LEN - valid
    fits = pad <= FIT
    jobs = images + jnp.where((pad > 0) & fits, 1, 0)
    wide = jnp.where(fits, 0, (pad + 15 + QW - 1) // QW)
    table = jnp.concatenate([starts, ends, jobs, valid, wide], axis=1).reshape(-1)
    return jnp.concatenate([table, device.astype(jnp.int32).reshape(1)])


def lane_of(count):
    return lax.broadcasted_iota(jnp.int32, (count, 128), 1)


def slot_of(count, base):
    return lax.broadcasted_iota(jnp.int32, (count, 128), 0) + base


def half_lanes(count, par):
    return (lane_of(count) < 64) if par == 0 else (lane_of(count) >= 64)


def spare_lane(count, par):
    return lane_of(count) == (64 if par == 0 else 0)


def query_side(q, par):
    n = q.shape[0]
    return jnp.where(half_lanes(n, par), q * BF(0.125), jnp.where(spare_lane(n, par), BF(1), BF(0)))


def key_side(k, par, inside):
    n = k.shape[0]
    return jnp.where(half_lanes(n, par), k, jnp.where(spare_lane(n, par) & (~inside), BF(-1e30), BF(0)))


def one_head(x, par):
    return jnp.where(half_lanes(x.shape[0], par), x, BF(0))


def image_window(tab, base, job):
    begin = tab[base + job]
    end = tab[base + 16 + job]
    low = lax.div(begin, 16) * 16
    q0 = pl.multiple_of(jnp.minimum(low, ROW_LEN - QW), 16)
    k0 = pl.multiple_of(jnp.minimum(low, ROW_LEN - KW), 16)
    return begin, end, q0, k0


def attend_kernel(pairs, row0, tab, q_ref, k_ref, v_ref, o_ref, a_sc):
    base = (pl.program_id(0) + row0) * STRIDE
    o_ref[...] = jnp.zeros_like(o_ref)

    def job(j, carry):
        begin, end, q0, k0 = image_window(tab, base, j)
        kr = slot_of(KW, k0)
        inside = (kr >= begin) & (kr < end)
        qr = slot_of(QW, q0)
        qin = (qr >= begin) & (qr < end)
        scores = []
        for p in range(pairs):
            cs = pl.ds(128 * p, 128)
            q = q_ref[pl.ds(q0, QW), cs]
            k = k_ref[pl.ds(k0, KW), cs]
            for par in range(2):
                scores.append(mm(key_side(k, par, inside), query_side(q, par), NT))
        probs = []
        for st in scores:
            expo = jnp.exp(st - jnp.max(st, axis=0, keepdims=True))
            total = jnp.sum(expo, axis=0, keepdims=True)
            probs.append((expo * (1.0 / total)).astype(BF))
        for p in range(pairs):
            cs = pl.ds(128 * p, 128)
            v = v_ref[pl.ds(k0, KW), cs]
            o = jnp.concatenate(
                [mm(v[:, 64 * par : 64 * par + 64], probs[2 * p + par], TN) for par in range(2)], axis=0
            ).T
            o_ref[pl.ds(q0, QW), cs] = jnp.where(qin, o.astype(BF), o_ref[pl.ds(q0, QW), cs])
        return carry

    lax.fori_loop(0, tab[base + 32], job, 0)

    start = tab[base + 33]
    low = lax.div(start, 16) * 16

    def wide(i, carry):
        q0 = pl.multiple_of(jnp.minimum(low + i * QW, ROW_LEN - QW), 16)
        qin = slot_of(QW, q0) >= start
        for p in range(pairs):
            cs = pl.ds(128 * p, 128)
            q = q_ref[pl.ds(q0, QW), cs]
            for par in range(2):
                qs = query_side(q, par)

                def block(kb):
                    k0 = pl.multiple_of(kb * KB, KB)
                    k = k_ref[pl.ds(k0, KB), cs]
                    return k0, mm(key_side(k, par, slot_of(KB, k0) >= start), qs, NT)

                def take_max(kb, top):
                    return jnp.maximum(top, jnp.max(block(kb)[1], axis=0, keepdims=True))

                top = lax.fori_loop(0, ROW_LEN // KB, take_max, jnp.full((1, QW), -1e30, F32))

                def take_sum(kb, total):
                    return total + jnp.sum(jnp.exp(block(kb)[1] - top), axis=0, keepdims=True)

                total = lax.fori_loop(0, ROW_LEN // KB, take_sum, jnp.zeros((1, QW), F32))
                a_sc[...] = jnp.zeros_like(a_sc)

                def take_out(kb, c):
                    k0, st = block(kb)
                    prob = (jnp.exp(st - top) * (1.0 / total)).astype(BF)
                    a_sc[...] += mm(one_head(v_ref[pl.ds(k0, KB), cs], par), prob, TN)
                    return c

                lax.fori_loop(0, ROW_LEN // KB, take_out, 0)
                hit = qin & half_lanes(QW, par)
                o_ref[pl.ds(q0, QW), cs] = jnp.where(hit, a_sc[...].T.astype(BF), o_ref[pl.ds(q0, QW), cs])
        return carry

    lax.fori_loop(0, tab[base + 34], wide, 0)


def attend_back_kernel(pairs, row0, tab, q_ref, k_ref, v_ref, d_ref, *rest):
    dq_ref, dk_ref, dv_ref, a_sc, dk_sc, dv_sc = rest[-6:]
    base = (pl.program_id(0) + row0) * STRIDE
    dq_ref[...] = jnp.zeros_like(dq_ref)
    dk_ref[...] = jnp.zeros_like(dk_ref)
    dv_ref[...] = jnp.zeros_like(dv_ref)

    def job(j, carry):
        begin, end, q0, k0 = image_window(tab, base, j)
        kr = slot_of(KW, k0)
        inside = (kr >= begin) & (kr < end)
        qr = slot_of(QW, q0)
        qin = (qr >= begin) & (qr < end)
        ks = pl.ds(k0, KW)
        qs = pl.ds(q0, QW)
        scores = []
        grads = []
        for p in range(pairs):
            cs = pl.ds(128 * p, 128)
            q = q_ref[qs, cs]
            k = k_ref[ks, cs]
            v = v_ref[ks, cs]
            d = jnp.where(qin, d_ref[qs, cs], BF(0))
            for par in range(2):
                scores.append(mm(key_side(k, par, inside), query_side(q, par), NT))
                grads.append(mm(v, one_head(d, par), NT))
        probs = []
        dscores = []
        for st, dp in zip(scores, grads):
            expo = jnp.exp(st - jnp.max(st, axis=0, keepdims=True))
            total = jnp.sum(expo, axis=0, keepdims=True)
            prob = expo * (1.0 / total)
            center = jnp.sum(prob * dp, axis=0, keepdims=True)
            dscores.append((prob * (dp - center)).astype(BF))
            probs.append(prob.astype(BF))
        for p in range(pairs):
            cs = pl.ds(128 * p, 128)
            q = q_ref[qs, cs]
            k = k_ref[ks, cs]
            d = jnp.where(qin, d_ref[qs, cs], BF(0))
            dv = mm(probs[2 * p], one_head(d, 0), NN) + mm(probs[2 * p + 1], one_head(d, 1), NN)
            dk = mm(dscores[2 * p], one_head(q, 0), NN) + mm(dscores[2 * p + 1], one_head(q, 1), NN)
            dq = jnp.concatenate(
                [mm(k[:, 64 * par : 64 * par + 64], dscores[2 * p + par], TN) for par in range(2)], axis=0
            ).T
            dq_ref[qs, cs] = jnp.where(qin, (dq * 0.125).astype(BF), dq_ref[qs, cs])
            dk_ref[ks, cs] = jnp.where(inside, (dk * 0.125).astype(BF), dk_ref[ks, cs])
            dv_ref[ks, cs] = jnp.where(inside, dv.astype(BF), dv_ref[ks, cs])
        return carry

    lax.fori_loop(0, tab[base + 32], job, 0)

    start = tab[base + 33]
    low = lax.div(start, 16) * 16
    windows = tab[base + 34]
    for p in range(pairs):
        cs = pl.ds(128 * p, 128)

        @pl.when(windows > 0)
        def _():
            dk_sc[...] = jnp.zeros_like(dk_sc)
            dv_sc[...] = jnp.zeros_like(dv_sc)

        def wide(i, carry):
            first = jnp.maximum(start, low + i * QW)
            q0 = pl.multiple_of(jnp.minimum(low + i * QW, ROW_LEN - QW), 16)
            qin = slot_of(QW, q0) >= first
            q = q_ref[pl.ds(q0, QW), cs]
            d = jnp.where(qin, d_ref[pl.ds(q0, QW), cs], BF(0))
            for par in range(2):
                qh = query_side(q, par)
                dh = one_head(d, par)
                qo = one_head(q, par)

                def block(kb):
                    k0 = pl.multiple_of(kb * KB, KB)
                    k = k_ref[pl.ds(k0, KB), cs]
                    v = v_ref[pl.ds(k0, KB), cs]
                    return k0, k, mm(key_side(k, par, slot_of(KB, k0) >= start), qh, NT), mm(v, dh, NT)

                def take_max(kb, top):
                    return jnp.maximum(top, jnp.max(block(kb)[2], axis=0, keepdims=True))

                top = lax.fori_loop(0, ROW_LEN // KB, take_max, jnp.full((1, QW), -1e30, F32))

                def take_sums(kb, sums):
                    _, _, st, dp = block(kb)
                    expo = jnp.exp(st - top)
                    return (
                        sums[0] + jnp.sum(expo, axis=0, keepdims=True),
                        sums[1] + jnp.sum(expo * dp, axis=0, keepdims=True),
                    )

                none = jnp.zeros((1, QW), F32)
                total, weighted = lax.fori_loop(0, ROW_LEN // KB, take_sums, (none, none))
                scale = 1.0 / total
                center = weighted * scale
                a_sc[...] = jnp.zeros_like(a_sc)

                def take_grads(kb, c):
                    k0, k, st, dp = block(kb)
                    prob = jnp.exp(st - top) * scale
                    ds = (prob * (dp - center)).astype(BF)
                    a_sc[...] += mm(one_head(k, par), ds, TN)
                    dk_sc[pl.ds(k0, KB), :] += mm(ds, qo, NN)
                    dv_sc[pl.ds(k0, KB), :] += mm(prob.astype(BF), dh, NN)
                    return c

                lax.fori_loop(0, ROW_LEN // KB, take_grads, 0)
                hit = qin & half_lanes(QW, par)
                dq = (a_sc[...].T * 0.125).astype(BF)
                dq_ref[pl.ds(q0, QW), cs] = jnp.where(hit, dq, dq_ref[pl.ds(q0, QW), cs])
            return carry

        lax.fori_loop(0, windows, wide, 0)

        @pl.when(windows > 0)
        def _():
            kin = slot_of(ROW_LEN, 0) >= start
            dk_ref[:, cs] = jnp.where(kin, (dk_sc[...] * 0.125).astype(BF), dk_ref[:, cs])
            dv_ref[:, cs] = jnp.where(kin, dv_sc[...].astype(BF), dv_ref[:, cs])


def attention_forward(qkv, table, rows, pairs=6):
    n = qkv.shape[0]
    width = qkv.shape[1] // 3
    w = 128 * pairs
    g = width // w
    spec = lambda part: pl.BlockSpec((ROW_LEN, w), lambda r, h, t: (r, part * g + h))
    return pl.pallas_call(
        partial(attend_kernel, pairs, 0),
        out_shape=jax.ShapeDtypeStruct((n, width), BF),
        grid_spec=pltpu.PrefetchScalarGridSpec(
            num_scalar_prefetch=1,
            grid=(rows, g),
            in_specs=[spec(0), spec(1), spec(2)],
            out_specs=spec(0),
            scratch_shapes=[pltpu.VMEM((128, QW), F32)],
        ),
        compiler_params=pltpu.CompilerParams(vmem_limit_bytes=VMEM_LIMIT),
        cost_estimate=cost(18e9, n * width * 8),
        name="attend",
    )(table, qkv, qkv, qkv)


def attention_backward(qkv, da, table, row, rows, before, pairs=6):
    n = qkv.shape[0]
    width = qkv.shape[1] // 3
    w = 128 * pairs
    g = width // w
    spec = lambda part: pl.BlockSpec((ROW_LEN, w), lambda r, h, t: (r + row, part * g + h))
    anywhere = pl.BlockSpec(memory_space=pl.ANY)
    extra = list(before) if before is not None else []
    return pl.pallas_call(
        partial(attend_back_kernel, pairs, row),
        out_shape=[jax.ShapeDtypeStruct((n, width), BF)] * 3,
        grid_spec=pltpu.PrefetchScalarGridSpec(
            num_scalar_prefetch=1,
            grid=(rows, g),
            in_specs=[spec(0), spec(1), spec(2), spec(0)] + [anywhere] * len(extra),
            out_specs=[spec(0)] * 3,
            scratch_shapes=[
                pltpu.VMEM((128, QW), F32),
                pltpu.VMEM((ROW_LEN, 128), F32),
                pltpu.VMEM((ROW_LEN, 128), F32),
            ],
        ),
        input_output_aliases={5 + i: i for i in range(len(extra))},
        compiler_params=pltpu.CompilerParams(vmem_limit_bytes=VMEM_LIMIT),
        cost_estimate=cost(18e9 * rows, rows * ROW_LEN * width * 14),
        name="attend_back",
    )(table, qkv, qkv, qkv, da, *extra)


def hop(value, bit, size):
    return lax.ppermute(value, "fsdp", [(i, i ^ bit) for i in range(size)])


def gather_cross(shard):
    half = shard.shape[0] // 2
    along_x = hop(shard, 2, 8)
    along_y = hop(shard, 4, 8)
    first = hop(along_x[:half], 4, 8)
    second = hop(along_y[half:], 2, 8)
    return [(shard, 0, 0), (along_x, 2, 0), (along_y, 4, 0), (first, 6, 0), (second, 6, half)]


def gather(shard, size):
    if size != 8:
        return [(lax.all_gather(shard, "fsdp", axis=0, tiled=True), None, 0)]
    pieces = gather_cross(shard)
    return pieces + [(hop(array, 1, 8), slot + 1, row) for array, slot, row in pieces]


def after(value, *others):
    return lax.optimization_barrier((value, *others))[0]


def low_sum(a, b):
    return (a.astype(F32) + b.astype(F32)).astype(BF)


def scatter_core(even, odd):
    return even, hop(odd, 1, 8)


def scatter_cross(even, received):
    half = even.shape[1] // 2
    add = lambda q, part: low_sum(even[q, part], received[q, part])
    up, down = slice(0, half), slice(half, None)
    from_x = hop(jnp.stack([add(1, up), add(3, up)]), 2, 8)
    from_y = hop(jnp.stack([add(2, down), add(3, down)]), 4, 8)
    up_own = low_sum(add(0, up), from_x[0])
    down_own = low_sum(add(0, down), from_y[0])
    up_last = hop(low_sum(add(2, up), from_x[1]), 4, 8)
    down_last = hop(low_sum(add(1, down), from_y[1]), 2, 8)
    return jnp.concatenate([low_sum(up_own, up_last), low_sum(down_own, down_last)], axis=0)


def replica_sum(block, size):
    if size != 4:
        return lax.psum(block, "rep").astype(F32)
    z = lax.axis_index("rep")
    inner = low_sum(block, lax.ppermute(block, "rep", [(0, 1), (3, 2)]))
    whole = low_sum(inner, lax.ppermute(inner, "rep", [(1, 2), (2, 1)]))
    outer = lax.ppermute(whole, "rep", [(1, 0), (2, 3)])
    return jnp.where((z == 1) | (z == 2), whole, outer).astype(F32)


def everywhere_sum(value, size, replicas):
    if size != 8 or replicas not in (None, 4):
        return lax.psum(value, "fsdp" if replicas is None else ("fsdp", "rep"))
    for bit in (1, 2, 4):
        value = value + hop(value, bit, 8)
    if replicas is not None:
        for bit in (1, 2):
            value = value + lax.ppermute(value, "rep", [(i, i ^ bit) for i in range(4)])
    return value


class Pieces:
    def __init__(self, pieces, per):
        self.arrays = [p[0] for p in pieces]
        self.places = [(p[1], p[2]) for p in pieces]
        self.per = per

    def copies(self, refs, dst, sems, me, cols=None):
        out = []
        for i, (ref, (slot, row)) in enumerate(zip(refs, self.places)):
            src = ref if cols is None else ref.at[:, cols]
            if slot is None:
                into = dst
            else:
                at = pl.multiple_of((me ^ slot) * self.per + row, math.gcd(self.per, row) if row else self.per)
                into = dst.at[pl.ds(at, ref.shape[0]), :]
            out.append(pltpu.make_async_copy(src, into, sems.at[i]))
        return out


def norm_stats(values):
    center = values - jnp.mean(values, axis=1, keepdims=True)
    rate = lax.rsqrt(jnp.mean(center * center, axis=1, keepdims=True) + layer_eps)
    return center * rate, rate


def norm_back(unit, rate, gain, grad):
    scaled = grad * gain
    mean = jnp.mean(scaled, axis=1, keepdims=True)
    along = jnp.mean(scaled * unit, axis=1, keepdims=True)
    return rate * (scaled - mean - unit * along)


def project_kernel(weight, count, tab, nrm_ref, x_ref, *rest):
    w_refs = rest[:count]
    h_ref, qkv_ref, w_sc, sems = rest[count:]
    me = tab[tab.shape[0] - 1]

    @pl.when(pl.program_id(0) == 0)
    def _():
        copies = weight.copies(w_refs, w_sc, sems, me)
        for c in copies:
            c.start()
        for c in copies:
            c.wait()

    unit, _ = norm_stats(x_ref[...].astype(F32))
    h = (unit * nrm_ref[0:1, :] + nrm_ref[1:2, :]).astype(BF)
    h_ref[...] = h
    width = x_ref.shape[1]
    for part in range(3):
        at = pl.ds(part * width, width)
        qkv_ref[:, at] = mm(h, w_sc[at, :], NT).astype(BF)


def project(table, norms, x, weight, tb=512):
    n, width = x.shape
    count = len(weight.arrays)
    anywhere = pl.BlockSpec(memory_space=pl.ANY)
    return pl.pallas_call(
        partial(project_kernel, weight, count),
        out_shape=[jax.ShapeDtypeStruct((n, width), BF), jax.ShapeDtypeStruct((n, 3 * width), BF)],
        grid_spec=pltpu.PrefetchScalarGridSpec(
            num_scalar_prefetch=1,
            grid=(n // tb,),
            in_specs=[
                pl.BlockSpec((8, width), lambda t, tab: (0, 0)),
                pl.BlockSpec((tb, width), lambda t, tab: (t, 0)),
            ]
            + [anywhere] * count,
            out_specs=[
                pl.BlockSpec((tb, width), lambda t, tab: (t, 0)),
                pl.BlockSpec((tb, 3 * width), lambda t, tab: (t, 0)),
            ],
            scratch_shapes=[pltpu.VMEM((3 * width, width), BF), pltpu.SemaphoreType.DMA((count,))],
        ),
        compiler_params=pltpu.CompilerParams(vmem_limit_bytes=VMEM_LIMIT),
        cost_estimate=cost(6 * n * width * width, n * width * 10 + 6 * width * width),
        name="project",
    )(table, norms, x, *weight.arrays)


def by_owner(acc, per, even_ref, odd_ref, me):
    for q in range(4):
        for parity, ref in ((0, even_ref), (1, odd_ref)):
            at = pl.multiple_of((me ^ (2 * q + parity)) * per, per)
            ref[q] = acc[pl.ds(at, per), :].astype(BF)


def project_grad_kernel(size, tab, dq_ref, dk_ref, dv_ref, h_ref, *rest):
    out_refs, acc = rest[:-1], rest[-1]
    t = pl.program_id(0)
    width = h_ref.shape[1]

    @pl.when(t == 0)
    def _():
        acc[...] = jnp.zeros_like(acc)

    for part, ref in enumerate((dq_ref, dk_ref, dv_ref)):
        acc[pl.ds(part * width, width), :] += mm(ref[...], h_ref[...], TN)

    @pl.when(t == pl.num_programs(0) - 1)
    def _():
        if size == 8:
            by_owner(acc, acc.shape[0] // 8, *out_refs, tab[tab.shape[0] - 1])
        else:
            out_refs[0][...] = acc[...].astype(BF)


def project_grad(table, dq, dk, dv, h, size, tb=512):
    n, width = h.shape
    rows = 3 * width
    block = pl.BlockSpec((tb, width), lambda t, tab: (t, 0))
    shapes = [(4, rows // 8, width)] * 2 if size == 8 else [(rows, width)]
    return pl.pallas_call(
        partial(project_grad_kernel, size),
        out_shape=[jax.ShapeDtypeStruct(s, BF) for s in shapes],
        grid_spec=pltpu.PrefetchScalarGridSpec(
            num_scalar_prefetch=1,
            grid=(n // tb,),
            in_specs=[block] * 4,
            out_specs=[pl.BlockSpec(s, lambda t, tab, k=len(s): (0,) * k) for s in shapes],
            scratch_shapes=[pltpu.VMEM((rows, width), F32)],
        ),
        compiler_params=pltpu.CompilerParams(vmem_limit_bytes=VMEM_LIMIT),
        cost_estimate=cost(6 * n * width * width, n * width * 8 + 6 * width * width),
        name="project_grad",
    )(table, dq, dk, dv, h)


def project_back_kernel(weight, count, tab, nrm_ref, dq_ref, dk_ref, dv_ref, x_ref, dx_ref, *rest):
    w_refs = rest[:count]
    out_ref, gn_ref, w_sc, sems = rest[count:]
    t = pl.program_id(0)
    me = tab[tab.shape[0] - 1]
    width = x_ref.shape[1]

    @pl.when(t == 0)
    def _():
        copies = weight.copies(w_refs, w_sc, sems, me)
        for c in copies:
            c.start()
        gn_ref[...] = jnp.zeros_like(gn_ref)
        for c in copies:
            c.wait()

    grad = mm(dq_ref[...], w_sc[pl.ds(0, width), :], NN)
    grad += mm(dk_ref[...], w_sc[pl.ds(width, width), :], NN)
    grad += mm(dv_ref[...], w_sc[pl.ds(2 * width, width), :], NN)
    unit, rate = norm_stats(x_ref[...].astype(F32))
    out_ref[...] = (dx_ref[...] + norm_back(unit, rate, nrm_ref[0:1, :], grad)).astype(BF)
    gn_ref[0:1, :] += jnp.sum(grad * unit, axis=0, keepdims=True)
    gn_ref[1:2, :] += jnp.sum(grad, axis=0, keepdims=True)


def project_back(table, norms, dq, dk, dv, x, dx, weight, tb=512):
    n, width = x.shape
    count = len(weight.arrays)
    anywhere = pl.BlockSpec(memory_space=pl.ANY)
    block = pl.BlockSpec((tb, width), lambda t, tab: (t, 0))
    fixed = pl.BlockSpec((8, width), lambda t, tab: (0, 0))
    return pl.pallas_call(
        partial(project_back_kernel, weight, count),
        out_shape=[jax.ShapeDtypeStruct((n, width), BF), jax.ShapeDtypeStruct((8, width), F32)],
        grid_spec=pltpu.PrefetchScalarGridSpec(
            num_scalar_prefetch=1,
            grid=(n // tb,),
            in_specs=[fixed] + [block] * 5 + [anywhere] * count,
            out_specs=[block, fixed],
            scratch_shapes=[pltpu.VMEM((3 * width, width), BF), pltpu.SemaphoreType.DMA((count,))],
        ),
        compiler_params=pltpu.CompilerParams(vmem_limit_bytes=VMEM_LIMIT),
        cost_estimate=cost(6 * n * width * width, n * width * 14 + 6 * width * width),
        name="project_back",
    )(table, norms, dq, dk, dv, x, dx, *weight.arrays)


def gelu_both(values):
    phi = 0.5 + 0.5 * lax.erf(values * math.sqrt(0.5))
    bell = jnp.exp(values * values * -0.5) * (1.0 / math.sqrt(2.0 * math.pi))
    return values * phi, phi + values * bell


def middle_kernel(size, tb, sub, chunks, w_proj, w_up, w_down, tab, nrm_ref, att_ref, x_ref, cot_ref, *rest):
    counts = [len(w.arrays) for w in (w_proj, w_up, w_down)]
    proj_refs = rest[: counts[0]]
    up_refs = rest[counts[0] : counts[0] + counts[1]]
    down_refs = rest[counts[0] + counts[1] : sum(counts)]
    rest = rest[sum(counts) :]
    outs = 6 if size == 8 else 3
    out_ref, dx_ref, da_ref, gn_ref = rest[:4]
    g_refs = rest[4 : 4 + outs]
    x1_sc, h_sc, ht_sc, dy_sc, dyt_sc, x2_sc, dh_sc, gu_sc, gd_sc, wp_sc, wu_sc, wd_sc, p_sem, u_sem, d_sem = rest[4 + outs :]
    j = pl.program_id(0)
    t = pl.program_id(1)
    steps = pl.num_programs(1)
    me = tab[tab.shape[0] - 1]
    per = ROW_LEN // tb
    valid = tab[lax.div(t, per) * STRIDE + 33]
    ok = (lax.broadcasted_iota(jnp.int32, (tb, 1), 0) + lax.rem(t, per) * tb) < valid
    ts = pl.ds(pl.multiple_of(t * tb, tb), tb)
    width = x_ref.shape[1]
    gain = nrm_ref[2:3, :]
    shift = nrm_ref[3:4, :]

    def chunk_copies(m):
        b = m % 2
        if size != 8:
            piece = pl.ds(m * width, width)
            up = [pltpu.make_async_copy(up_refs[0].at[piece, :], wu_sc.at[b], u_sem.at[b, 0])]
            down = [pltpu.make_async_copy(down_refs[0].at[:, piece], wd_sc.at[b], d_sem.at[b, 0])]
            return up + down
        up = []
        for i, (ref, (slot, row)) in enumerate(zip(up_refs, w_up.places)):
            if slot // 2 == m:
                at = pl.multiple_of(((me & 1) ^ (slot & 1)) * w_up.per + row, w_up.per // 2)
                into = wu_sc.at[b].at[pl.ds(at, ref.shape[0]), :]
                up.append(pltpu.make_async_copy(ref, into, u_sem.at[b, i]))
        piece = pl.ds(pl.multiple_of(((me >> 1) ^ m) * width, width), width)
        return up + w_down.copies(down_refs, wd_sc.at[b], d_sem.at[b], me, piece)

    @pl.when((j == 0) & (t == 0))
    def _():
        for c in w_proj.copies(proj_refs, wp_sc, p_sem, me):
            c.start()
        for c in chunk_copies(0):
            c.start()
        for c in w_proj.copies(proj_refs, wp_sc, p_sem, me):
            c.wait()

    for m in range(chunks):

        @pl.when((j == m) & (t == 0))
        def _():
            for c in chunk_copies(m):
                c.wait()
            if m + 1 < chunks:
                for c in chunk_copies(m + 1):
                    c.start()

    @pl.when(j == 0)
    def _():
        x1 = x_ref[...].astype(F32) + mm(att_ref[...], wp_sc[...], NT)
        x1_sc[ts, :] = x1
        x2_sc[ts, :] = x1
        unit, _ = norm_stats(x1)
        h = (unit * gain + shift).astype(BF)
        h_sc[ts, :] = h
        ht_sc[:, ts] = h.T
        dy = jnp.where(ok, cot_ref[...], BF(0))
        dy_sc[ts, :] = dy
        dyt_sc[:, ts] = dy.T
        dh_sc[ts, :] = jnp.zeros((tb, width), F32)

    @pl.when((t == 0) & (j < chunks))
    def _():
        gu_sc[...] = jnp.zeros_like(gu_sc)
        gd_sc[...] = jnp.zeros_like(gd_sc)

    @pl.when(j < chunks)
    def _():
        wu = wu_sc[lax.rem(j, 2)]
        wd = wd_sc[lax.rem(j, 2)]
        parts = [pl.ds(pl.multiple_of(t * tb + i * sub, sub), sub) for i in range(tb // sub)]
        uppers = [mm(h_sc[p, :], wu, NT) for p in parts]
        acts = []
        dups = []
        for p, upper in zip(parts, uppers):
            dact = mm(dy_sc[p, :], wd, NN)
            act, slope = gelu_both(upper)
            acts.append(act.astype(BF))
            dups.append((dact * slope).astype(BF))
        for p, act, dup in zip(parts, acts, dups):
            x2_sc[p, :] += mm(act, wd, NT)
            dh_sc[p, :] += mm(dup, wu, NN)
        gd_sc[...] += mm(dyt_sc[:, ts], jnp.concatenate(acts, axis=0), NN)
        gu_sc[...] += mm(ht_sc[:, ts], jnp.concatenate(dups, axis=0), NN)

    @pl.when((t == steps - 1) & (j < chunks))
    def _():
        if size == 8:
            half = w_up.per
            for parity in range(2):
                at = pl.multiple_of(((me & 1) ^ parity) * half, half)
                g_refs[parity][0] = gu_sc[:, pl.ds(at, half)].astype(BF)
            by_owner(gd_sc, w_down.per, g_refs[2], g_refs[3], me)
        else:
            g_refs[0][...] = gu_sc[...].astype(BF)
            g_refs[1][...] = gd_sc[...].astype(BF)

    @pl.when(j == chunks)
    def _():
        out_ref[...] = jnp.where(ok, x2_sc[ts, :], 0.0).astype(BF)
        unit, rate = norm_stats(x1_sc[ts, :])
        dh = dh_sc[ts, :]
        dx = dy_sc[ts, :].astype(F32) + norm_back(unit, rate, gain, dh)
        dx_ref[...] = dx
        db = dx.astype(BF)
        da_ref[...] = mm(db, wp_sc[...], NN).astype(BF)

        @pl.when(t == 0)
        def _():
            gu_sc[...] = jnp.zeros_like(gu_sc)
            gn_ref[...] = jnp.zeros_like(gn_ref)

        gu_sc[...] += mm(db, att_ref[...], TN)
        gn_ref[0:1, :] += jnp.sum(dh * unit, axis=0, keepdims=True)
        gn_ref[1:2, :] += jnp.sum(dh, axis=0, keepdims=True)

        @pl.when(t == steps - 1)
        def _():
            if size == 8:
                by_owner(gu_sc, w_proj.per, g_refs[4], g_refs[5], me)
            else:
                g_refs[2][...] = gu_sc[...].astype(BF)


def middle(table, norms, att, x, cot, w_proj, w_up, w_down, hidden, size, tb=512, sub=256):
    n, width = x.shape
    chunks = hidden // width
    steps = n // tb
    last = chunks - 1
    dev = table.shape[0] - 1
    first = lambda j, t, tab: (jnp.where(j == 0, t, steps - 1), 0)
    ends = lambda j, t, tab: (jnp.where((j == 0) | (j == chunks), t, steps - 1), 0)
    final = lambda j, t, tab: (jnp.where(j == chunks, t, 0), 0)
    fixed = lambda j, t, tab: (0, 0)
    anywhere = pl.BlockSpec(memory_space=pl.ANY)
    now = lambda j: jnp.minimum(j, last)
    sds = jax.ShapeDtypeStruct
    if size == 8:
        fw, dw = w_up.per, w_down.per
        pair = lambda j, tab: lax.bitwise_xor(lax.shift_right_logical(tab[dev], 1), now(j))
        g_shapes = [sds((4, width, fw), BF)] * 2 + [sds((4, dw, hidden), BF)] * 2 + [sds((4, dw, width), BF)] * 2
        g_specs = (
            [pl.BlockSpec((1, width, fw), lambda j, t, tab: (now(j), 0, 0))] * 2
            + [pl.BlockSpec((4, dw, width), lambda j, t, tab: (0, 0, pair(j, tab)))] * 2
            + [pl.BlockSpec((4, dw, width), lambda j, t, tab: (0, 0, 0))] * 2
        )
    else:
        g_shapes = [sds((width, hidden), BF)] * 2 + [sds((width, width), BF)]
        g_specs = [pl.BlockSpec((width, width), lambda j, t, tab: (0, now(j)))] * 2 + [
            pl.BlockSpec((width, width), fixed)
        ]
    block = lambda index: pl.BlockSpec((tb, width), index)
    weights = w_proj.arrays + w_up.arrays + w_down.arrays
    dma = pltpu.SemaphoreType.DMA
    return pl.pallas_call(
        partial(middle_kernel, size, tb, sub, chunks, w_proj, w_up, w_down),
        out_shape=[sds((n, width), BF), sds((n, width), F32), sds((n, width), BF), sds((8, width), F32)] + g_shapes,
        grid_spec=pltpu.PrefetchScalarGridSpec(
            num_scalar_prefetch=1,
            grid=(chunks + 1, steps),
            in_specs=[pl.BlockSpec((8, width), fixed), block(ends), block(first), block(first)]
            + [anywhere] * len(weights),
            out_specs=[block(final), block(final), block(final), pl.BlockSpec((8, width), fixed)] + g_specs,
            scratch_shapes=[
                pltpu.VMEM((n, width), F32),
                pltpu.VMEM((n, width), BF),
                pltpu.VMEM((width, n), BF),
                pltpu.VMEM((n, width), BF),
                pltpu.VMEM((width, n), BF),
                pltpu.VMEM((n, width), F32),
                pltpu.VMEM((n, width), F32),
                pltpu.VMEM((width, width), F32),
                pltpu.VMEM((width, width), F32),
                pltpu.VMEM((width, width), BF),
                pltpu.VMEM((2, width, width), BF),
                pltpu.VMEM((2, width, width), BF),
                dma((len(w_proj.arrays),)),
                dma((2, len(w_up.arrays))),
                dma((2, len(w_down.arrays))),
            ],
        ),
        compiler_params=pltpu.CompilerParams(vmem_limit_bytes=VMEM_LIMIT),
        cost_estimate=cost(n * width * (12 * hidden + 6 * width), n * width * 22 + 8 * hidden * width),
        name="middle",
    )(table, norms, att, x, cot, *weights)


def per_device(
    size,
    replicas,
    tokens,
    segment_ids,
    cotangent,
    norm_params,
    qkv_weight,
    proj_weight,
    up_weight,
    down_weight,
    target_norms,
    target_qkv,
    target_proj,
    target_up,
    target_down,
):
    count, width = tokens.shape
    rows = count // ROW_LEN
    hidden = down_weight.shape[0]
    own = width // size
    me = lax.axis_index("fsdp")
    with jax.named_scope("gather_weights"):
        placed = lax.dynamic_update_slice(jnp.zeros((8, width), F32), norm_params.astype(F32), (0, me * own))
        norms = everywhere_sum(placed, size, None)
        pieces = gather(qkv_weight.T, size)
        w_qkv = Pieces(pieces, qkv_weight.shape[1])
        late = after((proj_weight.T, up_weight.T, down_weight.T), *[p[0] for p in pieces[1:3]])
        w_proj = Pieces(gather(late[0], size), own)
        w_up = Pieces(gather(late[1], size), up_weight.shape[1])
        w_down = Pieces(gather(late[2], size), own)
    table = job_table(segment_ids, rows, me)

    h1, qkv = project(table, norms, tokens, w_qkv)
    attended = attention_forward(qkv, table, rows)
    block_output, grad_middle, grad_attended, grad_norm2, *grads = middle(
        table, norms, attended, tokens, cotangent, w_proj, w_up, w_down, hidden, size
    )
    dqkv = None
    for row in range(rows):
        dqkv = attention_backward(qkv, grad_attended, table, row, 1, dqkv)
    grad_qkv = project_grad(table, *dqkv, h1, size)
    input_grad, grad_norm1 = project_back(table, norms, *dqkv, tokens, grad_middle, w_qkv)

    with jax.named_scope("sum_gradients"):
        if size == 8:
            up, down, proj, qkv_own = (
                scatter_cross(*scatter_core(*pair)) for pair in (grads[0:2], grads[2:4], grads[4:6], grad_qkv)
            )
        else:
            sums = lambda g, dim: lax.psum_scatter(g, "fsdp", scatter_dimension=dim, tiled=True)
            up, down, proj, qkv_own = sums(grads[0], 1), sums(grads[1], 0), sums(grads[2], 0), sums(grad_qkv[0], 0)
        up, down, proj, qkv_own = (replica_sum(g, replicas) for g in (up, down, proj, qkv_own))
        sums = [everywhere_sum(g, size, replicas)[:2] for g in (grad_norm1, grad_norm2)]
        norm_grad = lax.dynamic_slice(jnp.concatenate(sums, axis=0), (0, me * own), (4, own))

    keep_rate = 1.0 - ema_rate
    blend = lambda target, weight: ema_rate * target + keep_rate * weight.astype(F32)
    return (
        block_output,
        input_grad,
        norm_grad,
        qkv_own.T,
        proj.T,
        up,
        down.T,
        blend(target_norms, norm_params),
        blend(target_qkv, qkv_weight),
        blend(target_proj, proj_weight),
        blend(target_up, up_weight),
        blend(target_down, down_weight),
    )


def solution(mesh):
    tokens = P(("fsdp", "rep"), None)
    columns = P(None, "fsdp")
    return jax.shard_map(
        partial(per_device, mesh.shape["fsdp"], mesh.shape["rep"]),
        mesh=mesh,
        in_specs=(tokens, P(("fsdp", "rep")), tokens) + (columns,) * 10,
        out_specs=(tokens, tokens) + (columns,) * 10,
        check_vma=False,
    )
```

```python
import math
from functools import partial

import jax
import jax.numpy as jnp
from jax import lax
from jax.experimental import pallas as pl
from jax.experimental.pallas import tpu as pltpu
from jax.sharding import PartitionSpec as P

HEAD = 64
ROW_LEN = 1024
layer_eps = 1e-06
ema_rate = 0.75

BF = jnp.bfloat16
F32 = jnp.float32
NN = (((1,), (0,)), ((), ()))
NT = (((1,), (1,)), ((), ()))
TN = (((0,), (0,)), ((), ()))
VMEM_LIMIT = 66_000_000
GRANT = 32_000_000
COST_SCALE = 0.02

QW = 256
KW = 224
FIT = KW - 15
SMALL = 128
FIT_SMALL = SMALL - 15
KB = 128
STRIDE = 35


def mm(left, right, dims):
    return lax.dot_general(left, right, dims, preferred_element_type=F32)


def cost(flops, moved):
    return pl.CostEstimate(flops=int(flops * COST_SCALE), bytes_accessed=int(moved * COST_SCALE), transcendentals=0)


def job_table(segment_ids, rows, device):
    seg = segment_ids.reshape(rows, 1, ROW_LEN)
    ident = jnp.arange(16, dtype=jnp.int32)[None, :, None]
    real = seg >= 0
    starts = jnp.sum((real & (seg < ident)).astype(jnp.int32), axis=2)
    after = jnp.sum((real & (seg < ident + 1)).astype(jnp.int32), axis=2)
    images = jnp.max(seg, axis=2) + 1
    ends = jnp.where(jnp.arange(16, dtype=jnp.int32)[None, :] < images, after, ROW_LEN)
    valid = jnp.sum(real.astype(jnp.int32), axis=2)
    pad = ROW_LEN - valid
    fits = pad <= FIT
    jobs = images + jnp.where((pad > 0) & fits, 1, 0)
    wide = jnp.where(fits, 0, (pad + 15 + QW - 1) // QW)
    table = jnp.concatenate([starts, ends, jobs, valid, wide], axis=1).reshape(-1)
    return jnp.concatenate([table, device.astype(jnp.int32).reshape(1)])


def lane_of(count):
    return lax.broadcasted_iota(jnp.int32, (count, 128), 1)


def slot_of(count, base):
    return lax.broadcasted_iota(jnp.int32, (count, 128), 0) + base


def half_lanes(count, par):
    return (lane_of(count) < 64) if par == 0 else (lane_of(count) >= 64)


def spare_lane(count, par):
    return lane_of(count) == (64 if par == 0 else 0)


def query_side(q, par):
    n = q.shape[0]
    return jnp.where(half_lanes(n, par), q * BF(0.125), jnp.where(spare_lane(n, par), BF(1), BF(0)))


def key_side(k, par, inside):
    n = k.shape[0]
    return jnp.where(half_lanes(n, par), k, jnp.where(spare_lane(n, par) & (~inside), BF(-1e30), BF(0)))


def one_head(x, par):
    return jnp.where(half_lanes(x.shape[0], par), x, BF(0))


def each_image(tab, base, work):
    def job(j, carry):
        begin = tab[base + j]
        end = tab[base + 16 + j]
        low = lax.div(begin, 16) * 16
        small = end - begin <= FIT_SMALL
        for fits, nq, nk in ((small, SMALL, SMALL), (~small, QW, KW)):

            @pl.when(fits)
            def _():
                q0 = pl.multiple_of(jnp.minimum(low, ROW_LEN - nq), 16)
                k0 = pl.multiple_of(jnp.minimum(low, ROW_LEN - nk), 16)
                kr = slot_of(nk, k0)
                qr = slot_of(nq, q0)
                work(pl.ds(q0, nq), pl.ds(k0, nk), (qr >= begin) & (qr < end), (kr >= begin) & (kr < end))

        return carry

    lax.fori_loop(0, tab[base + 32], job, 0)


def attend_kernel(pairs, row0, tab, q_ref, k_ref, v_ref, *rest):
    o_ref, a_sc = rest[-2:]
    base = (pl.program_id(0) + row0) * STRIDE
    o_ref[...] = jnp.zeros_like(o_ref)

    def work(qs, ks, qin, inside):
        scores = []
        for p in range(pairs):
            cs = pl.ds(128 * p, 128)
            q = q_ref[qs, cs]
            k = k_ref[ks, cs]
            for par in range(2):
                scores.append(mm(key_side(k, par, inside), query_side(q, par), NT))
        probs = []
        for st in scores:
            expo = jnp.exp(st - jnp.max(st, axis=0, keepdims=True))
            total = jnp.sum(expo, axis=0, keepdims=True)
            probs.append((expo * (1.0 / total)).astype(BF))
        for p in range(pairs):
            cs = pl.ds(128 * p, 128)
            v = v_ref[ks, cs]
            o = jnp.concatenate(
                [mm(v[:, 64 * par : 64 * par + 64], probs[2 * p + par], TN) for par in range(2)], axis=0
            ).T
            o_ref[qs, cs] = jnp.where(qin, o.astype(BF), o_ref[qs, cs])

    each_image(tab, base, work)

    start = tab[base + 33]
    low = lax.div(start, 16) * 16

    def wide(i, carry):
        q0 = pl.multiple_of(jnp.minimum(low + i * QW, ROW_LEN - QW), 16)
        qin = slot_of(QW, q0) >= start
        for p in range(pairs):
            cs = pl.ds(128 * p, 128)
            q = q_ref[pl.ds(q0, QW), cs]
            for par in range(2):
                qs = query_side(q, par)

                def block(kb):
                    k0 = pl.multiple_of(kb * KB, KB)
                    k = k_ref[pl.ds(k0, KB), cs]
                    return k0, mm(key_side(k, par, slot_of(KB, k0) >= start), qs, NT)

                def take_max(kb, top):
                    return jnp.maximum(top, jnp.max(block(kb)[1], axis=0, keepdims=True))

                top = lax.fori_loop(0, ROW_LEN // KB, take_max, jnp.full((1, QW), -1e30, F32))

                def take_sum(kb, total):
                    return total + jnp.sum(jnp.exp(block(kb)[1] - top), axis=0, keepdims=True)

                total = lax.fori_loop(0, ROW_LEN // KB, take_sum, jnp.zeros((1, QW), F32))
                a_sc[...] = jnp.zeros_like(a_sc)

                def take_out(kb, c):
                    k0, st = block(kb)
                    prob = (jnp.exp(st - top) * (1.0 / total)).astype(BF)
                    a_sc[...] += mm(one_head(v_ref[pl.ds(k0, KB), cs], par), prob, TN)
                    return c

                lax.fori_loop(0, ROW_LEN // KB, take_out, 0)
                hit = qin & half_lanes(QW, par)
                o_ref[pl.ds(q0, QW), cs] = jnp.where(hit, a_sc[...].T.astype(BF), o_ref[pl.ds(q0, QW), cs])
        return carry

    lax.fori_loop(0, tab[base + 34], wide, 0)


def attend_back_kernel(pairs, row0, tab, q_ref, k_ref, v_ref, d_ref, *rest):
    dq_ref, dk_ref, dv_ref, a_sc, dk_sc, dv_sc = rest[-6:]
    base = (pl.program_id(0) + row0) * STRIDE
    dq_ref[...] = jnp.zeros_like(dq_ref)
    dk_ref[...] = jnp.zeros_like(dk_ref)
    dv_ref[...] = jnp.zeros_like(dv_ref)

    def work(qs, ks, qin, inside):
        scores = []
        grads = []
        for p in range(pairs):
            cs = pl.ds(128 * p, 128)
            q = q_ref[qs, cs]
            k = k_ref[ks, cs]
            v = v_ref[ks, cs]
            d = jnp.where(qin, d_ref[qs, cs], BF(0))
            for par in range(2):
                scores.append(mm(key_side(k, par, inside), query_side(q, par), NT))
                grads.append(mm(v, one_head(d, par), NT))
        probs = []
        dscores = []
        for st, dp in zip(scores, grads):
            expo = jnp.exp(st - jnp.max(st, axis=0, keepdims=True))
            total = jnp.sum(expo, axis=0, keepdims=True)
            prob = expo * (1.0 / total)
            center = jnp.sum(prob * dp, axis=0, keepdims=True)
            dscores.append((prob * (dp - center)).astype(BF))
            probs.append(prob.astype(BF))
        for p in range(pairs):
            cs = pl.ds(128 * p, 128)
            q = q_ref[qs, cs]
            k = k_ref[ks, cs]
            d = jnp.where(qin, d_ref[qs, cs], BF(0))
            dv = mm(probs[2 * p], one_head(d, 0), NN) + mm(probs[2 * p + 1], one_head(d, 1), NN)
            dk = mm(dscores[2 * p], one_head(q, 0), NN) + mm(dscores[2 * p + 1], one_head(q, 1), NN)
            dq = jnp.concatenate(
                [mm(k[:, 64 * par : 64 * par + 64], dscores[2 * p + par], TN) for par in range(2)], axis=0
            ).T
            dq_ref[qs, cs] = jnp.where(qin, (dq * 0.125).astype(BF), dq_ref[qs, cs])
            dk_ref[ks, cs] = jnp.where(inside, (dk * 0.125).astype(BF), dk_ref[ks, cs])
            dv_ref[ks, cs] = jnp.where(inside, dv.astype(BF), dv_ref[ks, cs])

    each_image(tab, base, work)

    start = tab[base + 33]
    low = lax.div(start, 16) * 16
    windows = tab[base + 34]
    for p in range(pairs):
        cs = pl.ds(128 * p, 128)

        @pl.when(windows > 0)
        def _():
            dk_sc[...] = jnp.zeros_like(dk_sc)
            dv_sc[...] = jnp.zeros_like(dv_sc)

        def wide(i, carry):
            first = jnp.maximum(start, low + i * QW)
            q0 = pl.multiple_of(jnp.minimum(low + i * QW, ROW_LEN - QW), 16)
            qin = slot_of(QW, q0) >= first
            q = q_ref[pl.ds(q0, QW), cs]
            d = jnp.where(qin, d_ref[pl.ds(q0, QW), cs], BF(0))
            for par in range(2):
                qh = query_side(q, par)
                dh = one_head(d, par)
                qo = one_head(q, par)

                def block(kb):
                    k0 = pl.multiple_of(kb * KB, KB)
                    k = k_ref[pl.ds(k0, KB), cs]
                    v = v_ref[pl.ds(k0, KB), cs]
                    return k0, k, mm(key_side(k, par, slot_of(KB, k0) >= start), qh, NT), mm(v, dh, NT)

                def take_max(kb, top):
                    return jnp.maximum(top, jnp.max(block(kb)[2], axis=0, keepdims=True))

                top = lax.fori_loop(0, ROW_LEN // KB, take_max, jnp.full((1, QW), -1e30, F32))

                def take_sums(kb, sums):
                    _, _, st, dp = block(kb)
                    expo = jnp.exp(st - top)
                    return (
                        sums[0] + jnp.sum(expo, axis=0, keepdims=True),
                        sums[1] + jnp.sum(expo * dp, axis=0, keepdims=True),
                    )

                none = jnp.zeros((1, QW), F32)
                total, weighted = lax.fori_loop(0, ROW_LEN // KB, take_sums, (none, none))
                scale = 1.0 / total
                center = weighted * scale
                a_sc[...] = jnp.zeros_like(a_sc)

                def take_grads(kb, c):
                    k0, k, st, dp = block(kb)
                    prob = jnp.exp(st - top) * scale
                    ds = (prob * (dp - center)).astype(BF)
                    a_sc[...] += mm(one_head(k, par), ds, TN)
                    dk_sc[pl.ds(k0, KB), :] += mm(ds, qo, NN)
                    dv_sc[pl.ds(k0, KB), :] += mm(prob.astype(BF), dh, NN)
                    return c

                lax.fori_loop(0, ROW_LEN // KB, take_grads, 0)
                hit = qin & half_lanes(QW, par)
                dq = (a_sc[...].T * 0.125).astype(BF)
                dq_ref[pl.ds(q0, QW), cs] = jnp.where(hit, dq, dq_ref[pl.ds(q0, QW), cs])
            return carry

        lax.fori_loop(0, windows, wide, 0)

        @pl.when(windows > 0)
        def _():
            kin = slot_of(ROW_LEN, 0) >= start
            dk_ref[:, cs] = jnp.where(kin, (dk_sc[...] * 0.125).astype(BF), dk_ref[:, cs])
            dv_ref[:, cs] = jnp.where(kin, dv_sc[...].astype(BF), dv_ref[:, cs])


def row_call(kernel, name, outs, scratch, qkv, extra, table, row, half, halves, before, flops, moved):
    n = qkv.shape[0]
    width = qkv.shape[1] // 3
    w = width // halves
    spec = lambda part: pl.BlockSpec((ROW_LEN, w), lambda r, t: (row, part * halves + half))
    before = [] if before is None else list(before)
    return pl.pallas_call(
        partial(kernel, w // 128, row),
        out_shape=[jax.ShapeDtypeStruct((n, width), BF)] * outs,
        grid_spec=pltpu.PrefetchScalarGridSpec(
            num_scalar_prefetch=1,
            grid=(1,),
            in_specs=[spec(0), spec(1), spec(2)]
            + [spec(0)] * len(extra)
            + [pl.BlockSpec(memory_space=pl.ANY)] * len(before),
            out_specs=[spec(0)] * outs,
            scratch_shapes=scratch,
        ),
        input_output_aliases={4 + len(extra) + i: i for i in range(len(before))},
        compiler_params=pltpu.CompilerParams(vmem_limit_bytes=GRANT),
        cost_estimate=cost(flops / halves, moved * ROW_LEN * w),
        name=name,
    )(table, qkv, qkv, qkv, *extra, *before)


def attention_forward(qkv, table, row, before):
    scratch = [pltpu.VMEM((128, QW), F32)]
    return row_call(attend_kernel, "attend", 1, scratch, qkv, [], table, row, 0, 1, before, 12e9, 8)


def attention_backward(qkv, da, table, row, half, halves, before):
    scratch = [pltpu.VMEM((128, QW), F32), pltpu.VMEM((ROW_LEN, 128), F32), pltpu.VMEM((ROW_LEN, 128), F32)]
    return row_call(attend_back_kernel, "attend_back", 3, scratch, qkv, [da], table, row, half, halves, before, 24e9, 14)


def hop(value, bit, size):
    return lax.ppermute(value, "fsdp", [(i, i ^ bit) for i in range(size)])


def gather_cross(first, second):
    first_x, second_y = hop(first, 2, 8), hop(second, 4, 8)
    first_y, second_x = hop(first, 4, 8), hop(second, 2, 8)
    return (first, first_x, first_y), (second, second_x, second_y)


def forward_cross(firsts, seconds):
    return hop(firsts[1], 4, 8), hop(seconds[2], 2, 8)


def both_cores(arrays):
    own = [(array, 2 * i) for i, array in enumerate(arrays)]
    return own + [(hop(array, 1, 8), slot + 1) for array, slot in own]


def after(value, *others):
    return lax.optimization_barrier((value, *others))[0]


def total(*terms):
    return sum(t.astype(F32) for t in terms).astype(BF)


class Scatter:
    def __init__(self, even, odd):
        self.even = even
        self.core = hop(odd, 1, 8)

    def send(self, done):
        self.core = after(self.core, done)
        self.out = [total(self.even[q], self.core[q]) for q in (1, 2, 3)]
        return self.out

    def block(self, done):
        come = after([hop(block, 2 * q, 8) for q, block in zip((1, 2, 3), self.out)], done)
        return total(self.even[0], self.core[0], *come)


def direct_sum(block, done):
    shift = lambda value, by: lax.ppermute(value, "rep", [(i, (i + by) % 4) for i in range(4)])
    z = lax.axis_index("rep")
    quarters = block.reshape(4, block.shape[0] // 4, block.shape[1])
    pick = lambda by: lax.dynamic_index_in_dim(quarters, lax.rem(z + by, 4), 0, False)
    mine = total(pick(0), *after([shift(pick(by), by) for by in (2, 1, 3)], done))
    parts = [mine] + [shift(mine, by) for by in (1, 2, 3)]
    out = jnp.zeros(quarters.shape, F32)
    for by, part in enumerate(parts):
        out = lax.dynamic_update_index_in_dim(out, part.astype(F32), lax.rem(z - by + 4, 4), 0)
    return out.reshape(block.shape)


class Weight:
    def __init__(self, pieces, per):
        self.arrays = [p[0] for p in pieces]
        self.places = [p[1:] for p in pieces]
        self.per = per

    def copies(self, refs, dst, sems, me):
        out = []
        for i, (ref, (slot, row)) in enumerate(zip(refs, self.places)):
            src, into = ref, dst
            if slot is not None:
                half = self.per // 2
                src = ref.at[pl.ds(0, half), :]
                into = dst.at[pl.ds(pl.multiple_of((me ^ slot) * self.per + row, half), half), :]
            out.append(pltpu.make_async_copy(src, into, sems.at[i]))
        return out


def norm_stats(values):
    center = values - jnp.mean(values, axis=1, keepdims=True)
    rate = lax.rsqrt(jnp.mean(center * center, axis=1, keepdims=True) + layer_eps)
    return center * rate, rate


def norm_back(unit, rate, gain, grad):
    scaled = grad * gain
    mean = jnp.mean(scaled, axis=1, keepdims=True)
    along = jnp.mean(scaled * unit, axis=1, keepdims=True)
    return rate * (scaled - mean - unit * along)


def project_kernel(weight, count, tab, x_ref, *rest):
    w_refs = rest[:count]
    h_ref, qkv_ref, nrm_ref, w_sc, n_sc, sems, n_sems = rest[-7:]
    me = tab[tab.shape[0] - 1]
    half = weight.per // 2

    @pl.when(pl.program_id(0) == 0)
    def _():
        if len(rest) - 7 > count:
            norm_copies = [pltpu.make_async_copy(rest[count], n_sc.at[0], n_sems.at[0])]
        else:
            norm_copies = [
                pltpu.make_async_copy(w_refs[i].at[pl.ds(half, 16), :], n_sc.at[i], n_sems.at[i]) for i in range(8)
            ]
        copies = weight.copies(w_refs, w_sc, sems, me)
        for c in norm_copies + copies:
            c.start()
        for c in norm_copies:
            c.wait()
        placed = sum(n_sc[i].astype(F32) for i in range(len(norm_copies)))
        nrm_ref[...] = placed[:8, :]
        for c in copies:
            c.wait()

    tb, width = x_ref.shape
    parts = [pl.ds(i, tb // 2) for i in range(0, tb, tb // 2)]
    for p in parts:
        unit, _ = norm_stats(x_ref[p, :].astype(F32))
        h_ref[p, :] = (unit * nrm_ref[0:1, :] + nrm_ref[1:2, :]).astype(BF)
    for p in parts:
        qkv_ref[p, :] = mm(h_ref[p, :], w_sc[...], NT).astype(BF)


def project(table, norm_parts, x, weight, tb=512):
    n, width = x.shape
    count = len(weight.arrays)
    anywhere = pl.BlockSpec(memory_space=pl.ANY)
    block = lambda w: pl.BlockSpec((tb, w), lambda t, tab: (t, 0))
    sds = jax.ShapeDtypeStruct
    return pl.pallas_call(
        partial(project_kernel, weight, count),
        out_shape=[sds((n, width), BF), sds((n, 3 * width), BF), sds((8, width), F32)],
        grid_spec=pltpu.PrefetchScalarGridSpec(
            num_scalar_prefetch=1,
            grid=(n // tb,),
            in_specs=[block(width)] + [anywhere] * (count + len(norm_parts)),
            out_specs=[block(width), block(3 * width), pl.BlockSpec((8, width), lambda t, tab: (0, 0))],
            scratch_shapes=[
                pltpu.VMEM((3 * width, width), BF),
                pltpu.VMEM((8, 16, width), BF),
                pltpu.SemaphoreType.DMA((count,)),
                pltpu.SemaphoreType.DMA((8,)),
            ],
        ),
        compiler_params=pltpu.CompilerParams(vmem_limit_bytes=VMEM_LIMIT),
        cost_estimate=cost(6 * n * width * width, n * width * 10 + 6 * width * width),
        name="project",
    )(table, x, *weight.arrays, *norm_parts)


def by_owner(acc, per, even_ref, odd_ref, me):
    for q in range(4):
        for parity, ref in ((0, even_ref), (1, odd_ref)):
            at = pl.multiple_of((me ^ (2 * q + parity)) * per, per)
            ref[q] = acc[pl.ds(at, per), :].astype(BF)


def project_grad_kernel(size, tab, dq_ref, dk_ref, dv_ref, h_ref, *rest):
    out_refs, acc = rest[:-1], rest[-1]
    t = pl.program_id(0)
    width = h_ref.shape[1]

    @pl.when(t == 0)
    def _():
        acc[...] = jnp.zeros_like(acc)

    for part, ref in enumerate((dq_ref, dk_ref, dv_ref)):
        acc[pl.ds(part * width, width), :] += mm(ref[...], h_ref[...], TN)

    @pl.when(t == pl.num_programs(0) - 1)
    def _():
        if size == 8:
            by_owner(acc, acc.shape[0] // 8, *out_refs, tab[tab.shape[0] - 1])
        else:
            out_refs[0][...] = acc[...].astype(BF)


def project_grad(table, dq, dk, dv, h, size, tb=512):
    n, width = h.shape
    rows = 3 * width
    block = pl.BlockSpec((tb, width), lambda t, tab: (t, 0))
    shapes = [(4, rows // 8, width)] * 2 if size == 8 else [(rows, width)]
    return pl.pallas_call(
        partial(project_grad_kernel, size),
        out_shape=[jax.ShapeDtypeStruct(s, BF) for s in shapes],
        grid_spec=pltpu.PrefetchScalarGridSpec(
            num_scalar_prefetch=1,
            grid=(n // tb,),
            in_specs=[block] * 4,
            out_specs=[pl.BlockSpec(s, lambda t, tab, k=len(s): (0,) * k) for s in shapes],
            scratch_shapes=[pltpu.VMEM((rows, width), F32)],
        ),
        compiler_params=pltpu.CompilerParams(vmem_limit_bytes=VMEM_LIMIT),
        cost_estimate=cost(6 * n * width * width, n * width * 8 + 6 * width * width),
        name="project_grad",
    )(table, dq, dk, dv, h)


def project_back_kernel(weight, count, tab, nrm_ref, dq_ref, dk_ref, dv_ref, x_ref, dx_ref, *rest):
    w_refs = rest[:count]
    out_ref, gn_ref, w_sc, sems = rest[-4:]
    t = pl.program_id(0)
    me = tab[tab.shape[0] - 1]
    width = x_ref.shape[1]

    @pl.when(t == 0)
    def _():
        copies = weight.copies(w_refs, w_sc, sems, me)
        for c in copies:
            c.start()
        gn_ref[...] = jnp.zeros_like(gn_ref)
        for c in copies:
            c.wait()

    tb = x_ref.shape[0]
    parts = [pl.ds(i, tb // 2) for i in range(0, tb, tb // 2)]
    units = [norm_stats(x_ref[p, :].astype(F32)) for p in parts]
    dgain = jnp.zeros((1, width), F32)
    dshift = jnp.zeros((1, width), F32)
    for p, (unit, rate) in zip(parts, units):
        grad = mm(dq_ref[p, :], w_sc[pl.ds(0, width), :], NN)
        grad += mm(dk_ref[p, :], w_sc[pl.ds(width, width), :], NN)
        grad += mm(dv_ref[p, :], w_sc[pl.ds(2 * width, width), :], NN)
        out_ref[p, :] = (dx_ref[p, :] + norm_back(unit, rate, nrm_ref[0:1, :], grad)).astype(BF)
        dgain += jnp.sum(grad * unit, axis=0, keepdims=True)
        dshift += jnp.sum(grad, axis=0, keepdims=True)
    gn_ref[0:1, :] += dgain
    gn_ref[1:2, :] += dshift


def project_back(table, norms, dq, dk, dv, x, dx, weight, row, before, tb=512):
    n, width = x.shape
    count = len(weight.arrays)
    anywhere = pl.BlockSpec(memory_space=pl.ANY)
    per = ROW_LEN // tb
    block = pl.BlockSpec((tb, width), lambda t, tab: (row * per + t, 0))
    fixed = pl.BlockSpec((8, width), lambda t, tab: (0, 0))
    before = [] if before is None else [before]
    return pl.pallas_call(
        partial(project_back_kernel, weight, count),
        out_shape=[jax.ShapeDtypeStruct((n, width), BF), jax.ShapeDtypeStruct((8, width), F32)],
        grid_spec=pltpu.PrefetchScalarGridSpec(
            num_scalar_prefetch=1,
            grid=(per,),
            in_specs=[fixed] + [block] * 5 + [anywhere] * (count + len(before)),
            out_specs=[block, fixed],
            scratch_shapes=[pltpu.VMEM((3 * width, width), BF), pltpu.SemaphoreType.DMA((count,))],
        ),
        input_output_aliases={7 + count: 0} if before else {},
        compiler_params=pltpu.CompilerParams(vmem_limit_bytes=VMEM_LIMIT),
        cost_estimate=cost(6 * ROW_LEN * width * width, ROW_LEN * width * 14 + 6 * width * width),
        name="project_back",
    )(table, norms, dq, dk, dv, x, dx, *weight.arrays, *before)


def gelu_both(values):
    phi = 0.5 + 0.5 * lax.erf(values * math.sqrt(0.5))
    bell = jnp.exp(values * values * -0.5) * (1.0 / math.sqrt(2.0 * math.pi))
    return values * phi, phi + values * bell


def down_copies(weight, refs, block, dst, sems, me):
    out = []
    for i, (ref, (slot, _)) in enumerate(zip(refs, weight.places)):
        src = ref.at[pl.ds(pl.multiple_of(block * weight.per, weight.per), weight.per), :]
        at = pl.multiple_of((me ^ slot) * weight.per, weight.per)
        out.append(pltpu.make_async_copy(src, dst.at[pl.ds(at, weight.per), :], sems.at[i]))
    return out


def middle_kernel(size, tb, sub, chunks, w_up, w_down, w_proj, tab, nrm_ref, att_ref, x_ref, cot_ref, *rest):
    ups, downs = len(w_up.arrays), len(w_down.arrays)
    up_refs, down_refs = rest[:ups], rest[ups : ups + downs]
    proj_refs = down_refs if size == 8 else rest[ups + downs : ups + downs + 1]
    outs = 1 if size == 8 else 3
    rest = rest[-(22 + outs) :]
    x1_ref, act_ref, dx_ref, da_ref, gn_ref = rest[:5]
    g_refs = rest[5 : 5 + outs]
    x1_sc, h_sc, ht_sc, dy_sc, dyt_sc, dh_sc, gu_sc, gd_sc, wp_sc, wu_sc, wd_sc, su_sc, sd_sc, p_sem, u_sem, d_sem, g_sem = rest[
        5 + outs :
    ]
    j = pl.program_id(0)
    t = pl.program_id(1)
    steps = pl.num_programs(1)
    me = tab[tab.shape[0] - 1]
    per = ROW_LEN // tb
    valid = tab[lax.div(t, per) * STRIDE + 33]
    ok = (lax.broadcasted_iota(jnp.int32, (tb, 1), 0) + lax.rem(t, per) * tb) < valid
    ts = pl.ds(pl.multiple_of(t * tb, tb), tb)
    width = x_ref.shape[1]
    gain = nrm_ref[2:3, :]
    shift = nrm_ref[3:4, :]
    parts = [pl.ds(pl.multiple_of(t * tb + i, sub), sub) for i in range(0, tb, sub)]
    pieces = [pl.ds(i, sub) for i in range(0, tb, sub)]

    def chunk_copies(m):
        b = m % 2
        if size != 8:
            piece = pl.ds(m * width, width)
            up = [pltpu.make_async_copy(up_refs[0].at[piece, :], wu_sc.at[b], u_sem.at[b, 0])]
            down = [pltpu.make_async_copy(down_refs[0].at[:, piece], wd_sc.at[b], d_sem.at[b, 0])]
            return up + down
        up = []
        for i, (ref, (slot, _)) in enumerate(zip(up_refs, w_up.places)):
            if slot // 2 == m:
                at = pl.multiple_of(((me & 1) ^ (slot & 1)) * w_up.per, w_up.per)
                into = wu_sc.at[b].at[pl.ds(at, w_up.per), :]
                up.append(pltpu.make_async_copy(ref, into, u_sem.at[b, len(up)]))
        return up + down_copies(w_down, down_refs, (me >> 1) ^ m, wd_sc.at[b], d_sem.at[b], me)

    def proj_copies():
        if size != 8:
            return [pltpu.make_async_copy(proj_refs[0], wp_sc, p_sem.at[0])]
        return down_copies(w_down, proj_refs, chunks, wp_sc, p_sem, me)

    def packed_copies(block, up_pair=None):
        fw, dw = w_up.per, w_down.per
        whole = fw + (chunks + 1) * dw
        out = []
        for d in range(8):
            at = pl.multiple_of(d * whole + fw + block * dw, dw)
            out.append(pltpu.make_async_copy(sd_sc.at[pl.ds(d * dw, dw), :], g_refs[0].at[pl.ds(at, dw), :], g_sem.at[d]))
        if up_pair is not None:
            for k in range(2):
                at = pl.multiple_of((2 * up_pair + k) * whole, dw)
                out.append(pltpu.make_async_copy(su_sc.at[k], g_refs[0].at[pl.ds(at, fw), :], g_sem.at[8 + k]))
        return out

    @pl.when((j == 0) & (t == 0))
    def _():
        for c in proj_copies() + chunk_copies(0):
            c.start()
        for c in proj_copies():
            c.wait()

    for m in range(chunks):

        @pl.when((j == m) & (t == 0))
        def _():
            for c in chunk_copies(m):
                c.wait()
            if m + 1 < chunks:
                for c in chunk_copies(m + 1):
                    c.start()

    @pl.when(j == 0)
    def _():
        dy = jnp.where(ok, cot_ref[...], BF(0))
        dy_sc[ts, :] = dy
        x1s = [x_ref[p, :].astype(F32) + mm(att_ref[p, :], wp_sc[...], NT) for p in pieces]
        dyt_sc[:, ts] = dy.T
        for p, full, x1 in zip(pieces, parts, x1s):
            x1_sc[full, :] = x1
            x1_ref[p, :] = x1
            unit, _ = norm_stats(x1)
            h = (unit * gain + shift).astype(BF)
            h_sc[full, :] = h
            ht_sc[:, full] = h.T
        dh_sc[ts, :] = jnp.zeros((tb, width), F32)

    @pl.when((t == 0) & (j < chunks))
    def _():
        gu_sc[...] = jnp.zeros_like(gu_sc)
        gd_sc[...] = jnp.zeros_like(gd_sc)

    @pl.when(j < chunks)
    def _():
        wu = wu_sc[lax.rem(j, 2)]
        wd = wd_sc[lax.rem(j, 2)]
        uppers = [mm(h_sc[p, :], wu, NT) for p in parts]
        acts = []
        dups = []
        for p, upper in zip(parts, uppers):
            dact = mm(dy_sc[p, :], wd, NN)
            act, slope = gelu_both(upper)
            acts.append(act.astype(BF))
            dups.append((dact * slope).astype(BF))
        for p, dup in zip(parts, dups):
            dh_sc[p, :] += mm(dup, wu, NN)
        act = jnp.concatenate(acts, axis=0)
        act_ref[...] = act
        gd_sc[...] += mm(dyt_sc[:, ts], act, NN)
        gu_sc[...] += mm(ht_sc[:, ts], jnp.concatenate(dups, axis=0), NN)

    @pl.when((t == steps - 1) & (j < chunks))
    def _():
        if size == 8:
            pair = (me >> 1) ^ j

            @pl.when(j > 0)
            def _():
                before = (me >> 1) ^ (j - 1)
                for c in packed_copies(before, before):
                    c.wait()

            fw = w_up.per
            for k in range(2):
                for i in range(2):
                    su_sc[k, :, i * fw : (i + 1) * fw] = gu_sc[i * fw : (i + 1) * fw, k * fw : (k + 1) * fw].astype(BF)
            sd_sc[...] = gd_sc[...].astype(BF)
            for c in packed_copies(pair, pair):
                c.start()
        else:
            g_refs[0][...] = gu_sc[...].astype(BF)
            g_refs[1][...] = gd_sc[...].astype(BF)

    @pl.when(j == chunks)
    def _():
        @pl.when(t == 0)
        def _():
            gu_sc[...] = jnp.zeros_like(gu_sc)
            gn_ref[...] = jnp.zeros_like(gn_ref)

        dgain = jnp.zeros((1, width), F32)
        dshift = jnp.zeros((1, width), F32)
        dbs = []
        for p, full in zip(pieces, parts):
            unit, rate = norm_stats(x1_sc[full, :])
            dh = dh_sc[full, :]
            dx = dy_sc[full, :].astype(F32) + norm_back(unit, rate, gain, dh)
            dx_ref[p, :] = dx
            dbs.append(dx.astype(BF))
            da_ref[p, :] = mm(dbs[-1], wp_sc[...], NN).astype(BF)
            dgain += jnp.sum(dh * unit, axis=0, keepdims=True)
            dshift += jnp.sum(dh, axis=0, keepdims=True)
        gu_sc[...] += mm(jnp.concatenate(dbs, axis=0), att_ref[...], TN)
        gn_ref[0:1, :] += dgain
        gn_ref[1:2, :] += dshift

        @pl.when(t == steps - 1)
        def _():
            if size == 8:
                before = (me >> 1) ^ (chunks - 1)
                for c in packed_copies(before, before):
                    c.wait()
                sd_sc[...] = gu_sc[...].astype(BF)
                for c in packed_copies(chunks):
                    c.start()
                for c in packed_copies(chunks):
                    c.wait()
            else:
                g_refs[2][...] = gu_sc[...].astype(BF)


def middle(table, norms, att, x, cot, w_up, w_down, w_proj, hidden, size, tb=512, sub=256):
    n, width = x.shape
    chunks = hidden // width
    steps = n // tb
    last = chunks - 1
    dev = table.shape[0] - 1
    first = lambda j, t, tab: (jnp.where(j == 0, t, steps - 1), 0)
    ends = lambda j, t, tab: (jnp.where((j == 0) | (j == chunks), t, steps - 1), 0)
    final = lambda j, t, tab: (jnp.where(j == chunks, t, 0), 0)
    fixed = lambda j, t, tab: (0, 0)
    anywhere = pl.BlockSpec(memory_space=pl.ANY)
    now = lambda j: jnp.minimum(j, last)
    sds = jax.ShapeDtypeStruct
    if size == 8:
        fw, dw = w_up.per, w_down.per
        pair = lambda j, tab: lax.bitwise_xor(lax.shift_right_logical(tab[dev], 1), now(j))
        assert hidden == 8 * fw and width == 2 * fw == 8 * dw
        g_shapes = [sds((8 * (fw + (chunks + 1) * dw), width), BF)]
        g_specs = [anywhere]
    else:
        pair = lambda j, tab: now(j)
        g_shapes = [sds((width, hidden), BF)] * 2 + [sds((width, width), BF)]
        g_specs = [pl.BlockSpec((width, width), lambda j, t, tab: (0, now(j)))] * 2 + [
            pl.BlockSpec((width, width), fixed)
        ]
    block = lambda index: pl.BlockSpec((tb, width), index)
    acts = lambda j, t, tab: (jnp.where(j == chunks, steps - 1, t), pair(j, tab))
    weights = w_up.arrays + w_down.arrays + w_proj.arrays
    dma = pltpu.SemaphoreType.DMA
    return pl.pallas_call(
        partial(middle_kernel, size, tb, sub, chunks, w_up, w_down, w_proj),
        out_shape=[
            sds((n, width), F32),
            sds((n, hidden), BF),
            sds((n, width), F32),
            sds((n, width), BF),
            sds((8, width), F32),
        ]
        + g_shapes,
        grid_spec=pltpu.PrefetchScalarGridSpec(
            num_scalar_prefetch=1,
            grid=(chunks + 1, steps),
            in_specs=[pl.BlockSpec((8, width), fixed), block(ends), block(first), block(first)]
            + [anywhere] * len(weights),
            out_specs=[block(first), block(acts), block(final), block(final), pl.BlockSpec((8, width), fixed)]
            + g_specs,
            scratch_shapes=[
                pltpu.VMEM((n, width), F32),
                pltpu.VMEM((n, width), BF),
                pltpu.VMEM((width, n), BF),
                pltpu.VMEM((n, width), BF),
                pltpu.VMEM((width, n), BF),
                pltpu.VMEM((n, width), F32),
                pltpu.VMEM((width, width), F32),
                pltpu.VMEM((width, width), F32),
                pltpu.VMEM((width, width), BF),
                pltpu.VMEM((2, width, width), BF),
                pltpu.VMEM((2, width, width), BF),
                pltpu.VMEM((2, width // 2, width), BF),
                pltpu.VMEM((width, width), BF),
                dma((8,)),
                dma((2, 2)),
                dma((2, 8)),
                dma((10,)),
            ],
        ),
        compiler_params=pltpu.CompilerParams(vmem_limit_bytes=VMEM_LIMIT),
        cost_estimate=cost(n * width * (10 * hidden + 6 * width), n * (width * 22 + 2 * hidden) + 8 * hidden * width),
        name="middle",
    )(table, norms, att, x, cot, *weights)


def finish_kernel(size, blocks, w_down, row, tab, x1_ref, act_ref, *rest):
    w_refs = rest[: len(w_down.arrays)]
    out_ref, w_sc, sems = rest[-3:]
    t = pl.program_id(0)
    me = tab[tab.shape[0] - 1]
    tb, width = x1_ref.shape

    def copies(b):
        if size == 8:
            return down_copies(w_down, w_refs, b, w_sc.at[:, pl.ds(b * width, width)], sems.at[b], me)
        at = pl.ds(b * width, width)
        return [pltpu.make_async_copy(w_refs[0].at[:, at], w_sc.at[:, at], sems.at[b, 0])]

    @pl.when(t == 0)
    def _():
        for b in range(blocks):
            for c in copies(b):
                c.start()
        for b in range(blocks):
            for c in copies(b):
                c.wait()

    x2 = x1_ref[...] + mm(act_ref[...], w_sc[...], NT)
    ok = (lax.broadcasted_iota(jnp.int32, (tb, 1), 0) + t * tb) < tab[row * STRIDE + 33]
    out_ref[...] = jnp.where(ok, x2, 0.0).astype(BF)


def finish(table, x1, act, w_down, row, before, size, tb=512):
    n, width = x1.shape
    hidden = act.shape[1]
    blocks = hidden // width
    per = ROW_LEN // tb
    before = [] if before is None else [before]
    count = len(w_down.arrays)
    block = lambda w: pl.BlockSpec((tb, w), lambda t, tab: (row * per + t, 0))
    return pl.pallas_call(
        partial(finish_kernel, size, blocks, w_down, row),
        out_shape=jax.ShapeDtypeStruct((n, width), BF),
        grid_spec=pltpu.PrefetchScalarGridSpec(
            num_scalar_prefetch=1,
            grid=(per,),
            in_specs=[block(width), block(hidden)] + [pl.BlockSpec(memory_space=pl.ANY)] * (count + len(before)),
            out_specs=block(width),
            scratch_shapes=[pltpu.VMEM((width, hidden), BF), pltpu.SemaphoreType.DMA((blocks, 8))],
        ),
        input_output_aliases={3 + count: 0} if before else {},
        compiler_params=pltpu.CompilerParams(vmem_limit_bytes=VMEM_LIMIT),
        cost_estimate=cost(2 * ROW_LEN * width * hidden, ROW_LEN * (width * 6 + hidden * 2) + 2 * width * hidden),
        name="finish",
    )(table, x1, act, *w_down.arrays, *before)


def per_device(
    size,
    replicas,
    tokens,
    segment_ids,
    cotangent,
    norm_params,
    qkv_weight,
    proj_weight,
    up_weight,
    down_weight,
    target_norms,
    target_qkv,
    target_proj,
    target_up,
    target_down,
):
    count, width = tokens.shape
    rows = count // ROW_LEN
    hidden = down_weight.shape[0]
    own = width // size
    blocks = hidden // width
    fast = size == 8 and replicas == 4
    size = size if fast else 0
    me = lax.axis_index("fsdp")
    table = job_table(segment_ids, rows, me)
    with jax.named_scope("gather_weights"):
        placed = lax.dynamic_update_slice(jnp.zeros((16, width), BF), norm_params, (0, me * own))
        qkv_t, up_t, down_t, proj_t = qkv_weight.T, up_weight.T, down_weight.T, proj_weight.T
        if fast:
            half = qkv_t.shape[0] // 2
            first, second = gather_cross(jnp.concatenate([qkv_t[:half], placed], axis=0), qkv_t[half:])
            far = forward_cross(first, second)
            upper = both_cores([*first, far[0]])
            lower = both_cores([*second, far[1]])
            w_qkv = Weight([(a, s, 0) for a, s in upper] + [(a, s, half) for a, s in lower], 2 * half)
            norm_parts = []
            packed = jnp.concatenate([down_t[:, b * width : (b + 1) * width] for b in range(blocks)] + [proj_t], axis=0)
            up_1, down_1 = after((up_t, packed), first[1], second[2])
            up_x, down_y = hop(up_1, 2, 8), hop(down_1, 4, 8)
            up_2, down_2 = after((up_t, packed), *far)
            up_y, down_x = hop(up_2, 4, 8), hop(down_2, 2, 8)
        else:
            whole = lambda shard: lax.all_gather(shard, "fsdp", axis=0, tiled=True)
            w_qkv, w_up, w_down, w_proj = (Weight([(whole(w), None, 0)], 0) for w in (qkv_t, up_t, down_t, proj_t))
            norm_parts = [lax.psum(placed.astype(F32), "fsdp").astype(BF)]

    keep_rate = 1.0 - ema_rate
    blend = lambda target, weight: ema_rate * target + keep_rate * weight.astype(F32)
    targets = (
        blend(target_norms, norm_params),
        blend(target_qkv, qkv_weight),
        blend(target_proj, proj_weight),
        blend(target_up, up_weight),
        blend(target_down, down_weight),
    )
    stage, *targets = lax.optimization_barrier((table, *targets))
    h1, qkv, norms = project(stage, norm_parts, tokens, w_qkv)
    attended = None
    stage = table
    if fast:
        with jax.named_scope("gather_weights"):
            up_x, down_y, up_t, packed = after((up_x, down_y, up_t, packed), qkv)
            up_far, down_far = forward_cross((None, up_x), (None, None, down_y))
            near = both_cores([up_t, up_x]), both_cores([packed])
            stage = after(table, up_x, down_y)
    for row in range(rows):
        attended = attention_forward(qkv, stage, row, attended)
        if fast and row == 0:
            with jax.named_scope("gather_weights"):
                up_y, down_x, down_y = after((up_y, down_x, down_y), attended[0])
                along = hop(up_y, 1, 8), hop(down_x, 1, 8), hop(down_y, 1, 8)
                stage = after(table, up_y, down_x, down_y)
    if fast:
        with jax.named_scope("gather_weights"):
            up_far, down_far = after((up_far, down_far), attended[0])
            ups = near[0] + [(up_y, 4), (along[0], 5), (up_far, 6), (hop(up_far, 1, 8), 7)]
            downs = near[1] + [(down_x, 2), (along[1], 3), (down_y, 4), (along[2], 5)]
            downs += [(down_far, 6), (hop(down_far, 1, 8), 7)]
            w_up = Weight([(a, s, 0) for a, s in ups], up_t.shape[0])
            w_down = Weight([(a, s, 0) for a, s in downs], own)
            w_proj = Weight([], own)
    x1, act, grad_middle, grad_attended, grad_norm2, *grads = middle(
        table, norms, attended[0], tokens, cotangent, w_up, w_down, w_proj, hidden, size
    )

    dqkv = None
    input_grad = None
    block_output = None
    norm_grads = []
    after_table = lambda *values: after(table, *values)
    if fast:
        packed_own = lax.psum_scatter(grads[0], "fsdp", scatter_dimension=0, tiled=True)
    for row in range(rows):
        dqkv = attention_backward(qkv, grad_attended, table, row, 0, 1, dqkv)
    if fast:
        grad_qkv = project_grad(table, *dqkv, h1, size)
        qkv_sum = Scatter(*grad_qkv)
        block_output = finish(after_table(grad_qkv[0]), x1, act, w_down, 0, None, size)
        stage = after_table(*qkv_sum.send(block_output))
        for row in range(1, rows):
            block_output = finish(stage, x1, act, w_down, row, block_output, size)
        packed_own = after(packed_own, block_output)
        packed_sum = lax.psum(packed_own, "rep")
        stage = after_table(packed_own)
        input_grad, part = project_back(stage, norms, *dqkv, tokens, grad_middle, w_qkv, 0, None)
        norm_grads.append(part)
        qkv_own = qkv_sum.block(part)
        stage = after_table(qkv_own)
        for row in range(1, rows):
            input_grad, part = project_back(stage, norms, *dqkv, tokens, grad_middle, w_qkv, row, input_grad)
            norm_grads.append(part)
        qkv_own = direct_sum(qkv_own, part)
        norm_sum = jnp.concatenate(
            [sum(p[:2] for p in norm_grads), grad_norm2[:2], jnp.zeros((4, width), F32)], axis=0
        )
        for bit in (1, 2, 4):
            norm_sum = norm_sum + hop(norm_sum, bit, 8)
        for bit in (1, 2):
            norm_sum = norm_sum + lax.ppermute(norm_sum, "rep", [(i, i ^ bit) for i in range(4)])
        packed_sum = packed_sum.astype(F32)
        fw = hidden // 8
        up = jnp.concatenate([packed_sum[:fw, :fw], packed_sum[:fw, fw:]], axis=0)
        down = packed_sum[fw : fw + blocks * own].reshape(blocks, own, width).transpose(1, 0, 2).reshape(own, hidden)
        proj = packed_sum[fw + blocks * own :]
    else:
        grad_qkv = project_grad(table, *dqkv, h1, size)
        for row in range(rows):
            input_grad, part = project_back(table, norms, *dqkv, tokens, grad_middle, w_qkv, row, input_grad)
            norm_grads.append(part)
            block_output = finish(table, x1, act, w_down, row, block_output, size)
        sums = lambda g, dim: lax.psum(lax.psum_scatter(g, "fsdp", scatter_dimension=dim, tiled=True), "rep").astype(F32)
        up, down, proj, qkv_own = sums(grads[0], 1), sums(grads[1], 0), sums(grads[2], 0), sums(grad_qkv[0], 0)
        norm_sum = jnp.concatenate([sum(p[:2] for p in norm_grads), grad_norm2[:2]], axis=0)
        norm_sum = lax.psum(norm_sum, ("fsdp", "rep"))
    norm_grad = lax.dynamic_slice(norm_sum, (0, me * own), (4, own))
    return (block_output, input_grad, norm_grad, qkv_own.T, proj.T, up, down.T, *targets)


def solution(mesh):
    tokens = P(("fsdp", "rep"), None)
    columns = P(None, "fsdp")
    return jax.shard_map(
        partial(per_device, mesh.shape["fsdp"], mesh.shape["rep"]),
        mesh=mesh,
        in_specs=(tokens, P(("fsdp", "rep")), tokens) + (columns,) * 10,
        out_specs=(tokens, tokens) + (columns,) * 10,
        check_vma=False,
    )
```

```python
import math
from functools import partial

import jax
import jax.numpy as jnp
from jax import lax
from jax.experimental import pallas as pl
from jax.experimental.pallas import tpu as pltpu
from jax.sharding import PartitionSpec as P

HEAD = 64
ROW_LEN = 1024
layer_eps = 1e-06
ema_rate = 0.75

BF = jnp.bfloat16
F32 = jnp.float32
NN = (((1,), (0,)), ((), ()))
NT = (((1,), (1,)), ((), ()))
TN = (((0,), (0,)), ((), ()))
VMEM_LIMIT = 66_000_000
GRANT = 32_000_000
COST_SCALE = 0.02

QW = 256
KW = 224
FIT = KW - 15
SMALL = 128
FIT_SMALL = SMALL - 15
KB = 128
STRIDE = 35


def mm(left, right, dims):
    return lax.dot_general(left, right, dims, preferred_element_type=F32)


def cost(flops, moved):
    return pl.CostEstimate(flops=int(flops * COST_SCALE), bytes_accessed=int(moved * COST_SCALE), transcendentals=0)


def job_table(segment_ids, rows, device):
    seg = segment_ids.reshape(rows, 1, ROW_LEN)
    ident = jnp.arange(16, dtype=jnp.int32)[None, :, None]
    real = seg >= 0
    starts = jnp.sum((real & (seg < ident)).astype(jnp.int32), axis=2)
    after = jnp.sum((real & (seg < ident + 1)).astype(jnp.int32), axis=2)
    images = jnp.max(seg, axis=2) + 1
    ends = jnp.where(jnp.arange(16, dtype=jnp.int32)[None, :] < images, after, ROW_LEN)
    valid = jnp.sum(real.astype(jnp.int32), axis=2)
    pad = ROW_LEN - valid
    fits = pad <= FIT
    jobs = images + jnp.where((pad > 0) & fits, 1, 0)
    wide = jnp.where(fits, 0, (pad + 15 + QW - 1) // QW)
    table = jnp.concatenate([starts, ends, jobs, valid, wide], axis=1).reshape(-1)
    return jnp.concatenate([table, device.astype(jnp.int32).reshape(1)])


def lane_of(count):
    return lax.broadcasted_iota(jnp.int32, (count, 128), 1)


def slot_of(count, base):
    return lax.broadcasted_iota(jnp.int32, (count, 128), 0) + base


def half_lanes(count, par):
    return (lane_of(count) < 64) if par == 0 else (lane_of(count) >= 64)


def spare_lane(count, par):
    return lane_of(count) == (64 if par == 0 else 0)


def query_side(q, par):
    n = q.shape[0]
    return jnp.where(half_lanes(n, par), q * BF(0.125), jnp.where(spare_lane(n, par), BF(1), BF(0)))


def key_side(k, par, inside):
    n = k.shape[0]
    return jnp.where(half_lanes(n, par), k, jnp.where(spare_lane(n, par) & (~inside), BF(-1e30), BF(0)))


def one_head(x, par):
    return jnp.where(half_lanes(x.shape[0], par), x, BF(0))


def each_image(tab, base, work):
    def job(j, carry):
        begin = tab[base + j]
        end = tab[base + 16 + j]
        low = lax.div(begin, 16) * 16
        small = end - begin <= FIT_SMALL
        for fits, nq, nk in ((small, SMALL, SMALL), (~small, QW, KW)):

            @pl.when(fits)
            def _():
                q0 = pl.multiple_of(jnp.minimum(low, ROW_LEN - nq), 16)
                k0 = pl.multiple_of(jnp.minimum(low, ROW_LEN - nk), 16)
                kr = slot_of(nk, k0)
                qr = slot_of(nq, q0)
                work(pl.ds(q0, nq), pl.ds(k0, nk), (qr >= begin) & (qr < end), (kr >= begin) & (kr < end))

        return carry

    lax.fori_loop(0, tab[base + 32], job, 0)


def attend_kernel(pairs, tab, q_ref, k_ref, v_ref, o_ref, a_sc):
    base = pl.program_id(0) * STRIDE
    o_ref[...] = jnp.zeros_like(o_ref)

    def work(qs, ks, qin, inside):
        scores = []
        for p in range(pairs):
            cs = pl.ds(128 * p, 128)
            q = q_ref[qs, cs]
            k = k_ref[ks, cs]
            for par in range(2):
                scores.append(mm(key_side(k, par, inside), query_side(q, par), NT))
        probs = []
        for st in scores:
            expo = jnp.exp(st - jnp.max(st, axis=0, keepdims=True))
            total = jnp.sum(expo, axis=0, keepdims=True)
            probs.append((expo * (1.0 / total)).astype(BF))
        for p in range(pairs):
            cs = pl.ds(128 * p, 128)
            v = v_ref[ks, cs]
            o = jnp.concatenate(
                [mm(v[:, 64 * par : 64 * par + 64], probs[2 * p + par], TN) for par in range(2)], axis=0
            ).T
            o_ref[qs, cs] = jnp.where(qin, o.astype(BF), o_ref[qs, cs])

    each_image(tab, base, work)

    start = tab[base + 33]
    low = lax.div(start, 16) * 16

    def wide(i, carry):
        q0 = pl.multiple_of(jnp.minimum(low + i * QW, ROW_LEN - QW), 16)
        qin = slot_of(QW, q0) >= start

        def pair(p, none):
            cs = pl.ds(pl.multiple_of(128 * p, 128), 128)
            q = q_ref[pl.ds(q0, QW), cs]
            for par in range(2):
                qs = query_side(q, par)

                def block(kb):
                    k0 = pl.multiple_of(kb * KB, KB)
                    k = k_ref[pl.ds(k0, KB), cs]
                    return k0, mm(key_side(k, par, slot_of(KB, k0) >= start), qs, NT)

                def take_max(kb, top):
                    return jnp.maximum(top, jnp.max(block(kb)[1], axis=0, keepdims=True))

                top = lax.fori_loop(0, ROW_LEN // KB, take_max, jnp.full((1, QW), -1e30, F32))

                def take_sum(kb, total):
                    return total + jnp.sum(jnp.exp(block(kb)[1] - top), axis=0, keepdims=True)

                total = lax.fori_loop(0, ROW_LEN // KB, take_sum, jnp.zeros((1, QW), F32))
                a_sc[...] = jnp.zeros_like(a_sc)

                def take_out(kb, c):
                    k0, st = block(kb)
                    prob = (jnp.exp(st - top) * (1.0 / total)).astype(BF)
                    a_sc[...] += mm(one_head(v_ref[pl.ds(k0, KB), cs], par), prob, TN)
                    return c

                lax.fori_loop(0, ROW_LEN // KB, take_out, 0)
                hit = qin & half_lanes(QW, par)
                o_ref[pl.ds(q0, QW), cs] = jnp.where(hit, a_sc[...].T.astype(BF), o_ref[pl.ds(q0, QW), cs])
            return none

        lax.fori_loop(0, pairs, pair, 0)
        return carry

    lax.fori_loop(0, tab[base + 34], wide, 0)


def attend_back_kernel(pairs, tab, q_ref, k_ref, v_ref, d_ref, *rest):
    dq_ref, dk_ref, dv_ref, a_sc, dk_sc, dv_sc = rest[-6:]
    base = pl.program_id(0) * STRIDE
    dq_ref[...] = jnp.zeros_like(dq_ref)
    dk_ref[...] = jnp.zeros_like(dk_ref)
    dv_ref[...] = jnp.zeros_like(dv_ref)

    def work(qs, ks, qin, inside):
        scores = []
        grads = []
        for p in range(pairs):
            cs = pl.ds(128 * p, 128)
            q = q_ref[qs, cs]
            k = k_ref[ks, cs]
            v = v_ref[ks, cs]
            d = jnp.where(qin, d_ref[qs, cs], BF(0))
            for par in range(2):
                scores.append(mm(key_side(k, par, inside), query_side(q, par), NT))
                grads.append(mm(v, one_head(d, par), NT))
        probs = []
        dscores = []
        for st, dp in zip(scores, grads):
            expo = jnp.exp(st - jnp.max(st, axis=0, keepdims=True))
            total = jnp.sum(expo, axis=0, keepdims=True)
            prob = expo * (1.0 / total)
            center = jnp.sum(prob * dp, axis=0, keepdims=True)
            dscores.append((prob * (dp - center)).astype(BF))
            probs.append(prob.astype(BF))
        for p in range(pairs):
            cs = pl.ds(128 * p, 128)
            q = q_ref[qs, cs]
            k = k_ref[ks, cs]
            d = jnp.where(qin, d_ref[qs, cs], BF(0))
            dv = mm(probs[2 * p], one_head(d, 0), NN) + mm(probs[2 * p + 1], one_head(d, 1), NN)
            dk = mm(dscores[2 * p], one_head(q, 0), NN) + mm(dscores[2 * p + 1], one_head(q, 1), NN)
            dq = jnp.concatenate(
                [mm(k[:, 64 * par : 64 * par + 64], dscores[2 * p + par], TN) for par in range(2)], axis=0
            ).T
            dq_ref[qs, cs] = jnp.where(qin, (dq * 0.125).astype(BF), dq_ref[qs, cs])
            dk_ref[ks, cs] = jnp.where(inside, (dk * 0.125).astype(BF), dk_ref[ks, cs])
            dv_ref[ks, cs] = jnp.where(inside, dv.astype(BF), dv_ref[ks, cs])

    each_image(tab, base, work)

    start = tab[base + 33]
    low = lax.div(start, 16) * 16
    windows = tab[base + 34]

    def pair(p, none):
        cs = pl.ds(pl.multiple_of(128 * p, 128), 128)

        @pl.when(windows > 0)
        def _():
            dk_sc[...] = jnp.zeros_like(dk_sc)
            dv_sc[...] = jnp.zeros_like(dv_sc)

        def wide(i, carry):
            first = jnp.maximum(start, low + i * QW)
            q0 = pl.multiple_of(jnp.minimum(low + i * QW, ROW_LEN - QW), 16)
            qin = slot_of(QW, q0) >= first
            q = q_ref[pl.ds(q0, QW), cs]
            d = jnp.where(qin, d_ref[pl.ds(q0, QW), cs], BF(0))
            for par in range(2):
                qh = query_side(q, par)
                dh = one_head(d, par)
                qo = one_head(q, par)

                def block(kb):
                    k0 = pl.multiple_of(kb * KB, KB)
                    k = k_ref[pl.ds(k0, KB), cs]
                    v = v_ref[pl.ds(k0, KB), cs]
                    return k0, k, mm(key_side(k, par, slot_of(KB, k0) >= start), qh, NT), mm(v, dh, NT)

                def take_max(kb, top):
                    return jnp.maximum(top, jnp.max(block(kb)[2], axis=0, keepdims=True))

                top = lax.fori_loop(0, ROW_LEN // KB, take_max, jnp.full((1, QW), -1e30, F32))

                def take_sums(kb, sums):
                    _, _, st, dp = block(kb)
                    expo = jnp.exp(st - top)
                    return (
                        sums[0] + jnp.sum(expo, axis=0, keepdims=True),
                        sums[1] + jnp.sum(expo * dp, axis=0, keepdims=True),
                    )

                none = jnp.zeros((1, QW), F32)
                total, weighted = lax.fori_loop(0, ROW_LEN // KB, take_sums, (none, none))
                scale = 1.0 / total
                center = weighted * scale
                a_sc[...] = jnp.zeros_like(a_sc)

                def take_grads(kb, c):
                    k0, k, st, dp = block(kb)
                    prob = jnp.exp(st - top) * scale
                    ds = (prob * (dp - center)).astype(BF)
                    a_sc[...] += mm(one_head(k, par), ds, TN)
                    dk_sc[pl.ds(k0, KB), :] += mm(ds, qo, NN)
                    dv_sc[pl.ds(k0, KB), :] += mm(prob.astype(BF), dh, NN)
                    return c

                lax.fori_loop(0, ROW_LEN // KB, take_grads, 0)
                hit = qin & half_lanes(QW, par)
                dq = (a_sc[...].T * 0.125).astype(BF)
                dq_ref[pl.ds(q0, QW), cs] = jnp.where(hit, dq, dq_ref[pl.ds(q0, QW), cs])
            return carry

        lax.fori_loop(0, windows, wide, 0)

        @pl.when(windows > 0)
        def _():
            kin = slot_of(ROW_LEN, 0) >= start
            dk_ref[:, cs] = jnp.where(kin, (dk_sc[...] * 0.125).astype(BF), dk_ref[:, cs])
            dv_ref[:, cs] = jnp.where(kin, dv_sc[...].astype(BF), dv_ref[:, cs])

        return none

    lax.fori_loop(0, jnp.where(windows > 0, pairs, 0), pair, 0)


def attention_call(kernel, name, outs, scratch, qkv, extra, table, rows, flops, moved):
    n = qkv.shape[0]
    width = qkv.shape[1] // 3
    spec = lambda part: pl.BlockSpec((ROW_LEN, width), lambda r, t: (r, part))
    return pl.pallas_call(
        partial(kernel, width // 128),
        out_shape=[jax.ShapeDtypeStruct((n, width), BF)] * outs,
        grid_spec=pltpu.PrefetchScalarGridSpec(
            num_scalar_prefetch=1,
            grid=(rows,),
            in_specs=[spec(0), spec(1), spec(2)] + [spec(0)] * len(extra),
            out_specs=[spec(0)] * outs,
            scratch_shapes=scratch,
        ),
        compiler_params=pltpu.CompilerParams(vmem_limit_bytes=VMEM_LIMIT),
        cost_estimate=cost(rows * flops, rows * moved * ROW_LEN * width),
        name=name,
    )(table, qkv, qkv, qkv, *extra)


def attention_forward(qkv, table, rows):
    scratch = [pltpu.VMEM((128, QW), F32)]
    return attention_call(attend_kernel, "attend", 1, scratch, qkv, [], table, rows, 12e9, 8)[0]


def attention_backward(qkv, da, table, rows):
    scratch = [pltpu.VMEM((128, QW), F32), pltpu.VMEM((ROW_LEN, 128), F32), pltpu.VMEM((ROW_LEN, 128), F32)]
    return attention_call(attend_back_kernel, "attend_back", 3, scratch, qkv, [da], table, rows, 24e9, 14)


def hop(value, bit, size):
    return lax.ppermute(value, "fsdp", [(i, i ^ bit) for i in range(size)])


def gather_cross(first, second):
    first_x, second_y = hop(first, 2, 8), hop(second, 4, 8)
    first_late, second_late = after((first, second), hop(second[:16], 1, 8))
    first_y, second_x = hop(first_late, 4, 8), hop(second_late, 2, 8)
    return (first, first_x, first_y), (second, second_x, second_y)


def forward_cross(firsts, seconds):
    return hop(firsts[1], 4, 8), hop(seconds[2], 2, 8)


def both_cores(arrays):
    own = [(array, 2 * i) for i, array in enumerate(arrays)]
    return own + [(hop(array, 1, 8), slot + 1) for array, slot in own]


def after(value, *others):
    return lax.optimization_barrier((value, *others))[0]


def total(*terms):
    return sum(t.astype(F32) for t in terms).astype(BF)


class Scatter:
    def __init__(self, even, odd):
        self.even = even
        self.core = hop(odd, 1, 8)

    def send(self):
        self.out = [total(self.even[q], self.core[q]) for q in (1, 2, 3)]
        return self.out

    def block(self, done):
        come = after([hop(block, 2 * q, 8) for q, block in zip((1, 2, 3), self.out)], done)
        return total(self.even[0], self.core[0], *come)


def shift(value, by):
    return lax.ppermute(value, "rep", [(i, (i + by) % 4) for i in range(4)])


def quarter_sum(block, done):
    z = lax.axis_index("rep")
    quarters = block.reshape(4, block.shape[0] // 4, block.shape[1])
    pick = lambda by: lax.dynamic_index_in_dim(quarters, lax.rem(z + by, 4), 0, False)
    return total(pick(0), *after([shift(pick(by), by) for by in (2, 1, 3)], done))


def all_quarters(mine):
    z = lax.axis_index("rep")
    parts = [mine] + [shift(mine, by) for by in (1, 2, 3)]
    out = jnp.zeros((4, *mine.shape), F32)
    for by, part in enumerate(parts):
        out = lax.dynamic_update_index_in_dim(out, part.astype(F32), lax.rem(z - by + 4, 4), 0)
    return out.reshape(4 * mine.shape[0], mine.shape[1])


class Weight:
    def __init__(self, pieces, per):
        self.arrays = [p[0] for p in pieces]
        self.places = [p[1:] for p in pieces]
        self.per = per

    def copies(self, refs, dst, sems, me):
        out = []
        for i, (ref, (slot, row)) in enumerate(zip(refs, self.places)):
            src, into = ref, dst
            if slot is not None:
                half = self.per // 2
                src = ref.at[pl.ds(0, half), :]
                into = dst.at[pl.ds(pl.multiple_of((me ^ slot) * self.per + row, half), half), :]
            out.append(pltpu.make_async_copy(src, into, sems.at[i]))
        return out


def norm_stats(values):
    center = values - jnp.mean(values, axis=1, keepdims=True)
    rate = lax.rsqrt(jnp.mean(center * center, axis=1, keepdims=True) + layer_eps)
    return center * rate, rate


def norm_back(unit, rate, gain, grad):
    scaled = grad * gain
    mean = jnp.mean(scaled, axis=1, keepdims=True)
    along = jnp.mean(scaled * unit, axis=1, keepdims=True)
    return rate * (scaled - mean - unit * along)


def project_kernel(weight, count, tab, x_ref, *rest):
    w_refs = rest[:count]
    h_ref, qkv_ref, nrm_ref, w_sc, n_sc, sems, n_sems = rest[-7:]
    me = tab[tab.shape[0] - 1]
    half = weight.per // 2

    @pl.when(pl.program_id(0) == 0)
    def _():
        if len(rest) - 7 > count:
            norm_copies = [pltpu.make_async_copy(rest[count], n_sc.at[0], n_sems.at[0])]
        else:
            norm_copies = [
                pltpu.make_async_copy(w_refs[i].at[pl.ds(half, 16), :], n_sc.at[i], n_sems.at[i]) for i in range(8)
            ]
        copies = weight.copies(w_refs, w_sc, sems, me)
        for c in norm_copies + copies:
            c.start()
        for c in norm_copies:
            c.wait()
        placed = sum(n_sc[i].astype(F32) for i in range(len(norm_copies)))
        nrm_ref[...] = placed[:8, :]

    tb, width = x_ref.shape
    parts = [pl.ds(i, tb // 2) for i in range(0, tb, tb // 2)]
    for p in parts:
        unit, _ = norm_stats(x_ref[p, :].astype(F32))
        h_ref[p, :] = (unit * nrm_ref[0:1, :] + nrm_ref[1:2, :]).astype(BF)

    @pl.when(pl.program_id(0) == 0)
    def _():
        for c in weight.copies(w_refs, w_sc, sems, me):
            c.wait()

    for p in parts:
        qkv_ref[p, :] = mm(h_ref[p, :], w_sc[...], NT).astype(BF)


def project(table, norm_parts, x, weight, tb=512):
    n, width = x.shape
    count = len(weight.arrays)
    anywhere = pl.BlockSpec(memory_space=pl.ANY)
    block = lambda w: pl.BlockSpec((tb, w), lambda t, tab: (t, 0))
    sds = jax.ShapeDtypeStruct
    return pl.pallas_call(
        partial(project_kernel, weight, count),
        out_shape=[sds((n, width), BF), sds((n, 3 * width), BF), sds((8, width), F32)],
        grid_spec=pltpu.PrefetchScalarGridSpec(
            num_scalar_prefetch=1,
            grid=(n // tb,),
            in_specs=[block(width)] + [anywhere] * (count + len(norm_parts)),
            out_specs=[block(width), block(3 * width), pl.BlockSpec((8, width), lambda t, tab: (0, 0))],
            scratch_shapes=[
                pltpu.VMEM((3 * width, width), BF),
                pltpu.VMEM((8, 16, width), BF),
                pltpu.SemaphoreType.DMA((count,)),
                pltpu.SemaphoreType.DMA((8,)),
            ],
        ),
        compiler_params=pltpu.CompilerParams(vmem_limit_bytes=VMEM_LIMIT),
        cost_estimate=cost(6 * n * width * width, n * width * 10 + 6 * width * width),
        name="project",
    )(table, x, *weight.arrays, *norm_parts)


def by_owner(acc, per, even_ref, odd_ref, me):
    for q in range(4):
        for parity, ref in ((0, even_ref), (1, odd_ref)):
            at = pl.multiple_of((me ^ (2 * q + parity)) * per, per)
            ref[q] = acc[pl.ds(at, per), :].astype(BF)


def project_grad_kernel(size, tab, dq_ref, dk_ref, dv_ref, h_ref, *rest):
    acc = rest[-1]
    t = pl.program_id(0)
    width = h_ref.shape[1]

    @pl.when(t == 0)
    def _():
        acc[...] = jnp.zeros_like(acc)

    for part, ref in enumerate((dq_ref, dk_ref, dv_ref)):
        acc[pl.ds(part * width, width), :] += mm(ref[...], h_ref[...], TN)

    @pl.when(t == pl.num_programs(0) - 1)
    def _():
        if size == 8:
            per = acc.shape[0] // 8
            by_owner(acc, per, *(ref.at[:, pl.ds(0, per), :] for ref in rest[2:4]), tab[tab.shape[0] - 1])
            for src, dst in zip(rest[0:2], rest[2:4]):
                dst[:, pl.ds(per, src.shape[1]), :] = src[...]
        else:
            rest[0][...] = acc[...].astype(BF)


def project_grad(table, dq, dk, dv, h, proj, size, tb=512):
    n, width = h.shape
    rows = 3 * width
    block = pl.BlockSpec((tb, width), lambda t, tab: (t, 0))
    whole = lambda s: pl.BlockSpec(s, lambda t, tab, k=len(s): (0,) * k)
    shapes = [(4, rows // 8 + proj[0].shape[1], width)] * 2 if size == 8 else [(rows, width)]
    return pl.pallas_call(
        partial(project_grad_kernel, size),
        out_shape=[jax.ShapeDtypeStruct(s, BF) for s in shapes],
        grid_spec=pltpu.PrefetchScalarGridSpec(
            num_scalar_prefetch=1,
            grid=(n // tb,),
            in_specs=[block] * 4 + [whole(p.shape) for p in proj],
            out_specs=[whole(s) for s in shapes],
            scratch_shapes=[pltpu.VMEM((rows, width), F32)],
        ),
        compiler_params=pltpu.CompilerParams(vmem_limit_bytes=VMEM_LIMIT),
        cost_estimate=cost(6 * n * width * width, n * width * 8 + 6 * width * width),
        name="project_grad",
    )(table, dq, dk, dv, h, *proj)


def project_back_kernel(weight, count, tab, nrm_ref, dq_ref, dk_ref, dv_ref, x_ref, dx_ref, *rest):
    w_refs = rest[:count]
    out_ref, gn_ref, w_sc, sems = rest[-4:]
    t = pl.program_id(0)
    me = tab[tab.shape[0] - 1]
    width = x_ref.shape[1]

    @pl.when(t == 0)
    def _():
        copies = weight.copies(w_refs, w_sc, sems, me)
        for c in copies:
            c.start()
        gn_ref[...] = jnp.zeros_like(gn_ref)
        for c in copies:
            c.wait()

    tb = x_ref.shape[0]
    parts = [pl.ds(i, tb // 2) for i in range(0, tb, tb // 2)]
    units = [norm_stats(x_ref[p, :].astype(F32)) for p in parts]
    dgain = jnp.zeros((1, width), F32)
    dshift = jnp.zeros((1, width), F32)
    for p, (unit, rate) in zip(parts, units):
        grad = mm(dq_ref[p, :], w_sc[pl.ds(0, width), :], NN)
        grad += mm(dk_ref[p, :], w_sc[pl.ds(width, width), :], NN)
        grad += mm(dv_ref[p, :], w_sc[pl.ds(2 * width, width), :], NN)
        out_ref[p, :] = (dx_ref[p, :] + norm_back(unit, rate, nrm_ref[0:1, :], grad)).astype(BF)
        dgain += jnp.sum(grad * unit, axis=0, keepdims=True)
        dshift += jnp.sum(grad, axis=0, keepdims=True)
    gn_ref[0:1, :] += dgain
    gn_ref[1:2, :] += dshift


def project_back(table, norms, dq, dk, dv, x, dx, weight, tb=256):
    n, width = x.shape
    count = len(weight.arrays)
    anywhere = pl.BlockSpec(memory_space=pl.ANY)
    block = pl.BlockSpec((tb, width), lambda t, tab: (t, 0))
    fixed = pl.BlockSpec((8, width), lambda t, tab: (0, 0))
    return pl.pallas_call(
        partial(project_back_kernel, weight, count),
        out_shape=[jax.ShapeDtypeStruct((n, width), BF), jax.ShapeDtypeStruct((8, width), F32)],
        grid_spec=pltpu.PrefetchScalarGridSpec(
            num_scalar_prefetch=1,
            grid=(n // tb,),
            in_specs=[fixed] + [block] * 5 + [anywhere] * count,
            out_specs=[block, fixed],
            scratch_shapes=[pltpu.VMEM((3 * width, width), BF), pltpu.SemaphoreType.DMA((count,))],
        ),
        compiler_params=pltpu.CompilerParams(vmem_limit_bytes=VMEM_LIMIT),
        cost_estimate=cost(6 * n * width * width, n * width * 14 + 6 * width * width),
        name="project_back",
    )(table, norms, dq, dk, dv, x, dx, *weight.arrays)


def gelu_both(values):
    phi = 0.5 + 0.5 * lax.erf(values * math.sqrt(0.5))
    bell = jnp.exp(values * values * -0.5) * (1.0 / math.sqrt(2.0 * math.pi))
    return values * phi, phi + values * bell


def down_copies(weight, refs, block, dst, sems, me):
    out = []
    for i, (ref, (slot, _)) in enumerate(zip(refs, weight.places)):
        src = ref.at[pl.ds(pl.multiple_of(block * weight.per, weight.per), weight.per), :]
        at = pl.multiple_of((me ^ slot) * weight.per, weight.per)
        out.append(pltpu.make_async_copy(src, dst.at[pl.ds(at, weight.per), :], sems.at[i]))
    return out


def middle_kernel(size, tb, sub, chunks, w_up, w_down, w_proj, tab, nrm_ref, att_ref, x_ref, cot_ref, *rest):
    ups, downs = len(w_up.arrays), len(w_down.arrays)
    up_refs, down_refs = rest[:ups], rest[ups : ups + downs]
    proj_refs = down_refs if size == 8 else rest[ups + downs : ups + downs + 1]
    outs = 1 if size == 8 else 2
    rest = rest[-(19 + outs) :]
    x1_ref, act_ref, dh_ref = rest[:3]
    g_refs = rest[3 : 3 + outs]
    h_sc, ht_sc, dy_sc, dyt_sc, dh_sc, gu_sc, gd_sc, wp_sc, wu_sc, wd_sc, su_sc, sd_sc, p_sem, u_sem, d_sem, g_sem = rest[3 + outs :]
    j = pl.program_id(0)
    t = pl.program_id(1)
    steps = pl.num_programs(1)
    me = tab[tab.shape[0] - 1]
    per = ROW_LEN // tb
    valid = tab[lax.div(t, per) * STRIDE + 33]
    ok = (lax.broadcasted_iota(jnp.int32, (tb, 1), 0) + lax.rem(t, per) * tb) < valid
    ts = pl.ds(pl.multiple_of(t * tb, tb), tb)
    width = x_ref.shape[1]
    gain = nrm_ref[2:3, :]
    shift = nrm_ref[3:4, :]
    parts = [pl.ds(pl.multiple_of(t * tb + i, sub), sub) for i in range(0, tb, sub)]
    pieces = [pl.ds(i, sub) for i in range(0, tb, sub)]

    def chunk_copies(m):
        b = m % 2
        if size != 8:
            piece = pl.ds(m * width, width)
            up = [pltpu.make_async_copy(up_refs[0].at[piece, :], wu_sc.at[b], u_sem.at[b, 0])]
            down = [pltpu.make_async_copy(down_refs[0].at[:, piece], wd_sc.at[b], d_sem.at[b, 0])]
            return up + down
        up = []
        for i, (ref, (slot, _)) in enumerate(zip(up_refs, w_up.places)):
            if slot // 2 == m:
                at = pl.multiple_of(((me & 1) ^ (slot & 1)) * w_up.per, w_up.per)
                into = wu_sc.at[b].at[pl.ds(at, w_up.per), :]
                up.append(pltpu.make_async_copy(ref, into, u_sem.at[b, len(up)]))
        return up + down_copies(w_down, down_refs, (me >> 1) ^ m, wd_sc.at[b], d_sem.at[b], me)

    def proj_copies():
        if size != 8:
            return [pltpu.make_async_copy(proj_refs[0], wp_sc, p_sem.at[0])]
        return down_copies(w_down, proj_refs, chunks, wp_sc, p_sem, me)

    def packed_copies(pair):
        fw, dw = w_up.per, w_down.per
        whole = fw + chunks * dw
        out = []
        for d in range(8):
            at = pl.multiple_of(d * whole + fw + pair * dw, dw)
            out.append(pltpu.make_async_copy(sd_sc.at[pl.ds(d * dw, dw), :], g_refs[0].at[pl.ds(at, dw), :], g_sem.at[d]))
        for k in range(2):
            at = pl.multiple_of((2 * pair + k) * whole, dw)
            out.append(pltpu.make_async_copy(su_sc.at[k], g_refs[0].at[pl.ds(at, fw), :], g_sem.at[8 + k]))
        return out

    @pl.when((j == 0) & (t == 0))
    def _():
        for c in proj_copies() + chunk_copies(0):
            c.start()
        for c in proj_copies():
            c.wait()

    for m in range(chunks):

        @pl.when((j == m) & (t == 0))
        def _():
            for c in chunk_copies(m):
                c.wait()
            if m + 1 < chunks:
                for c in chunk_copies(m + 1):
                    c.start()

    @pl.when(j == 0)
    def _():
        dy = jnp.where(ok, cot_ref[...], BF(0))
        dy_sc[ts, :] = dy
        x1s = [x_ref[p, :].astype(F32) + mm(att_ref[p, :], wp_sc[...], NT) for p in pieces]
        dyt_sc[:, ts] = dy.T
        for p, full, x1 in zip(pieces, parts, x1s):
            x1_ref[p, :] = x1
            unit, _ = norm_stats(x1)
            h = (unit * gain + shift).astype(BF)
            h_sc[full, :] = h
            ht_sc[:, full] = h.T
        dh_sc[ts, :] = jnp.zeros((tb, width), F32)

    @pl.when(t == 0)
    def _():
        gu_sc[...] = jnp.zeros_like(gu_sc)
        gd_sc[...] = jnp.zeros_like(gd_sc)

    wu = wu_sc[lax.rem(j, 2)]
    wd = wd_sc[lax.rem(j, 2)]
    uppers = [mm(h_sc[p, :], wu, NT) for p in parts]
    acts = []
    dups = []
    for p, upper in zip(parts, uppers):
        dact = mm(dy_sc[p, :], wd, NN)
        act, slope = gelu_both(upper)
        acts.append(act.astype(BF))
        dups.append((dact * slope).astype(BF))
    for p, dup in zip(parts, dups):
        dh_sc[p, :] += mm(dup, wu, NN)
    act = jnp.concatenate(acts, axis=0)
    act_ref[...] = act
    gd_sc[...] += mm(dyt_sc[:, ts], act, NN)
    gu_sc[...] += mm(ht_sc[:, ts], jnp.concatenate(dups, axis=0), NN)

    @pl.when(j == chunks - 1)
    def _():
        dh_ref[...] = dh_sc[ts, :]

    @pl.when(t == steps - 1)
    def _():
        if size == 8:
            pair = (me >> 1) ^ j

            @pl.when(j > 0)
            def _():
                for c in packed_copies((me >> 1) ^ (j - 1)):
                    c.wait()

            fw = w_up.per
            for k in range(2):
                for i in range(2):
                    su_sc[k, :, i * fw : (i + 1) * fw] = gu_sc[i * fw : (i + 1) * fw, k * fw : (k + 1) * fw].astype(BF)
            sd_sc[...] = gd_sc[...].astype(BF)
            for c in packed_copies(pair):
                c.start()

            @pl.when(j == chunks - 1)
            def _():
                for c in packed_copies(pair):
                    c.wait()
        else:
            g_refs[0][...] = gu_sc[...].astype(BF)
            g_refs[1][...] = gd_sc[...].astype(BF)


def middle(table, norms, att, x, cot, w_up, w_down, w_proj, hidden, size, tb=512, sub=256):
    n, width = x.shape
    chunks = hidden // width
    steps = n // tb
    dev = table.shape[0] - 1
    first = lambda j, t, tab: (jnp.where(j == 0, t, steps - 1), 0)
    final = lambda j, t, tab: (jnp.where(j == chunks - 1, t, 0), 0)
    fixed = lambda j, t, tab: (0, 0)
    anywhere = pl.BlockSpec(memory_space=pl.ANY)
    sds = jax.ShapeDtypeStruct
    if size == 8:
        fw, dw = w_up.per, w_down.per
        assert hidden == 8 * fw and width == 2 * fw == 8 * dw
        pair = lambda j, tab: lax.bitwise_xor(lax.shift_right_logical(tab[dev], 1), j)
        g_shapes = [sds((8 * (fw + chunks * dw), width), BF)]
        g_specs = [anywhere]
    else:
        pair = lambda j, tab: j
        g_shapes = [sds((width, hidden), BF)] * 2
        g_specs = [pl.BlockSpec((width, width), lambda j, t, tab: (0, j))] * 2
    block = lambda index: pl.BlockSpec((tb, width), index)
    weights = w_up.arrays + w_down.arrays + w_proj.arrays
    dma = pltpu.SemaphoreType.DMA
    return pl.pallas_call(
        partial(middle_kernel, size, tb, sub, chunks, w_up, w_down, w_proj),
        out_shape=[sds((n, width), F32), sds((n, hidden), BF), sds((n, width), F32)] + g_shapes,
        grid_spec=pltpu.PrefetchScalarGridSpec(
            num_scalar_prefetch=1,
            grid=(chunks, steps),
            in_specs=[pl.BlockSpec((8, width), fixed)] + [block(first)] * 3 + [anywhere] * len(weights),
            out_specs=[block(first), block(lambda j, t, tab: (t, pair(j, tab))), block(final)] + g_specs,
            scratch_shapes=[
                pltpu.VMEM((n, width), BF),
                pltpu.VMEM((width, n), BF),
                pltpu.VMEM((n, width), BF),
                pltpu.VMEM((width, n), BF),
                pltpu.VMEM((n, width), F32),
                pltpu.VMEM((width, width), F32),
                pltpu.VMEM((width, width), F32),
                pltpu.VMEM((width, width), BF),
                pltpu.VMEM((2, width, width), BF),
                pltpu.VMEM((2, width, width), BF),
                pltpu.VMEM((2, width // 2, width), BF),
                pltpu.VMEM((width, width), BF),
                dma((8,)),
                dma((2, 2)),
                dma((2, 8)),
                dma((10,)),
            ],
        ),
        compiler_params=pltpu.CompilerParams(vmem_limit_bytes=VMEM_LIMIT),
        cost_estimate=cost(n * width * (10 * hidden + 2 * width), n * (width * 22 + 2 * hidden) + 8 * hidden * width),
        name="middle",
    )(table, norms, att, x, cot, *weights)


def attended_back_kernel(size, tb, sub, block, w_down, w_proj, tab, nrm_ref, x1_ref, dh_ref, cot_ref, att_ref, *rest):
    count = len(w_down.arrays) if size == 8 else 1
    w_refs = rest[:count]
    dx_ref, da_ref, gn_ref, *g_refs, acc, wp_sc, sems = rest[count:]
    t = pl.program_id(0)
    me = tab[tab.shape[0] - 1]
    per = ROW_LEN // tb
    valid = tab[lax.div(t, per) * STRIDE + 33] - lax.rem(t, per) * tb
    width = x1_ref.shape[1]

    @pl.when(t == 0)
    def _():
        if size == 8:
            copies = down_copies(w_down, w_refs, block, wp_sc, sems, me)
        else:
            copies = [pltpu.make_async_copy(w_refs[0], wp_sc, sems.at[0])]
        for c in copies:
            c.start()
        acc[...] = jnp.zeros_like(acc)
        gn_ref[...] = jnp.zeros_like(gn_ref)
        for c in copies:
            c.wait()

    dgain = jnp.zeros((1, width), F32)
    dshift = jnp.zeros((1, width), F32)
    dbs = []
    for i in range(0, tb, sub):
        p = pl.ds(i, sub)
        unit, rate = norm_stats(x1_ref[p, :])
        dh = dh_ref[p, :]
        ok = lax.broadcasted_iota(jnp.int32, (sub, 1), 0) + i < valid
        dx = jnp.where(ok, cot_ref[p, :].astype(F32), 0.0) + norm_back(unit, rate, nrm_ref[2:3, :], dh)
        dx_ref[p, :] = dx
        dbs.append(dx.astype(BF))
        da_ref[p, :] = mm(dbs[-1], wp_sc[...], NN).astype(BF)
        dgain += jnp.sum(dh * unit, axis=0, keepdims=True)
        dshift += jnp.sum(dh, axis=0, keepdims=True)
    acc[...] += mm(jnp.concatenate(dbs, axis=0), att_ref[...], TN)
    gn_ref[0:1, :] += dgain
    gn_ref[1:2, :] += dshift

    @pl.when(t == pl.num_programs(0) - 1)
    def _():
        if size == 8:
            by_owner(acc, w_down.per, *g_refs, me)
        else:
            g_refs[0][...] = acc[...].astype(BF)


def attended_back(table, norms, x1, dh, cot, att, w_down, w_proj, size, tb=256, sub=256):
    n, width = x1.shape
    weights = w_down.arrays if size == 8 else w_proj.arrays
    block = pl.BlockSpec((tb, width), lambda t, tab: (t, 0))
    fixed = pl.BlockSpec((8, width), lambda t, tab: (0, 0))
    sds = jax.ShapeDtypeStruct
    g_shapes = [(4, w_down.per, width)] * 2 if size == 8 else [(width, width)]
    return pl.pallas_call(
        partial(attended_back_kernel, size, tb, sub, 4, w_down, w_proj),
        out_shape=[sds((n, width), F32), sds((n, width), BF), sds((8, width), F32)] + [sds(g, BF) for g in g_shapes],
        grid_spec=pltpu.PrefetchScalarGridSpec(
            num_scalar_prefetch=1,
            grid=(n // tb,),
            in_specs=[fixed] + [block] * 4 + [pl.BlockSpec(memory_space=pl.ANY)] * len(weights),
            out_specs=[block, block, fixed] + [pl.BlockSpec(g, lambda t, tab, k=len(g): (0,) * k) for g in g_shapes],
            scratch_shapes=[
                pltpu.VMEM((width, width), F32),
                pltpu.VMEM((width, width), BF),
                pltpu.SemaphoreType.DMA((8,)),
            ],
        ),
        compiler_params=pltpu.CompilerParams(vmem_limit_bytes=VMEM_LIMIT),
        cost_estimate=cost(4 * n * width * width, n * width * 18),
        name="attended_back",
    )(table, norms, x1, dh, cot, att, *weights)


def finish_kernel(size, blocks, w_down, tab, x1_ref, act_ref, *rest):
    w_refs = rest[: len(w_down.arrays)]
    out_ref, w_sc, sems = rest[-3:]
    t = pl.program_id(0)
    me = tab[tab.shape[0] - 1]
    tb, width = x1_ref.shape

    def copies(b):
        if size == 8:
            return down_copies(w_down, w_refs, b, w_sc.at[:, pl.ds(b * width, width)], sems.at[b], me)
        at = pl.ds(b * width, width)
        return [pltpu.make_async_copy(w_refs[0].at[:, at], w_sc.at[:, at], sems.at[b, 0])]

    @pl.when(t == 0)
    def _():
        for b in range(blocks):
            for c in copies(b):
                c.start()
        for b in range(blocks):
            for c in copies(b):
                c.wait()

    x2 = x1_ref[...] + mm(act_ref[...], w_sc[...], NT)
    per = ROW_LEN // tb
    valid = tab[lax.div(t, per) * STRIDE + 33] - lax.rem(t, per) * tb
    ok = lax.broadcasted_iota(jnp.int32, (tb, 1), 0) < valid
    out_ref[...] = jnp.where(ok, x2, 0.0).astype(BF)


def finish(table, x1, act, w_down, size, tb=256):
    n, width = x1.shape
    hidden = act.shape[1]
    blocks = hidden // width
    count = len(w_down.arrays)
    block = lambda w: pl.BlockSpec((tb, w), lambda t, tab: (t, 0))
    return pl.pallas_call(
        partial(finish_kernel, size, blocks, w_down),
        out_shape=jax.ShapeDtypeStruct((n, width), BF),
        grid_spec=pltpu.PrefetchScalarGridSpec(
            num_scalar_prefetch=1,
            grid=(n // tb,),
            in_specs=[block(width), block(hidden)] + [pl.BlockSpec(memory_space=pl.ANY)] * count,
            out_specs=block(width),
            scratch_shapes=[pltpu.VMEM((width, hidden), BF), pltpu.SemaphoreType.DMA((blocks, 8))],
        ),
        compiler_params=pltpu.CompilerParams(vmem_limit_bytes=VMEM_LIMIT),
        cost_estimate=cost(2 * n * width * hidden, n * (width * 6 + hidden * 2) + 2 * width * hidden),
        name="finish",
    )(table, x1, act, *w_down.arrays)


def per_device(
    size,
    replicas,
    tokens,
    segment_ids,
    cotangent,
    norm_params,
    qkv_weight,
    proj_weight,
    up_weight,
    down_weight,
    target_norms,
    target_qkv,
    target_proj,
    target_up,
    target_down,
):
    count, width = tokens.shape
    rows = count // ROW_LEN
    hidden = down_weight.shape[0]
    own = width // size
    blocks = hidden // width
    fast = size == 8 and replicas == 4
    size = size if fast else 0
    me = lax.axis_index("fsdp")
    table = job_table(segment_ids, rows, me)
    with jax.named_scope("gather_weights"):
        placed = lax.dynamic_update_slice(jnp.zeros((16, width), BF), norm_params, (0, me * own))
        qkv_t, up_t, down_t, proj_t = qkv_weight.T, up_weight.T, down_weight.T, proj_weight.T
        if fast:
            half = qkv_t.shape[0] // 2
            first, second = gather_cross(jnp.concatenate([qkv_t[:half], placed], axis=0), qkv_t[half:])
            far = forward_cross(first, second)
            upper = both_cores([*first, far[0]])
            lower = both_cores([*second, far[1]])
            w_qkv = Weight([(a, s, 0) for a, s in upper] + [(a, s, half) for a, s in lower], 2 * half)
            norm_parts = []
            packed = jnp.concatenate([down_t[:, b * width : (b + 1) * width] for b in range(blocks)] + [proj_t], axis=0)
            up_1, down_1 = after((up_t, packed), first[1], second[2])
            up_x, down_y = hop(up_1, 2, 8), hop(down_1, 4, 8)
            up_2, down_2 = after((up_t, packed), *far)
            up_y, down_x = hop(up_2, 4, 8), hop(down_2, 2, 8)
        else:
            whole = lambda shard: lax.all_gather(shard, "fsdp", axis=0, tiled=True)
            w_qkv, w_up, w_down, w_proj = (Weight([(whole(w), None, 0)], 0) for w in (qkv_t, up_t, down_t, proj_t))
            norm_parts = [lax.psum(placed.astype(F32), "fsdp").astype(BF)]

    keep_rate = 1.0 - ema_rate
    blend = lambda target, weight: ema_rate * target + keep_rate * weight.astype(F32)
    targets = (
        blend(target_norms, norm_params),
        blend(target_qkv, qkv_weight),
        blend(target_proj, proj_weight),
        blend(target_up, up_weight),
        blend(target_down, down_weight),
    )
    stage, *targets = lax.optimization_barrier((table, *targets))
    h1, qkv, norms = project(stage, norm_parts, tokens, w_qkv)
    stage = table
    if fast:
        with jax.named_scope("gather_weights"):
            up_x, down_y, up_t, packed = after((up_x, down_y, up_t, packed), qkv)
            up_far, down_far = hop(up_x, 4, 8), hop(down_y, 2, 8)
            near = both_cores([up_t, up_x]), both_cores([packed])
            stage = after(table, up_x, down_y)
    attended = attention_forward(qkv, stage, rows)
    if fast:
        with jax.named_scope("gather_weights"):
            up_y, down_x, down_y, up_far, down_far = after((up_y, down_x, down_y, up_far, down_far), attended)
            along = hop(up_y, 1, 8), hop(down_x, 1, 8), hop(down_y, 1, 8)
            ups = near[0] + [(up_y, 4), (along[0], 5), (up_far, 6), (hop(up_far, 1, 8), 7)]
            downs = near[1] + [(down_x, 2), (along[1], 3), (down_y, 4), (along[2], 5)]
            downs += [(down_far, 6), (hop(down_far, 1, 8), 7)]
            w_up = Weight([(a, s, 0) for a, s in ups], up_t.shape[0])
            w_down = Weight([(a, s, 0) for a, s in downs], own)
            w_proj = Weight([], own)
    x1, act, grad_second, *grads = middle(
        table, norms, attended, tokens, cotangent, w_up, w_down, w_proj, hidden, size
    )
    grad_middle, grad_attended, grad_norm2, *grad_proj = attended_back(
        table, norms, x1, grad_second, cotangent, attended, w_down, w_proj, size
    )

    after_table = lambda *values: after(table, *values)
    if fast:
        packed_own = lax.psum_scatter(grads[0], "fsdp", scatter_dimension=0, tiled=True)
    dqkv = attention_backward(qkv, grad_attended, table, rows)
    if fast:
        grad_qkv = project_grad(table, *dqkv, h1, grad_proj, size)
        qkv_sum = Scatter(*grad_qkv)
        fw = hidden // 8
        packed_own = after(packed_own, grad_qkv[0])
        packed_sum = lax.psum(packed_own, "rep")
        stage = after_table(packed_own, *qkv_sum.send())
        block_output = finish(stage, x1, act, w_down, size)
        qkv_own = qkv_sum.block(block_output)
        input_grad, grad_norm1 = project_back(after_table(qkv_own), norms, *dqkv, tokens, grad_middle, w_qkv)
        norm_sum = jnp.concatenate([grad_norm1[:2], grad_norm2[:2], jnp.zeros((4, width), F32)], axis=0)
        quarter = quarter_sum(qkv_own, grad_norm1)
        quarter = after(quarter, packed_sum)
        for bit in (1, 2, 4):
            norm_sum = norm_sum + hop(norm_sum, bit, 8)
        for bit in (1, 2):
            norm_sum = norm_sum + lax.ppermute(norm_sum, "rep", [(i, i ^ bit) for i in range(4)])
        qkv_own = all_quarters(quarter)
        packed_sum = packed_sum.astype(F32)
        up = jnp.concatenate([packed_sum[:fw, :fw], packed_sum[:fw, fw:]], axis=0)
        down = packed_sum[fw:].reshape(blocks, own, width).transpose(1, 0, 2).reshape(own, hidden)
        qkv_own, proj = qkv_own[: 3 * own], qkv_own[3 * own :]
    else:
        grad_qkv = project_grad(table, *dqkv, h1, [], size)
        input_grad, grad_norm1 = project_back(table, norms, *dqkv, tokens, grad_middle, w_qkv)
        block_output = finish(table, x1, act, w_down, size)
        sums = lambda g, dim: lax.psum(lax.psum_scatter(g, "fsdp", scatter_dimension=dim, tiled=True), "rep").astype(F32)
        up, down, proj, qkv_own = sums(grads[0], 1), sums(grads[1], 0), sums(grad_proj[0], 0), sums(grad_qkv[0], 0)
        norm_sum = jnp.concatenate([grad_norm1[:2], grad_norm2[:2]], axis=0)
        norm_sum = lax.psum(norm_sum, ("fsdp", "rep"))
    norm_grad = lax.dynamic_slice(norm_sum, (0, me * own), (4, own))
    return (block_output, input_grad, norm_grad, qkv_own.T, proj.T, up, down.T, *targets)


def solution(mesh):
    tokens = P(("fsdp", "rep"), None)
    columns = P(None, "fsdp")
    return jax.shard_map(
        partial(per_device, mesh.shape["fsdp"], mesh.shape["rep"]),
        mesh=mesh,
        in_specs=(tokens, P(("fsdp", "rep")), tokens) + (columns,) * 10,
        out_specs=(tokens, tokens) + (columns,) * 10,
        check_vma=False,
    )
```

```python
import math
from functools import partial

import jax
import jax.numpy as jnp
from jax import lax
from jax.experimental import pallas as pl
from jax.experimental.pallas import tpu as pltpu
from jax.sharding import PartitionSpec as P

HEAD = 64
ROW_LEN = 1024
layer_eps = 1e-06
ema_rate = 0.75

BF = jnp.bfloat16
F32 = jnp.float32
NN = (((1,), (0,)), ((), ()))
NT = (((1,), (1,)), ((), ()))
TN = (((0,), (0,)), ((), ()))
VMEM_LIMIT = 66_000_000
GRANT = 32_000_000
COST_SCALE = 0.02

QW = 256
KW = 224
FIT = KW - 15
SMALL = 128
FIT_SMALL = SMALL - 15
KB = 128
STRIDE = 35


def mm(left, right, dims):
    return lax.dot_general(left, right, dims, preferred_element_type=F32)


def cost(flops, moved):
    return pl.CostEstimate(flops=int(flops * COST_SCALE), bytes_accessed=int(moved * COST_SCALE), transcendentals=0)


def job_table(segment_ids, rows, device):
    seg = segment_ids.reshape(rows, 1, ROW_LEN)
    ident = jnp.arange(16, dtype=jnp.int32)[None, :, None]
    real = seg >= 0
    starts = jnp.sum((real & (seg < ident)).astype(jnp.int32), axis=2)
    after = jnp.sum((real & (seg < ident + 1)).astype(jnp.int32), axis=2)
    images = jnp.max(seg, axis=2) + 1
    ends = jnp.where(jnp.arange(16, dtype=jnp.int32)[None, :] < images, after, ROW_LEN)
    valid = jnp.sum(real.astype(jnp.int32), axis=2)
    pad = ROW_LEN - valid
    fits = pad <= FIT
    jobs = images + jnp.where((pad > 0) & fits, 1, 0)
    wide = jnp.where(fits, 0, (pad + 15 + QW - 1) // QW)
    table = jnp.concatenate([starts, ends, jobs, valid, wide], axis=1).reshape(-1)
    return jnp.concatenate([table, device.astype(jnp.int32).reshape(1)])


def lane_of(count):
    return lax.broadcasted_iota(jnp.int32, (count, 128), 1)


def slot_of(count, base):
    return lax.broadcasted_iota(jnp.int32, (count, 128), 0) + base


def half_lanes(count, par):
    return (lane_of(count) < 64) if par == 0 else (lane_of(count) >= 64)


def spare_lane(count, par):
    return lane_of(count) == (64 if par == 0 else 0)


def query_side(q, par):
    n = q.shape[0]
    return jnp.where(half_lanes(n, par), q * BF(0.125), jnp.where(spare_lane(n, par), BF(1), BF(0)))


def key_side(k, par, inside):
    n = k.shape[0]
    return jnp.where(half_lanes(n, par), k, jnp.where(spare_lane(n, par) & (~inside), BF(-1e30), BF(0)))


def one_head(x, par):
    return jnp.where(half_lanes(x.shape[0], par), x, BF(0))


def each_image(tab, base, work):
    def job(j, carry):
        begin = tab[base + j]
        end = tab[base + 16 + j]
        low = lax.div(begin, 16) * 16
        small = end - begin <= FIT_SMALL
        for fits, nq, nk in ((small, SMALL, SMALL), (~small, QW, KW)):

            @pl.when(fits)
            def _():
                q0 = pl.multiple_of(jnp.minimum(low, ROW_LEN - nq), 16)
                k0 = pl.multiple_of(jnp.minimum(low, ROW_LEN - nk), 16)
                kr = slot_of(nk, k0)
                qr = slot_of(nq, q0)
                work(pl.ds(q0, nq), pl.ds(k0, nk), (qr >= begin) & (qr < end), (kr >= begin) & (kr < end))

        return carry

    lax.fori_loop(0, tab[base + 32], job, 0)


def attend_kernel(pairs, tab, q_ref, k_ref, v_ref, o_ref, a_sc):
    base = pl.program_id(0) * STRIDE
    o_ref[...] = jnp.zeros_like(o_ref)

    def work(qs, ks, qin, inside):
        scores = []
        for p in range(pairs):
            cs = pl.ds(128 * p, 128)
            q = q_ref[qs, cs]
            k = k_ref[ks, cs]
            for par in range(2):
                scores.append(mm(key_side(k, par, inside), query_side(q, par), NT))
        probs = []
        for st in scores:
            expo = jnp.exp(st - jnp.max(st, axis=0, keepdims=True))
            total = jnp.sum(expo, axis=0, keepdims=True)
            probs.append((expo * (1.0 / total)).astype(BF))
        for p in range(pairs):
            cs = pl.ds(128 * p, 128)
            v = v_ref[ks, cs]
            o = jnp.concatenate(
                [mm(v[:, 64 * par : 64 * par + 64], probs[2 * p + par], TN) for par in range(2)], axis=0
            ).T
            o_ref[qs, cs] = jnp.where(qin, o.astype(BF), o_ref[qs, cs])

    each_image(tab, base, work)

    start = tab[base + 33]
    low = lax.div(start, 16) * 16

    def wide(i, carry):
        q0 = pl.multiple_of(jnp.minimum(low + i * QW, ROW_LEN - QW), 16)
        qin = slot_of(QW, q0) >= start

        def pair(p, none):
            cs = pl.ds(pl.multiple_of(128 * p, 128), 128)
            q = q_ref[pl.ds(q0, QW), cs]
            for par in range(2):
                qs = query_side(q, par)

                def block(kb):
                    k0 = pl.multiple_of(kb * KB, KB)
                    k = k_ref[pl.ds(k0, KB), cs]
                    return k0, mm(key_side(k, par, slot_of(KB, k0) >= start), qs, NT)

                def take_max(kb, top):
                    return jnp.maximum(top, jnp.max(block(kb)[1], axis=0, keepdims=True))

                top = lax.fori_loop(0, ROW_LEN // KB, take_max, jnp.full((1, QW), -1e30, F32))

                def take_sum(kb, total):
                    return total + jnp.sum(jnp.exp(block(kb)[1] - top), axis=0, keepdims=True)

                total = lax.fori_loop(0, ROW_LEN // KB, take_sum, jnp.zeros((1, QW), F32))
                a_sc[...] = jnp.zeros_like(a_sc)

                def take_out(kb, c):
                    k0, st = block(kb)
                    prob = (jnp.exp(st - top) * (1.0 / total)).astype(BF)
                    a_sc[...] += mm(one_head(v_ref[pl.ds(k0, KB), cs], par), prob, TN)
                    return c

                lax.fori_loop(0, ROW_LEN // KB, take_out, 0)
                hit = qin & half_lanes(QW, par)
                o_ref[pl.ds(q0, QW), cs] = jnp.where(hit, a_sc[...].T.astype(BF), o_ref[pl.ds(q0, QW), cs])
            return none

        lax.fori_loop(0, pairs, pair, 0)
        return carry

    lax.fori_loop(0, tab[base + 34], wide, 0)


def attend_back_kernel(pairs, tab, q_ref, k_ref, v_ref, d_ref, *rest):
    dq_ref, dk_ref, dv_ref, a_sc, dk_sc, dv_sc = rest[-6:]
    base = pl.program_id(0) * STRIDE
    dq_ref[...] = jnp.zeros_like(dq_ref)
    dk_ref[...] = jnp.zeros_like(dk_ref)
    dv_ref[...] = jnp.zeros_like(dv_ref)

    def work(qs, ks, qin, inside):
        scores = []
        grads = []
        for p in range(pairs):
            cs = pl.ds(128 * p, 128)
            q = q_ref[qs, cs]
            k = k_ref[ks, cs]
            v = v_ref[ks, cs]
            d = jnp.where(qin, d_ref[qs, cs], BF(0))
            for par in range(2):
                scores.append(mm(key_side(k, par, inside), query_side(q, par), NT))
                grads.append(mm(v, one_head(d, par), NT))
        probs = []
        dscores = []
        for st, dp in zip(scores, grads):
            expo = jnp.exp(st - jnp.max(st, axis=0, keepdims=True))
            total = jnp.sum(expo, axis=0, keepdims=True)
            prob = expo * (1.0 / total)
            center = jnp.sum(prob * dp, axis=0, keepdims=True)
            dscores.append((prob * (dp - center)).astype(BF))
            probs.append(prob.astype(BF))
        for p in range(pairs):
            cs = pl.ds(128 * p, 128)
            q = q_ref[qs, cs]
            k = k_ref[ks, cs]
            d = jnp.where(qin, d_ref[qs, cs], BF(0))
            dv = mm(probs[2 * p], one_head(d, 0), NN) + mm(probs[2 * p + 1], one_head(d, 1), NN)
            dk = mm(dscores[2 * p], one_head(q, 0), NN) + mm(dscores[2 * p + 1], one_head(q, 1), NN)
            dq = jnp.concatenate(
                [mm(k[:, 64 * par : 64 * par + 64], dscores[2 * p + par], TN) for par in range(2)], axis=0
            ).T
            dq_ref[qs, cs] = jnp.where(qin, (dq * 0.125).astype(BF), dq_ref[qs, cs])
            dk_ref[ks, cs] = jnp.where(inside, (dk * 0.125).astype(BF), dk_ref[ks, cs])
            dv_ref[ks, cs] = jnp.where(inside, dv.astype(BF), dv_ref[ks, cs])

    each_image(tab, base, work)

    start = tab[base + 33]
    low = lax.div(start, 16) * 16
    windows = tab[base + 34]

    def pair(p, none):
        cs = pl.ds(pl.multiple_of(128 * p, 128), 128)

        @pl.when(windows > 0)
        def _():
            dk_sc[...] = jnp.zeros_like(dk_sc)
            dv_sc[...] = jnp.zeros_like(dv_sc)

        def wide(i, carry):
            first = jnp.maximum(start, low + i * QW)
            q0 = pl.multiple_of(jnp.minimum(low + i * QW, ROW_LEN - QW), 16)
            qin = slot_of(QW, q0) >= first
            q = q_ref[pl.ds(q0, QW), cs]
            d = jnp.where(qin, d_ref[pl.ds(q0, QW), cs], BF(0))
            for par in range(2):
                qh = query_side(q, par)
                dh = one_head(d, par)
                qo = one_head(q, par)

                def block(kb):
                    k0 = pl.multiple_of(kb * KB, KB)
                    k = k_ref[pl.ds(k0, KB), cs]
                    v = v_ref[pl.ds(k0, KB), cs]
                    return k0, k, mm(key_side(k, par, slot_of(KB, k0) >= start), qh, NT), mm(v, dh, NT)

                def take_max(kb, top):
                    return jnp.maximum(top, jnp.max(block(kb)[2], axis=0, keepdims=True))

                top = lax.fori_loop(0, ROW_LEN // KB, take_max, jnp.full((1, QW), -1e30, F32))

                def take_sums(kb, sums):
                    _, _, st, dp = block(kb)
                    expo = jnp.exp(st - top)
                    return (
                        sums[0] + jnp.sum(expo, axis=0, keepdims=True),
                        sums[1] + jnp.sum(expo * dp, axis=0, keepdims=True),
                    )

                none = jnp.zeros((1, QW), F32)
                total, weighted = lax.fori_loop(0, ROW_LEN // KB, take_sums, (none, none))
                scale = 1.0 / total
                center = weighted * scale
                a_sc[...] = jnp.zeros_like(a_sc)

                def take_grads(kb, c):
                    k0, k, st, dp = block(kb)
                    prob = jnp.exp(st - top) * scale
                    ds = (prob * (dp - center)).astype(BF)
                    a_sc[...] += mm(one_head(k, par), ds, TN)
                    dk_sc[pl.ds(k0, KB), :] += mm(ds, qo, NN)
                    dv_sc[pl.ds(k0, KB), :] += mm(prob.astype(BF), dh, NN)
                    return c

                lax.fori_loop(0, ROW_LEN // KB, take_grads, 0)
                hit = qin & half_lanes(QW, par)
                dq = (a_sc[...].T * 0.125).astype(BF)
                dq_ref[pl.ds(q0, QW), cs] = jnp.where(hit, dq, dq_ref[pl.ds(q0, QW), cs])
            return carry

        lax.fori_loop(0, windows, wide, 0)

        @pl.when(windows > 0)
        def _():
            kin = slot_of(ROW_LEN, 0) >= start
            dk_ref[:, cs] = jnp.where(kin, (dk_sc[...] * 0.125).astype(BF), dk_ref[:, cs])
            dv_ref[:, cs] = jnp.where(kin, dv_sc[...].astype(BF), dv_ref[:, cs])

        return none

    lax.fori_loop(0, jnp.where(windows > 0, pairs, 0), pair, 0)


def attention_call(kernel, name, outs, scratch, qkv, extra, table, rows, flops, moved):
    n = qkv.shape[0]
    width = qkv.shape[1] // 3
    spec = lambda part: pl.BlockSpec((ROW_LEN, width), lambda r, t: (r, part))
    return pl.pallas_call(
        partial(kernel, width // 128),
        out_shape=[jax.ShapeDtypeStruct((n, width), BF)] * outs,
        grid_spec=pltpu.PrefetchScalarGridSpec(
            num_scalar_prefetch=1,
            grid=(rows,),
            in_specs=[spec(0), spec(1), spec(2)] + [spec(0)] * len(extra),
            out_specs=[spec(0)] * outs,
            scratch_shapes=scratch,
        ),
        compiler_params=pltpu.CompilerParams(vmem_limit_bytes=VMEM_LIMIT),
        cost_estimate=cost(rows * flops, rows * moved * ROW_LEN * width),
        name=name,
    )(table, qkv, qkv, qkv, *extra)


def attention_forward(qkv, table, rows):
    scratch = [pltpu.VMEM((128, QW), F32)]
    return attention_call(attend_kernel, "attend", 1, scratch, qkv, [], table, rows, 12e9, 8)[0]


def attention_backward(qkv, da, table, rows):
    scratch = [pltpu.VMEM((128, QW), F32), pltpu.VMEM((ROW_LEN, 128), F32), pltpu.VMEM((ROW_LEN, 128), F32)]
    return attention_call(attend_back_kernel, "attend_back", 3, scratch, qkv, [da], table, rows, 24e9, 14)


def hop(value, bit, size):
    return lax.ppermute(value, "fsdp", [(i, i ^ bit) for i in range(size)])


def gather_cross(first, second):
    first_x, second_y = hop(first, 2, 8), hop(second, 4, 8)
    first_late, second_late = after((first, second), hop(second[:16], 1, 8))
    first_y, second_x = hop(first_late, 4, 8), hop(second_late, 2, 8)
    return (first, first_x, first_y), (second, second_x, second_y)


def forward_cross(firsts, seconds):
    return hop(firsts[1], 4, 8), hop(seconds[2], 2, 8)


def both_cores(arrays):
    own = [(array, 2 * i) for i, array in enumerate(arrays)]
    return own + [(hop(array, 1, 8), slot + 1) for array, slot in own]


def after(value, *others):
    return lax.optimization_barrier((value, *others))[0]


def total(*terms):
    return sum(t.astype(F32) for t in terms).astype(BF)


class Scatter:
    def __init__(self, even, odd):
        self.even = even
        self.core = hop(odd, 1, 8)

    def send(self):
        self.out = [total(self.even[q], self.core[q]) for q in (1, 2, 3)]
        return self.out

    def block(self, done):
        come = after([hop(block, 2 * q, 8) for q, block in zip((1, 2, 3), self.out)], done)
        return total(self.even[0], self.core[0], *come)


def shift(value, by):
    return lax.ppermute(value, "rep", [(i, (i + by) % 4) for i in range(4)])


def quarter_sum(block, done):
    z = lax.axis_index("rep")
    quarters = block.reshape(4, block.shape[0] // 4, block.shape[1])
    pick = lambda by: lax.dynamic_index_in_dim(quarters, lax.rem(z + by, 4), 0, False)
    return total(pick(0), *after([shift(pick(by), by) for by in (2, 1, 3)], done))


def all_quarters(mine):
    z = lax.axis_index("rep")
    parts = [mine] + [shift(mine, by) for by in (1, 2, 3)]
    out = jnp.zeros((4, *mine.shape), F32)
    for by, part in enumerate(parts):
        out = lax.dynamic_update_index_in_dim(out, part.astype(F32), lax.rem(z - by + 4, 4), 0)
    return out.reshape(4 * mine.shape[0], mine.shape[1])


class Weight:
    def __init__(self, pieces, per):
        self.arrays = [p[0] for p in pieces]
        self.places = [p[1:] for p in pieces]
        self.per = per

    def copies(self, refs, dst, sems, me):
        out = []
        for i, (ref, (slot, row)) in enumerate(zip(refs, self.places)):
            src, into = ref, dst
            if slot is not None:
                half = self.per // 2
                src = ref.at[pl.ds(0, half), :]
                into = dst.at[pl.ds(pl.multiple_of((me ^ slot) * self.per + row, half), half), :]
            out.append(pltpu.make_async_copy(src, into, sems.at[i]))
        return out


def norm_stats(values):
    center = values - jnp.mean(values, axis=1, keepdims=True)
    rate = lax.rsqrt(jnp.mean(center * center, axis=1, keepdims=True) + layer_eps)
    return center * rate, rate


def norm_back(unit, rate, gain, grad):
    scaled = grad * gain
    mean = jnp.mean(scaled, axis=1, keepdims=True)
    along = jnp.mean(scaled * unit, axis=1, keepdims=True)
    return rate * (scaled - mean - unit * along)


def project_kernel(weight, count, tab, x_ref, *rest):
    w_refs = rest[:count]
    h_ref, qkv_ref, nrm_ref, w_sc, n_sc, sems, n_sems = rest[-7:]
    me = tab[tab.shape[0] - 1]
    half = weight.per // 2

    @pl.when(pl.program_id(0) == 0)
    def _():
        if len(rest) - 7 > count:
            norm_copies = [pltpu.make_async_copy(rest[count], n_sc.at[0], n_sems.at[0])]
        else:
            norm_copies = [
                pltpu.make_async_copy(w_refs[i].at[pl.ds(half, 16), :], n_sc.at[i], n_sems.at[i]) for i in range(8)
            ]
        copies = weight.copies(w_refs, w_sc, sems, me)
        for c in norm_copies + copies:
            c.start()
        for c in norm_copies:
            c.wait()
        placed = sum(n_sc[i].astype(F32) for i in range(len(norm_copies)))
        nrm_ref[...] = placed[:8, :]

    tb, width = x_ref.shape
    parts = [pl.ds(i, tb // 2) for i in range(0, tb, tb // 2)]
    for p in parts:
        unit, _ = norm_stats(x_ref[p, :].astype(F32))
        h_ref[p, :] = (unit * nrm_ref[0:1, :] + nrm_ref[1:2, :]).astype(BF)

    @pl.when(pl.program_id(0) == 0)
    def _():
        for c in weight.copies(w_refs, w_sc, sems, me):
            c.wait()

    for p in parts:
        qkv_ref[p, :] = mm(h_ref[p, :], w_sc[...], NT).astype(BF)


def project(table, norm_parts, x, weight, tb=512):
    n, width = x.shape
    count = len(weight.arrays)
    anywhere = pl.BlockSpec(memory_space=pl.ANY)
    block = lambda w: pl.BlockSpec((tb, w), lambda t, tab: (t, 0))
    sds = jax.ShapeDtypeStruct
    return pl.pallas_call(
        partial(project_kernel, weight, count),
        out_shape=[sds((n, width), BF), sds((n, 3 * width), BF), sds((8, width), F32)],
        grid_spec=pltpu.PrefetchScalarGridSpec(
            num_scalar_prefetch=1,
            grid=(n // tb,),
            in_specs=[block(width)] + [anywhere] * (count + len(norm_parts)),
            out_specs=[block(width), block(3 * width), pl.BlockSpec((8, width), lambda t, tab: (0, 0))],
            scratch_shapes=[
                pltpu.VMEM((3 * width, width), BF),
                pltpu.VMEM((8, 16, width), BF),
                pltpu.SemaphoreType.DMA((count,)),
                pltpu.SemaphoreType.DMA((8,)),
            ],
        ),
        compiler_params=pltpu.CompilerParams(vmem_limit_bytes=VMEM_LIMIT),
        cost_estimate=cost(6 * n * width * width, n * width * 10 + 6 * width * width),
        name="project",
    )(table, x, *weight.arrays, *norm_parts)


def by_owner(acc, per, even_ref, odd_ref, me):
    for q in range(4):
        for parity, ref in ((0, even_ref), (1, odd_ref)):
            at = pl.multiple_of((me ^ (2 * q + parity)) * per, per)
            ref[q] = acc[pl.ds(at, per), :].astype(BF)


def project_grad_kernel(size, tab, dq_ref, dk_ref, dv_ref, h_ref, *rest):
    acc = rest[-1]
    t = pl.program_id(0)
    width = h_ref.shape[1]

    @pl.when(t == 0)
    def _():
        acc[...] = jnp.zeros_like(acc)

    for part, ref in enumerate((dq_ref, dk_ref, dv_ref)):
        acc[pl.ds(part * width, width), :] += mm(ref[...], h_ref[...], TN)

    @pl.when(t == pl.num_programs(0) - 1)
    def _():
        if size == 8:
            per = acc.shape[0] // 8
            by_owner(acc, per, *(ref.at[:, pl.ds(0, per), :] for ref in rest[2:4]), tab[tab.shape[0] - 1])
            for src, dst in zip(rest[0:2], rest[2:4]):
                dst[:, pl.ds(per, src.shape[1]), :] = src[...]
        else:
            rest[0][...] = acc[...].astype(BF)


def project_grad(table, dq, dk, dv, h, proj, size, tb=512):
    n, width = h.shape
    rows = 3 * width
    block = pl.BlockSpec((tb, width), lambda t, tab: (t, 0))
    whole = lambda s: pl.BlockSpec(s, lambda t, tab, k=len(s): (0,) * k)
    shapes = [(4, rows // 8 + proj[0].shape[1], width)] * 2 if size == 8 else [(rows, width)]
    return pl.pallas_call(
        partial(project_grad_kernel, size),
        out_shape=[jax.ShapeDtypeStruct(s, BF) for s in shapes],
        grid_spec=pltpu.PrefetchScalarGridSpec(
            num_scalar_prefetch=1,
            grid=(n // tb,),
            in_specs=[block] * 4 + [whole(p.shape) for p in proj],
            out_specs=[whole(s) for s in shapes],
            scratch_shapes=[pltpu.VMEM((rows, width), F32)],
        ),
        compiler_params=pltpu.CompilerParams(vmem_limit_bytes=VMEM_LIMIT),
        cost_estimate=cost(6 * n * width * width, n * width * 8 + 6 * width * width),
        name="project_grad",
    )(table, dq, dk, dv, h, *proj)


def project_back_kernel(weight, count, tab, nrm_ref, dq_ref, dk_ref, dv_ref, x_ref, dx_ref, *rest):
    w_refs = rest[:count]
    out_ref, gn_ref, w_sc, sems = rest[-4:]
    t = pl.program_id(0)
    me = tab[tab.shape[0] - 1]
    width = x_ref.shape[1]

    @pl.when(t == 0)
    def _():
        copies = weight.copies(w_refs, w_sc, sems, me)
        for c in copies:
            c.start()
        gn_ref[...] = jnp.zeros_like(gn_ref)
        for c in copies:
            c.wait()

    tb = x_ref.shape[0]
    parts = [pl.ds(i, tb // 2) for i in range(0, tb, tb // 2)]
    units = [norm_stats(x_ref[p, :].astype(F32)) for p in parts]
    dgain = jnp.zeros((1, width), F32)
    dshift = jnp.zeros((1, width), F32)
    for p, (unit, rate) in zip(parts, units):
        grad = mm(dq_ref[p, :], w_sc[pl.ds(0, width), :], NN)
        grad += mm(dk_ref[p, :], w_sc[pl.ds(width, width), :], NN)
        grad += mm(dv_ref[p, :], w_sc[pl.ds(2 * width, width), :], NN)
        out_ref[p, :] = (dx_ref[p, :] + norm_back(unit, rate, nrm_ref[0:1, :], grad)).astype(BF)
        dgain += jnp.sum(grad * unit, axis=0, keepdims=True)
        dshift += jnp.sum(grad, axis=0, keepdims=True)
    gn_ref[0:1, :] += dgain
    gn_ref[1:2, :] += dshift


def project_back(table, norms, dq, dk, dv, x, dx, weight, tb=256):
    n, width = x.shape
    count = len(weight.arrays)
    anywhere = pl.BlockSpec(memory_space=pl.ANY)
    block = pl.BlockSpec((tb, width), lambda t, tab: (t, 0))
    fixed = pl.BlockSpec((8, width), lambda t, tab: (0, 0))
    return pl.pallas_call(
        partial(project_back_kernel, weight, count),
        out_shape=[jax.ShapeDtypeStruct((n, width), BF), jax.ShapeDtypeStruct((8, width), F32)],
        grid_spec=pltpu.PrefetchScalarGridSpec(
            num_scalar_prefetch=1,
            grid=(n // tb,),
            in_specs=[fixed] + [block] * 5 + [anywhere] * count,
            out_specs=[block, fixed],
            scratch_shapes=[pltpu.VMEM((3 * width, width), BF), pltpu.SemaphoreType.DMA((count,))],
        ),
        compiler_params=pltpu.CompilerParams(vmem_limit_bytes=VMEM_LIMIT),
        cost_estimate=cost(6 * n * width * width, n * width * 14 + 6 * width * width),
        name="project_back",
    )(table, norms, dq, dk, dv, x, dx, *weight.arrays)


def gelu_both(values):
    phi = 0.5 + 0.5 * lax.erf(values * math.sqrt(0.5))
    bell = jnp.exp(values * values * -0.5) * (1.0 / math.sqrt(2.0 * math.pi))
    return values * phi, phi + values * bell


def down_copies(weight, refs, block, dst, sems, me):
    out = []
    for i, (ref, (slot, _)) in enumerate(zip(refs, weight.places)):
        src = ref.at[pl.ds(pl.multiple_of(block * weight.per, weight.per), weight.per), :]
        at = pl.multiple_of((me ^ slot) * weight.per, weight.per)
        out.append(pltpu.make_async_copy(src, dst.at[pl.ds(at, weight.per), :], sems.at[i]))
    return out


def middle_kernel(size, tb, sub, chunks, w_up, w_down, w_proj, tab, nrm_ref, att_ref, x_ref, cot_ref, *rest):
    ups, downs = len(w_up.arrays), len(w_down.arrays)
    up_refs, down_refs = rest[:ups], rest[ups : ups + downs]
    proj_refs = down_refs if size == 8 else rest[ups + downs : ups + downs + 1]
    outs = 1 if size == 8 else 2
    rest = rest[-(19 + outs) :]
    x1_ref, act_ref, dh_ref = rest[:3]
    g_refs = rest[3 : 3 + outs]
    h_sc, ht_sc, dy_sc, dyt_sc, dh_sc, gu_sc, gd_sc, wp_sc, wu_sc, wd_sc, su_sc, sd_sc, p_sem, u_sem, d_sem, g_sem = rest[3 + outs :]
    j = pl.program_id(0)
    t = pl.program_id(1)
    steps = pl.num_programs(1)
    me = tab[tab.shape[0] - 1]
    per = ROW_LEN // tb
    valid = tab[lax.div(t, per) * STRIDE + 33]
    ok = (lax.broadcasted_iota(jnp.int32, (tb, 1), 0) + lax.rem(t, per) * tb) < valid
    ts = pl.ds(pl.multiple_of(t * tb, tb), tb)
    width = x_ref.shape[1]
    gain = nrm_ref[2:3, :]
    shift = nrm_ref[3:4, :]
    parts = [pl.ds(pl.multiple_of(t * tb + i, sub), sub) for i in range(0, tb, sub)]
    pieces = [pl.ds(i, sub) for i in range(0, tb, sub)]

    def chunk_copies(m):
        b = m % 2
        if size != 8:
            piece = pl.ds(m * width, width)
            up = [pltpu.make_async_copy(up_refs[0].at[piece, :], wu_sc.at[b], u_sem.at[b, 0])]
            down = [pltpu.make_async_copy(down_refs[0].at[:, piece], wd_sc.at[b], d_sem.at[b, 0])]
            return up + down
        up = []
        for i, (ref, (slot, _)) in enumerate(zip(up_refs, w_up.places)):
            if slot // 2 == m:
                at = pl.multiple_of(((me & 1) ^ (slot & 1)) * w_up.per, w_up.per)
                into = wu_sc.at[b].at[pl.ds(at, w_up.per), :]
                up.append(pltpu.make_async_copy(ref, into, u_sem.at[b, len(up)]))
        return up + down_copies(w_down, down_refs, (me >> 1) ^ m, wd_sc.at[b], d_sem.at[b], me)

    def proj_copies():
        if size != 8:
            return [pltpu.make_async_copy(proj_refs[0], wp_sc, p_sem.at[0])]
        return down_copies(w_down, proj_refs, chunks, wp_sc, p_sem, me)

    def packed_copies(pair):
        fw, dw = w_up.per, w_down.per
        whole = fw + chunks * dw
        out = []
        for d in range(8):
            at = pl.multiple_of(d * whole + fw + pair * dw, dw)
            out.append(pltpu.make_async_copy(sd_sc.at[pl.ds(d * dw, dw), :], g_refs[0].at[pl.ds(at, dw), :], g_sem.at[d]))
        for k in range(2):
            at = pl.multiple_of((2 * pair + k) * whole, dw)
            out.append(pltpu.make_async_copy(su_sc.at[k], g_refs[0].at[pl.ds(at, fw), :], g_sem.at[8 + k]))
        return out

    @pl.when((j == 0) & (t == 0))
    def _():
        for c in proj_copies() + chunk_copies(0):
            c.start()
        for c in proj_copies():
            c.wait()

    for m in range(chunks):

        @pl.when((j == m) & (t == 0))
        def _():
            for c in chunk_copies(m):
                c.wait()
            if m + 1 < chunks:
                for c in chunk_copies(m + 1):
                    c.start()

    @pl.when(j == 0)
    def _():
        dy = jnp.where(ok, cot_ref[...], BF(0))
        dy_sc[ts, :] = dy
        x1s = [x_ref[p, :].astype(F32) + mm(att_ref[p, :], wp_sc[...], NT) for p in pieces]
        dyt_sc[:, ts] = dy.T
        for p, full, x1 in zip(pieces, parts, x1s):
            x1_ref[p, :] = x1
            unit, _ = norm_stats(x1)
            h = (unit * gain + shift).astype(BF)
            h_sc[full, :] = h
            ht_sc[:, full] = h.T
        dh_sc[ts, :] = jnp.zeros((tb, width), F32)

    @pl.when(t == 0)
    def _():
        gu_sc[...] = jnp.zeros_like(gu_sc)
        gd_sc[...] = jnp.zeros_like(gd_sc)

    wu = wu_sc[lax.rem(j, 2)]
    wd = wd_sc[lax.rem(j, 2)]
    uppers = [mm(h_sc[p, :], wu, NT) for p in parts]
    acts = []
    dups = []
    for p, upper in zip(parts, uppers):
        dact = mm(dy_sc[p, :], wd, NN)
        act, slope = gelu_both(upper)
        acts.append(act.astype(BF))
        dups.append((dact * slope).astype(BF))
    for p, dup in zip(parts, dups):
        dh_sc[p, :] += mm(dup, wu, NN)
    act = jnp.concatenate(acts, axis=0)
    act_ref[...] = act
    gd_sc[...] += mm(dyt_sc[:, ts], act, NN)
    gu_sc[...] += mm(ht_sc[:, ts], jnp.concatenate(dups, axis=0), NN)

    @pl.when(j == chunks - 1)
    def _():
        dh_ref[...] = dh_sc[ts, :]

    @pl.when(t == steps - 1)
    def _():
        if size == 8:
            pair = (me >> 1) ^ j

            @pl.when(j > 0)
            def _():
                for c in packed_copies((me >> 1) ^ (j - 1)):
                    c.wait()

            fw = w_up.per
            for k in range(2):
                for i in range(2):
                    su_sc[k, :, i * fw : (i + 1) * fw] = gu_sc[i * fw : (i + 1) * fw, k * fw : (k + 1) * fw].astype(BF)
            sd_sc[...] = gd_sc[...].astype(BF)
            for c in packed_copies(pair):
                c.start()

            @pl.when(j == chunks - 1)
            def _():
                for c in packed_copies(pair):
                    c.wait()
        else:
            g_refs[0][...] = gu_sc[...].astype(BF)
            g_refs[1][...] = gd_sc[...].astype(BF)


def middle(table, norms, att, x, cot, w_up, w_down, w_proj, hidden, size, tb=512, sub=512):
    n, width = x.shape
    chunks = hidden // width
    steps = n // tb
    dev = table.shape[0] - 1
    first = lambda j, t, tab: (jnp.where(j == 0, t, steps - 1), 0)
    final = lambda j, t, tab: (jnp.where(j == chunks - 1, t, 0), 0)
    fixed = lambda j, t, tab: (0, 0)
    anywhere = pl.BlockSpec(memory_space=pl.ANY)
    sds = jax.ShapeDtypeStruct
    if size == 8:
        fw, dw = w_up.per, w_down.per
        assert hidden == 8 * fw and width == 2 * fw == 8 * dw
        pair = lambda j, tab: lax.bitwise_xor(lax.shift_right_logical(tab[dev], 1), j)
        g_shapes = [sds((8 * (fw + chunks * dw), width), BF)]
        g_specs = [anywhere]
    else:
        pair = lambda j, tab: j
        g_shapes = [sds((width, hidden), BF)] * 2
        g_specs = [pl.BlockSpec((width, width), lambda j, t, tab: (0, j))] * 2
    block = lambda index: pl.BlockSpec((tb, width), index)
    weights = w_up.arrays + w_down.arrays + w_proj.arrays
    dma = pltpu.SemaphoreType.DMA
    return pl.pallas_call(
        partial(middle_kernel, size, tb, sub, chunks, w_up, w_down, w_proj),
        out_shape=[sds((n, width), F32), sds((n, hidden), BF), sds((n, width), F32)] + g_shapes,
        grid_spec=pltpu.PrefetchScalarGridSpec(
            num_scalar_prefetch=1,
            grid=(chunks, steps),
            in_specs=[pl.BlockSpec((8, width), fixed)] + [block(first)] * 3 + [anywhere] * len(weights),
            out_specs=[block(first), block(lambda j, t, tab: (t, pair(j, tab))), block(final)] + g_specs,
            scratch_shapes=[
                pltpu.VMEM((n, width), BF),
                pltpu.VMEM((width, n), BF),
                pltpu.VMEM((n, width), BF),
                pltpu.VMEM((width, n), BF),
                pltpu.VMEM((n, width), F32),
                pltpu.VMEM((width, width), F32),
                pltpu.VMEM((width, width), F32),
                pltpu.VMEM((width, width), BF),
                pltpu.VMEM((2, width, width), BF),
                pltpu.VMEM((2, width, width), BF),
                pltpu.VMEM((2, width // 2, width), BF),
                pltpu.VMEM((width, width), BF),
                dma((8,)),
                dma((2, 2)),
                dma((2, 8)),
                dma((10,)),
            ],
        ),
        compiler_params=pltpu.CompilerParams(vmem_limit_bytes=VMEM_LIMIT),
        cost_estimate=cost(n * width * (10 * hidden + 2 * width), n * (width * 22 + 2 * hidden) + 8 * hidden * width),
        name="middle",
    )(table, norms, att, x, cot, *weights)


def attended_back_kernel(size, tb, sub, block, w_down, w_proj, tab, nrm_ref, x1_ref, dh_ref, cot_ref, att_ref, *rest):
    count = len(w_down.arrays) if size == 8 else 1
    w_refs = rest[:count]
    dx_ref, da_ref, gn_ref, *g_refs, acc, wp_sc, sems = rest[count:]
    t = pl.program_id(0)
    me = tab[tab.shape[0] - 1]
    per = ROW_LEN // tb
    valid = tab[lax.div(t, per) * STRIDE + 33] - lax.rem(t, per) * tb
    width = x1_ref.shape[1]

    @pl.when(t == 0)
    def _():
        if size == 8:
            copies = down_copies(w_down, w_refs, block, wp_sc, sems, me)
        else:
            copies = [pltpu.make_async_copy(w_refs[0], wp_sc, sems.at[0])]
        for c in copies:
            c.start()
        acc[...] = jnp.zeros_like(acc)
        gn_ref[...] = jnp.zeros_like(gn_ref)
        for c in copies:
            c.wait()

    dgain = jnp.zeros((1, width), F32)
    dshift = jnp.zeros((1, width), F32)
    dbs = []
    for i in range(0, tb, sub):
        p = pl.ds(i, sub)
        unit, rate = norm_stats(x1_ref[p, :])
        dh = dh_ref[p, :]
        ok = lax.broadcasted_iota(jnp.int32, (sub, 1), 0) + i < valid
        dx = jnp.where(ok, cot_ref[p, :].astype(F32), 0.0) + norm_back(unit, rate, nrm_ref[2:3, :], dh)
        dx_ref[p, :] = dx
        dbs.append(dx.astype(BF))
        da_ref[p, :] = mm(dbs[-1], wp_sc[...], NN).astype(BF)
        dgain += jnp.sum(dh * unit, axis=0, keepdims=True)
        dshift += jnp.sum(dh, axis=0, keepdims=True)
    acc[...] += mm(jnp.concatenate(dbs, axis=0), att_ref[...], TN)
    gn_ref[0:1, :] += dgain
    gn_ref[1:2, :] += dshift

    @pl.when(t == pl.num_programs(0) - 1)
    def _():
        if size == 8:
            by_owner(acc, w_down.per, *g_refs, me)
        else:
            g_refs[0][...] = acc[...].astype(BF)


def attended_back(table, norms, x1, dh, cot, att, w_down, w_proj, size, tb=256, sub=256):
    n, width = x1.shape
    weights = w_down.arrays if size == 8 else w_proj.arrays
    block = pl.BlockSpec((tb, width), lambda t, tab: (t, 0))
    fixed = pl.BlockSpec((8, width), lambda t, tab: (0, 0))
    sds = jax.ShapeDtypeStruct
    g_shapes = [(4, w_down.per, width)] * 2 if size == 8 else [(width, width)]
    return pl.pallas_call(
        partial(attended_back_kernel, size, tb, sub, 4, w_down, w_proj),
        out_shape=[sds((n, width), F32), sds((n, width), BF), sds((8, width), F32)] + [sds(g, BF) for g in g_shapes],
        grid_spec=pltpu.PrefetchScalarGridSpec(
            num_scalar_prefetch=1,
            grid=(n // tb,),
            in_specs=[fixed] + [block] * 4 + [pl.BlockSpec(memory_space=pl.ANY)] * len(weights),
            out_specs=[block, block, fixed] + [pl.BlockSpec(g, lambda t, tab, k=len(g): (0,) * k) for g in g_shapes],
            scratch_shapes=[
                pltpu.VMEM((width, width), F32),
                pltpu.VMEM((width, width), BF),
                pltpu.SemaphoreType.DMA((8,)),
            ],
        ),
        compiler_params=pltpu.CompilerParams(vmem_limit_bytes=VMEM_LIMIT),
        cost_estimate=cost(4 * n * width * width, n * width * 18),
        name="attended_back",
    )(table, norms, x1, dh, cot, att, *weights)


def finish_kernel(size, blocks, w_down, tab, x1_ref, act_ref, *rest):
    w_refs = rest[: len(w_down.arrays)]
    out_ref, w_sc, sems = rest[-3:]
    t = pl.program_id(0)
    me = tab[tab.shape[0] - 1]
    tb, width = x1_ref.shape

    def copies(b):
        if size == 8:
            return down_copies(w_down, w_refs, b, w_sc.at[:, pl.ds(b * width, width)], sems.at[b], me)
        at = pl.ds(b * width, width)
        return [pltpu.make_async_copy(w_refs[0].at[:, at], w_sc.at[:, at], sems.at[b, 0])]

    @pl.when(t == 0)
    def _():
        for b in range(blocks):
            for c in copies(b):
                c.start()
        for b in range(blocks):
            for c in copies(b):
                c.wait()

    x2 = x1_ref[...] + mm(act_ref[...], w_sc[...], NT)
    per = ROW_LEN // tb
    valid = tab[lax.div(t, per) * STRIDE + 33] - lax.rem(t, per) * tb
    ok = lax.broadcasted_iota(jnp.int32, (tb, 1), 0) < valid
    out_ref[...] = jnp.where(ok, x2, 0.0).astype(BF)


def finish(table, x1, act, w_down, size, tb=256):
    n, width = x1.shape
    hidden = act.shape[1]
    blocks = hidden // width
    count = len(w_down.arrays)
    block = lambda w: pl.BlockSpec((tb, w), lambda t, tab: (t, 0))
    return pl.pallas_call(
        partial(finish_kernel, size, blocks, w_down),
        out_shape=jax.ShapeDtypeStruct((n, width), BF),
        grid_spec=pltpu.PrefetchScalarGridSpec(
            num_scalar_prefetch=1,
            grid=(n // tb,),
            in_specs=[block(width), block(hidden)] + [pl.BlockSpec(memory_space=pl.ANY)] * count,
            out_specs=block(width),
            scratch_shapes=[pltpu.VMEM((width, hidden), BF), pltpu.SemaphoreType.DMA((blocks, 8))],
        ),
        compiler_params=pltpu.CompilerParams(vmem_limit_bytes=VMEM_LIMIT),
        cost_estimate=cost(2 * n * width * hidden, n * (width * 6 + hidden * 2) + 2 * width * hidden),
        name="finish",
    )(table, x1, act, *w_down.arrays)


def per_device(
    size,
    replicas,
    tokens,
    segment_ids,
    cotangent,
    norm_params,
    qkv_weight,
    proj_weight,
    up_weight,
    down_weight,
    target_norms,
    target_qkv,
    target_proj,
    target_up,
    target_down,
):
    count, width = tokens.shape
    rows = count // ROW_LEN
    hidden = down_weight.shape[0]
    own = width // size
    blocks = hidden // width
    fast = size == 8 and replicas == 4
    size = size if fast else 0
    me = lax.axis_index("fsdp")
    table = job_table(segment_ids, rows, me)
    with jax.named_scope("gather_weights"):
        placed = lax.dynamic_update_slice(jnp.zeros((16, width), BF), norm_params, (0, me * own))
        qkv_t, up_t, down_t, proj_t = qkv_weight.T, up_weight.T, down_weight.T, proj_weight.T
        if fast:
            half = qkv_t.shape[0] // 2
            first, second = gather_cross(jnp.concatenate([qkv_t[:half], placed], axis=0), qkv_t[half:])
            far = forward_cross(first, second)
            upper = both_cores([*first, far[0]])
            lower = both_cores([*second, far[1]])
            w_qkv = Weight([(a, s, 0) for a, s in upper] + [(a, s, half) for a, s in lower], 2 * half)
            norm_parts = []
            packed = jnp.concatenate([down_t[:, b * width : (b + 1) * width] for b in range(blocks)] + [proj_t], axis=0)
            up_1, down_1 = after((up_t, packed), first[1], second[2])
            up_x, down_y = hop(up_1, 2, 8), hop(down_1, 4, 8)
            up_2, down_2 = after((up_t, packed), *far)
            up_y, down_x = hop(up_2, 4, 8), hop(down_2, 2, 8)
        else:
            whole = lambda shard: lax.all_gather(shard, "fsdp", axis=0, tiled=True)
            w_qkv, w_up, w_down, w_proj = (Weight([(whole(w), None, 0)], 0) for w in (qkv_t, up_t, down_t, proj_t))
            norm_parts = [lax.psum(placed.astype(F32), "fsdp").astype(BF)]

    keep_rate = 1.0 - ema_rate
    blend = lambda target, weight: ema_rate * target + keep_rate * weight.astype(F32)
    targets = (
        blend(target_norms, norm_params),
        blend(target_qkv, qkv_weight),
        blend(target_proj, proj_weight),
        blend(target_up, up_weight),
        blend(target_down, down_weight),
    )
    stage, *targets = lax.optimization_barrier((table, *targets))
    h1, qkv, norms = project(stage, norm_parts, tokens, w_qkv)
    stage = table
    if fast:
        with jax.named_scope("gather_weights"):
            up_x, down_y, up_t, packed = after((up_x, down_y, up_t, packed), qkv)
            up_far, down_far = hop(up_x, 4, 8), hop(down_y, 2, 8)
            near = both_cores([up_t, up_x]), both_cores([packed])
            stage = after(table, up_x, down_y)
    attended = attention_forward(qkv, stage, rows)
    if fast:
        with jax.named_scope("gather_weights"):
            up_y, down_x, down_y, up_far, down_far = after((up_y, down_x, down_y, up_far, down_far), attended)
            along = hop(up_y, 1, 8), hop(down_x, 1, 8), hop(down_y, 1, 8)
            ups = near[0] + [(up_y, 4), (along[0], 5), (up_far, 6), (hop(up_far, 1, 8), 7)]
            downs = near[1] + [(down_x, 2), (along[1], 3), (down_y, 4), (along[2], 5)]
            downs += [(down_far, 6), (hop(down_far, 1, 8), 7)]
            w_up = Weight([(a, s, 0) for a, s in ups], up_t.shape[0])
            w_down = Weight([(a, s, 0) for a, s in downs], own)
            w_proj = Weight([], own)
    x1, act, grad_second, *grads = middle(
        table, norms, attended, tokens, cotangent, w_up, w_down, w_proj, hidden, size
    )
    grad_middle, grad_attended, grad_norm2, *grad_proj = attended_back(
        table, norms, x1, grad_second, cotangent, attended, w_down, w_proj, size
    )

    after_table = lambda *values: after(table, *values)
    if fast:
        packed_own = lax.psum_scatter(grads[0], "fsdp", scatter_dimension=0, tiled=True)
    dqkv = attention_backward(qkv, grad_attended, table, rows)
    if fast:
        grad_qkv = project_grad(table, *dqkv, h1, grad_proj, size)
        qkv_sum = Scatter(*grad_qkv)
        fw = hidden // 8
        packed_own = after(packed_own, grad_qkv[0])
        packed_sum = lax.psum(packed_own, "rep")
        stage = after_table(packed_own, *qkv_sum.send())
        block_output = finish(stage, x1, act, w_down, size)
        qkv_own = qkv_sum.block(block_output)
        input_grad, grad_norm1 = project_back(after_table(qkv_own), norms, *dqkv, tokens, grad_middle, w_qkv)
        norm_sum = jnp.concatenate([grad_norm1[:2], grad_norm2[:2], jnp.zeros((4, width), F32)], axis=0)
        quarter = quarter_sum(qkv_own, grad_norm1)
        norm_sum = after(norm_sum, quarter)
        for bit in (1, 2):
            norm_sum = norm_sum + hop(norm_sum, bit, 8)
        quarter, norm_sum = after((quarter, norm_sum), packed_sum)
        for bit in (4,):
            norm_sum = norm_sum + hop(norm_sum, bit, 8)
        for bit in (1, 2):
            norm_sum = norm_sum + lax.ppermute(norm_sum, "rep", [(i, i ^ bit) for i in range(4)])
        qkv_own = all_quarters(quarter)
        packed_sum = packed_sum.astype(F32)
        up = jnp.concatenate([packed_sum[:fw, :fw], packed_sum[:fw, fw:]], axis=0)
        down = packed_sum[fw:].reshape(blocks, own, width).transpose(1, 0, 2).reshape(own, hidden)
        qkv_own, proj = qkv_own[: 3 * own], qkv_own[3 * own :]
    else:
        grad_qkv = project_grad(table, *dqkv, h1, [], size)
        input_grad, grad_norm1 = project_back(table, norms, *dqkv, tokens, grad_middle, w_qkv)
        block_output = finish(table, x1, act, w_down, size)
        sums = lambda g, dim: lax.psum(lax.psum_scatter(g, "fsdp", scatter_dimension=dim, tiled=True), "rep").astype(F32)
        up, down, proj, qkv_own = sums(grads[0], 1), sums(grads[1], 0), sums(grad_proj[0], 0), sums(grad_qkv[0], 0)
        norm_sum = jnp.concatenate([grad_norm1[:2], grad_norm2[:2]], axis=0)
        norm_sum = lax.psum(norm_sum, ("fsdp", "rep"))
    norm_grad = lax.dynamic_slice(norm_sum, (0, me * own), (4, own))
    return (block_output, input_grad, norm_grad, qkv_own.T, proj.T, up, down.T, *targets)


def solution(mesh):
    tokens = P(("fsdp", "rep"), None)
    columns = P(None, "fsdp")
    return jax.shard_map(
        partial(per_device, mesh.shape["fsdp"], mesh.shape["rep"]),
        mesh=mesh,
        in_specs=(tokens, P(("fsdp", "rep")), tokens) + (columns,) * 10,
        out_specs=(tokens, tokens) + (columns,) * 10,
        check_vma=False,
    )
```

```python
import math
from functools import partial

import jax
import jax.numpy as jnp
from jax import lax
from jax.experimental import pallas as pl
from jax.experimental.pallas import tpu as pltpu
from jax.sharding import PartitionSpec as P

HEAD = 64
ROW_LEN = 1024
layer_eps = 1e-06
ema_rate = 0.75

BF = jnp.bfloat16
F32 = jnp.float32
NN = (((1,), (0,)), ((), ()))
NT = (((1,), (1,)), ((), ()))
TN = (((0,), (0,)), ((), ()))
VMEM_LIMIT = 66_000_000
GRANT = 32_000_000
COST_SCALE = 0.02

QW = 256
KW = 224
FIT = KW - 15
SMALL = 128
FIT_SMALL = SMALL - 15
KB = 128
STRIDE = 35


def mm(left, right, dims):
    return lax.dot_general(left, right, dims, preferred_element_type=F32)


def cost(flops, moved):
    return pl.CostEstimate(flops=int(flops * COST_SCALE), bytes_accessed=int(moved * COST_SCALE), transcendentals=0)


def job_table(segment_ids, rows, device):
    seg = segment_ids.reshape(rows, 1, ROW_LEN)
    ident = jnp.arange(16, dtype=jnp.int32)[None, :, None]
    real = seg >= 0
    starts = jnp.sum((real & (seg < ident)).astype(jnp.int32), axis=2)
    after = jnp.sum((real & (seg < ident + 1)).astype(jnp.int32), axis=2)
    images = jnp.max(seg, axis=2) + 1
    ends = jnp.where(jnp.arange(16, dtype=jnp.int32)[None, :] < images, after, ROW_LEN)
    valid = jnp.sum(real.astype(jnp.int32), axis=2)
    pad = ROW_LEN - valid
    fits = pad <= FIT
    jobs = images + jnp.where((pad > 0) & fits, 1, 0)
    wide = jnp.where(fits, 0, (pad + 15 + QW - 1) // QW)
    table = jnp.concatenate([starts, ends, jobs, valid, wide], axis=1).reshape(-1)
    return jnp.concatenate([table, device.astype(jnp.int32).reshape(1)])


def lane_of(count):
    return lax.broadcasted_iota(jnp.int32, (count, 128), 1)


def slot_of(count, base):
    return lax.broadcasted_iota(jnp.int32, (count, 128), 0) + base


def half_lanes(count, par):
    return (lane_of(count) < 64) if par == 0 else (lane_of(count) >= 64)


def spare_lane(count, par):
    return lane_of(count) == (64 if par == 0 else 0)


def query_side(q, par):
    n = q.shape[0]
    return jnp.where(half_lanes(n, par), q * BF(0.125), jnp.where(spare_lane(n, par), BF(1), BF(0)))


def key_side(k, par, inside):
    n = k.shape[0]
    return jnp.where(half_lanes(n, par), k, jnp.where(spare_lane(n, par) & (~inside), BF(-1e30), BF(0)))


def one_head(x, par):
    return jnp.where(half_lanes(x.shape[0], par), x, BF(0))


def each_image(tab, base, work):
    def job(j, carry):
        begin = tab[base + j]
        end = tab[base + 16 + j]
        low = lax.div(begin, 16) * 16
        small = end - begin <= FIT_SMALL
        for fits, nq, nk in ((small, SMALL, SMALL), (~small, QW, KW)):

            @pl.when(fits)
            def _():
                q0 = pl.multiple_of(jnp.minimum(low, ROW_LEN - nq), 16)
                k0 = pl.multiple_of(jnp.minimum(low, ROW_LEN - nk), 16)
                kr = slot_of(nk, k0)
                qr = slot_of(nq, q0)
                work(pl.ds(q0, nq), pl.ds(k0, nk), (qr >= begin) & (qr < end), (kr >= begin) & (kr < end))

        return carry

    lax.fori_loop(0, tab[base + 32], job, 0)


def attend_kernel(pairs, tab, q_ref, k_ref, v_ref, o_ref, a_sc):
    base = pl.program_id(0) * STRIDE
    o_ref[...] = jnp.zeros_like(o_ref)

    def work(qs, ks, qin, inside):
        scores = []
        for p in range(pairs):
            cs = pl.ds(128 * p, 128)
            q = q_ref[qs, cs]
            k = k_ref[ks, cs]
            for par in range(2):
                scores.append(mm(key_side(k, par, inside), query_side(q, par), NT))
        probs = []
        for st in scores:
            expo = jnp.exp(st - jnp.max(st, axis=0, keepdims=True))
            total = jnp.sum(expo, axis=0, keepdims=True)
            probs.append((expo * (1.0 / total)).astype(BF))
        for p in range(pairs):
            cs = pl.ds(128 * p, 128)
            v = v_ref[ks, cs]
            o = jnp.concatenate(
                [mm(v[:, 64 * par : 64 * par + 64], probs[2 * p + par], TN) for par in range(2)], axis=0
            ).T
            o_ref[qs, cs] = jnp.where(qin, o.astype(BF), o_ref[qs, cs])

    each_image(tab, base, work)

    start = tab[base + 33]
    low = lax.div(start, 16) * 16

    def wide(i, carry):
        q0 = pl.multiple_of(jnp.minimum(low + i * QW, ROW_LEN - QW), 16)
        qin = slot_of(QW, q0) >= start

        def pair(p, none):
            cs = pl.ds(pl.multiple_of(128 * p, 128), 128)
            q = q_ref[pl.ds(q0, QW), cs]
            for par in range(2):
                qs = query_side(q, par)

                def block(kb):
                    k0 = pl.multiple_of(kb * KB, KB)
                    k = k_ref[pl.ds(k0, KB), cs]
                    return k0, mm(key_side(k, par, slot_of(KB, k0) >= start), qs, NT)

                def take_max(kb, top):
                    return jnp.maximum(top, jnp.max(block(kb)[1], axis=0, keepdims=True))

                top = lax.fori_loop(0, ROW_LEN // KB, take_max, jnp.full((1, QW), -1e30, F32))

                def take_sum(kb, total):
                    return total + jnp.sum(jnp.exp(block(kb)[1] - top), axis=0, keepdims=True)

                total = lax.fori_loop(0, ROW_LEN // KB, take_sum, jnp.zeros((1, QW), F32))
                a_sc[...] = jnp.zeros_like(a_sc)

                def take_out(kb, c):
                    k0, st = block(kb)
                    prob = (jnp.exp(st - top) * (1.0 / total)).astype(BF)
                    a_sc[...] += mm(one_head(v_ref[pl.ds(k0, KB), cs], par), prob, TN)
                    return c

                lax.fori_loop(0, ROW_LEN // KB, take_out, 0)
                hit = qin & half_lanes(QW, par)
                o_ref[pl.ds(q0, QW), cs] = jnp.where(hit, a_sc[...].T.astype(BF), o_ref[pl.ds(q0, QW), cs])
            return none

        lax.fori_loop(0, pairs, pair, 0)
        return carry

    lax.fori_loop(0, tab[base + 34], wide, 0)


def attend_back_kernel(pairs, tab, q_ref, k_ref, v_ref, d_ref, *rest):
    dq_ref, dk_ref, dv_ref, a_sc, dk_sc, dv_sc = rest[-6:]
    base = pl.program_id(0) * STRIDE
    dq_ref[...] = jnp.zeros_like(dq_ref)
    dk_ref[...] = jnp.zeros_like(dk_ref)
    dv_ref[...] = jnp.zeros_like(dv_ref)

    def work(qs, ks, qin, inside):
        scores = []
        grads = []
        for p in range(pairs):
            cs = pl.ds(128 * p, 128)
            q = q_ref[qs, cs]
            k = k_ref[ks, cs]
            v = v_ref[ks, cs]
            d = jnp.where(qin, d_ref[qs, cs], BF(0))
            for par in range(2):
                scores.append(mm(key_side(k, par, inside), query_side(q, par), NT))
                grads.append(mm(v, one_head(d, par), NT))
        probs = []
        dscores = []
        for st, dp in zip(scores, grads):
            expo = jnp.exp(st - jnp.max(st, axis=0, keepdims=True))
            total = jnp.sum(expo, axis=0, keepdims=True)
            prob = expo * (1.0 / total)
            center = jnp.sum(prob * dp, axis=0, keepdims=True)
            dscores.append((prob * (dp - center)).astype(BF))
            probs.append(prob.astype(BF))
        for p in range(pairs):
            cs = pl.ds(128 * p, 128)
            q = q_ref[qs, cs]
            k = k_ref[ks, cs]
            d = jnp.where(qin, d_ref[qs, cs], BF(0))
            dv = mm(probs[2 * p], one_head(d, 0), NN) + mm(probs[2 * p + 1], one_head(d, 1), NN)
            dk = mm(dscores[2 * p], one_head(q, 0), NN) + mm(dscores[2 * p + 1], one_head(q, 1), NN)
            dq = jnp.concatenate(
                [mm(k[:, 64 * par : 64 * par + 64], dscores[2 * p + par], TN) for par in range(2)], axis=0
            ).T
            dq_ref[qs, cs] = jnp.where(qin, (dq * 0.125).astype(BF), dq_ref[qs, cs])
            dk_ref[ks, cs] = jnp.where(inside, (dk * 0.125).astype(BF), dk_ref[ks, cs])
            dv_ref[ks, cs] = jnp.where(inside, dv.astype(BF), dv_ref[ks, cs])

    each_image(tab, base, work)

    start = tab[base + 33]
    low = lax.div(start, 16) * 16
    windows = tab[base + 34]

    def pair(p, none):
        cs = pl.ds(pl.multiple_of(128 * p, 128), 128)

        @pl.when(windows > 0)
        def _():
            dk_sc[...] = jnp.zeros_like(dk_sc)
            dv_sc[...] = jnp.zeros_like(dv_sc)

        def wide(i, carry):
            first = jnp.maximum(start, low + i * QW)
            q0 = pl.multiple_of(jnp.minimum(low + i * QW, ROW_LEN - QW), 16)
            qin = slot_of(QW, q0) >= first
            q = q_ref[pl.ds(q0, QW), cs]
            d = jnp.where(qin, d_ref[pl.ds(q0, QW), cs], BF(0))
            for par in range(2):
                qh = query_side(q, par)
                dh = one_head(d, par)
                qo = one_head(q, par)

                def block(kb):
                    k0 = pl.multiple_of(kb * KB, KB)
                    k = k_ref[pl.ds(k0, KB), cs]
                    v = v_ref[pl.ds(k0, KB), cs]
                    return k0, k, mm(key_side(k, par, slot_of(KB, k0) >= start), qh, NT), mm(v, dh, NT)

                def take_max(kb, top):
                    return jnp.maximum(top, jnp.max(block(kb)[2], axis=0, keepdims=True))

                top = lax.fori_loop(0, ROW_LEN // KB, take_max, jnp.full((1, QW), -1e30, F32))

                def take_sums(kb, sums):
                    _, _, st, dp = block(kb)
                    expo = jnp.exp(st - top)
                    return (
                        sums[0] + jnp.sum(expo, axis=0, keepdims=True),
                        sums[1] + jnp.sum(expo * dp, axis=0, keepdims=True),
                    )

                none = jnp.zeros((1, QW), F32)
                total, weighted = lax.fori_loop(0, ROW_LEN // KB, take_sums, (none, none))
                scale = 1.0 / total
                center = weighted * scale
                a_sc[...] = jnp.zeros_like(a_sc)

                def take_grads(kb, c):
                    k0, k, st, dp = block(kb)
                    prob = jnp.exp(st - top) * scale
                    ds = (prob * (dp - center)).astype(BF)
                    a_sc[...] += mm(one_head(k, par), ds, TN)
                    dk_sc[pl.ds(k0, KB), :] += mm(ds, qo, NN)
                    dv_sc[pl.ds(k0, KB), :] += mm(prob.astype(BF), dh, NN)
                    return c

                lax.fori_loop(0, ROW_LEN // KB, take_grads, 0)
                hit = qin & half_lanes(QW, par)
                dq = (a_sc[...].T * 0.125).astype(BF)
                dq_ref[pl.ds(q0, QW), cs] = jnp.where(hit, dq, dq_ref[pl.ds(q0, QW), cs])
            return carry

        lax.fori_loop(0, windows, wide, 0)

        @pl.when(windows > 0)
        def _():
            kin = slot_of(ROW_LEN, 0) >= start
            dk_ref[:, cs] = jnp.where(kin, (dk_sc[...] * 0.125).astype(BF), dk_ref[:, cs])
            dv_ref[:, cs] = jnp.where(kin, dv_sc[...].astype(BF), dv_ref[:, cs])

        return none

    lax.fori_loop(0, jnp.where(windows > 0, pairs, 0), pair, 0)


def attention_call(kernel, name, outs, scratch, qkv, extra, table, rows, flops, moved):
    n = qkv.shape[0]
    width = qkv.shape[1] // 3
    spec = lambda part: pl.BlockSpec((ROW_LEN, width), lambda r, t: (r, part))
    return pl.pallas_call(
        partial(kernel, width // 128),
        out_shape=[jax.ShapeDtypeStruct((n, width), BF)] * outs,
        grid_spec=pltpu.PrefetchScalarGridSpec(
            num_scalar_prefetch=1,
            grid=(rows,),
            in_specs=[spec(0), spec(1), spec(2)] + [spec(0)] * len(extra),
            out_specs=[spec(0)] * outs,
            scratch_shapes=scratch,
        ),
        compiler_params=pltpu.CompilerParams(vmem_limit_bytes=VMEM_LIMIT),
        cost_estimate=cost(rows * flops, rows * moved * ROW_LEN * width),
        name=name,
    )(table, qkv, qkv, qkv, *extra)


def attention_forward(qkv, table, rows):
    scratch = [pltpu.VMEM((128, QW), F32)]
    return attention_call(attend_kernel, "attend", 1, scratch, qkv, [], table, rows, 12e9, 8)[0]


def attention_backward(qkv, da, table, rows):
    scratch = [pltpu.VMEM((128, QW), F32), pltpu.VMEM((ROW_LEN, 128), F32), pltpu.VMEM((ROW_LEN, 128), F32)]
    return attention_call(attend_back_kernel, "attend_back", 3, scratch, qkv, [da], table, rows, 24e9, 14)


def hop(value, bit, size):
    return lax.ppermute(value, "fsdp", [(i, i ^ bit) for i in range(size)])


def gather_cross(first, second):
    first_x, second_y = hop(first, 2, 8), hop(second, 4, 8)
    first_late, second_late = after((first, second), hop(second[:16], 1, 8))
    first_y, second_x = hop(first_late, 4, 8), hop(second_late, 2, 8)
    return (first, first_x, first_y), (second, second_x, second_y)


def forward_cross(firsts, seconds):
    return hop(firsts[1], 4, 8), hop(seconds[2], 2, 8)


def both_cores(arrays):
    own = [(array, 2 * i) for i, array in enumerate(arrays)]
    return own + [(hop(array, 1, 8), slot + 1) for array, slot in own]


def after(value, *others):
    return lax.optimization_barrier((value, *others))[0]


def total(*terms):
    return sum(t.astype(F32) for t in terms).astype(BF)


class Scatter:
    def __init__(self, even, odd):
        self.even = even
        self.core = hop(odd, 1, 8)

    def send(self):
        self.out = [total(self.even[q], self.core[q]) for q in (1, 2, 3)]
        return self.out

    def block(self, done):
        come = after([hop(block, 2 * q, 8) for q, block in zip((1, 2, 3), self.out)], done)
        return total(self.even[0], self.core[0], *come)


def shift(value, by):
    return lax.ppermute(value, "rep", [(i, (i + by) % 4) for i in range(4)])


def quarter_sum(block, done):
    z = lax.axis_index("rep")
    quarters = block.reshape(4, block.shape[0] // 4, block.shape[1])
    pick = lambda by: lax.dynamic_index_in_dim(quarters, lax.rem(z + by, 4), 0, False)
    return total(pick(0), *after([shift(pick(by), by) for by in (2, 1, 3)], done))


def all_quarters(mine):
    z = lax.axis_index("rep")
    parts = [mine] + [shift(mine, by) for by in (1, 2, 3)]
    out = jnp.zeros((4, *mine.shape), F32)
    for by, part in enumerate(parts):
        out = lax.dynamic_update_index_in_dim(out, part.astype(F32), lax.rem(z - by + 4, 4), 0)
    return out.reshape(4 * mine.shape[0], mine.shape[1])


class Weight:
    def __init__(self, pieces, per):
        self.arrays = [p[0] for p in pieces]
        self.places = [p[1:] for p in pieces]
        self.per = per

    def copies(self, refs, dst, sems, me):
        out = []
        for i, (ref, (slot, row)) in enumerate(zip(refs, self.places)):
            src, into = ref, dst
            if slot is not None:
                half = self.per // 2
                src = ref.at[pl.ds(0, half), :]
                into = dst.at[pl.ds(pl.multiple_of((me ^ slot) * self.per + row, half), half), :]
            out.append(pltpu.make_async_copy(src, into, sems.at[i]))
        return out


def norm_stats(values):
    center = values - jnp.mean(values, axis=1, keepdims=True)
    rate = lax.rsqrt(jnp.mean(center * center, axis=1, keepdims=True) + layer_eps)
    return center * rate, rate


def norm_back(unit, rate, gain, grad):
    scaled = grad * gain
    mean = jnp.mean(scaled, axis=1, keepdims=True)
    along = jnp.mean(scaled * unit, axis=1, keepdims=True)
    return rate * (scaled - mean - unit * along)


def project_kernel(weight, count, tab, x_ref, *rest):
    w_refs = rest[:count]
    h_ref, qkv_ref, nrm_ref, w_sc, n_sc, sems, n_sems = rest[-7:]
    me = tab[tab.shape[0] - 1]
    half = weight.per // 2

    @pl.when(pl.program_id(0) == 0)
    def _():
        if len(rest) - 7 > count:
            norm_copies = [pltpu.make_async_copy(rest[count], n_sc.at[0], n_sems.at[0])]
        else:
            norm_copies = [
                pltpu.make_async_copy(w_refs[i].at[pl.ds(half, 16), :], n_sc.at[i], n_sems.at[i]) for i in range(8)
            ]
        copies = weight.copies(w_refs, w_sc, sems, me)
        for c in norm_copies + copies:
            c.start()
        for c in norm_copies:
            c.wait()
        if len(norm_copies) == 1:
            placed = n_sc[0].astype(F32)
        else:
            own = n_sc.shape[2] // 8
            placed = sum(
                pltpu.roll(n_sc[i].astype(F32), (me ^ weight.places[i][0]) * own, 1) for i in range(len(norm_copies))
            )
        nrm_ref[...] = placed[:8, :]

    tb, width = x_ref.shape
    parts = [pl.ds(i, tb // 2) for i in range(0, tb, tb // 2)]
    for p in parts:
        unit, _ = norm_stats(x_ref[p, :].astype(F32))
        h_ref[p, :] = (unit * nrm_ref[0:1, :] + nrm_ref[1:2, :]).astype(BF)

    @pl.when(pl.program_id(0) == 0)
    def _():
        for c in weight.copies(w_refs, w_sc, sems, me):
            c.wait()

    for p in parts:
        qkv_ref[p, :] = mm(h_ref[p, :], w_sc[...], NT).astype(BF)


def project(table, norm_parts, x, weight, tb=512):
    n, width = x.shape
    count = len(weight.arrays)
    anywhere = pl.BlockSpec(memory_space=pl.ANY)
    block = lambda w: pl.BlockSpec((tb, w), lambda t, tab: (t, 0))
    sds = jax.ShapeDtypeStruct
    return pl.pallas_call(
        partial(project_kernel, weight, count),
        out_shape=[sds((n, width), BF), sds((n, 3 * width), BF), sds((8, width), F32)],
        grid_spec=pltpu.PrefetchScalarGridSpec(
            num_scalar_prefetch=1,
            grid=(n // tb,),
            in_specs=[block(width)] + [anywhere] * (count + len(norm_parts)),
            out_specs=[block(width), block(3 * width), pl.BlockSpec((8, width), lambda t, tab: (0, 0))],
            scratch_shapes=[
                pltpu.VMEM((3 * width, width), BF),
                pltpu.VMEM((8, 16, width), BF),
                pltpu.SemaphoreType.DMA((count,)),
                pltpu.SemaphoreType.DMA((8,)),
            ],
        ),
        compiler_params=pltpu.CompilerParams(vmem_limit_bytes=VMEM_LIMIT),
        cost_estimate=cost(6 * n * width * width, n * width * 10 + 6 * width * width),
        name="project",
    )(table, x, *weight.arrays, *norm_parts)


def by_owner(acc, per, even_ref, odd_ref, me):
    for q in range(4):
        for parity, ref in ((0, even_ref), (1, odd_ref)):
            at = pl.multiple_of((me ^ (2 * q + parity)) * per, per)
            ref[q] = acc[pl.ds(at, per), :].astype(BF)


def project_grad_kernel(size, tab, dq_ref, dk_ref, dv_ref, h_ref, *rest):
    acc = rest[-1]
    t = pl.program_id(0)
    width = h_ref.shape[1]

    @pl.when(t == 0)
    def _():
        acc[...] = jnp.zeros_like(acc)

    for part, ref in enumerate((dq_ref, dk_ref, dv_ref)):
        acc[pl.ds(part * width, width), :] += mm(ref[...], h_ref[...], TN)

    @pl.when(t == pl.num_programs(0) - 1)
    def _():
        if size == 8:
            per = acc.shape[0] // 8
            by_owner(acc, per, *(ref.at[:, pl.ds(0, per), :] for ref in rest[2:4]), tab[tab.shape[0] - 1])
            for src, dst in zip(rest[0:2], rest[2:4]):
                dst[:, pl.ds(per, src.shape[1]), :] = src[...]
        else:
            rest[0][...] = acc[...].astype(BF)


def project_grad(table, dq, dk, dv, h, proj, size, tb=512):
    n, width = h.shape
    rows = 3 * width
    block = pl.BlockSpec((tb, width), lambda t, tab: (t, 0))
    whole = lambda s: pl.BlockSpec(s, lambda t, tab, k=len(s): (0,) * k)
    shapes = [(4, rows // 8 + proj[0].shape[1], width)] * 2 if size == 8 else [(rows, width)]
    return pl.pallas_call(
        partial(project_grad_kernel, size),
        out_shape=[jax.ShapeDtypeStruct(s, BF) for s in shapes],
        grid_spec=pltpu.PrefetchScalarGridSpec(
            num_scalar_prefetch=1,
            grid=(n // tb,),
            in_specs=[block] * 4 + [whole(p.shape) for p in proj],
            out_specs=[whole(s) for s in shapes],
            scratch_shapes=[pltpu.VMEM((rows, width), F32)],
        ),
        compiler_params=pltpu.CompilerParams(vmem_limit_bytes=VMEM_LIMIT),
        cost_estimate=cost(6 * n * width * width, n * width * 8 + 6 * width * width),
        name="project_grad",
    )(table, dq, dk, dv, h, *proj)


def project_back_kernel(weight, count, tab, nrm_ref, dq_ref, dk_ref, dv_ref, x_ref, dx_ref, *rest):
    w_refs = rest[:count]
    out_ref, gn_ref, w_sc, sems = rest[-4:]
    t = pl.program_id(0)
    me = tab[tab.shape[0] - 1]
    width = x_ref.shape[1]

    @pl.when(t == 0)
    def _():
        copies = weight.copies(w_refs, w_sc, sems, me)
        for c in copies:
            c.start()
        gn_ref[...] = jnp.zeros_like(gn_ref)
        for c in copies:
            c.wait()

    tb = x_ref.shape[0]
    parts = [pl.ds(i, tb // 2) for i in range(0, tb, tb // 2)]
    units = [norm_stats(x_ref[p, :].astype(F32)) for p in parts]
    dgain = jnp.zeros((1, width), F32)
    dshift = jnp.zeros((1, width), F32)
    for p, (unit, rate) in zip(parts, units):
        grad = mm(dq_ref[p, :], w_sc[pl.ds(0, width), :], NN)
        grad += mm(dk_ref[p, :], w_sc[pl.ds(width, width), :], NN)
        grad += mm(dv_ref[p, :], w_sc[pl.ds(2 * width, width), :], NN)
        out_ref[p, :] = (dx_ref[p, :] + norm_back(unit, rate, nrm_ref[0:1, :], grad)).astype(BF)
        dgain += jnp.sum(grad * unit, axis=0, keepdims=True)
        dshift += jnp.sum(grad, axis=0, keepdims=True)
    gn_ref[0:1, :] += dgain
    gn_ref[1:2, :] += dshift


def project_back(table, norms, dq, dk, dv, x, dx, weight, tb=256):
    n, width = x.shape
    count = len(weight.arrays)
    anywhere = pl.BlockSpec(memory_space=pl.ANY)
    block = pl.BlockSpec((tb, width), lambda t, tab: (t, 0))
    fixed = pl.BlockSpec((8, width), lambda t, tab: (0, 0))
    return pl.pallas_call(
        partial(project_back_kernel, weight, count),
        out_shape=[jax.ShapeDtypeStruct((n, width), BF), jax.ShapeDtypeStruct((8, width), F32)],
        grid_spec=pltpu.PrefetchScalarGridSpec(
            num_scalar_prefetch=1,
            grid=(n // tb,),
            in_specs=[fixed] + [block] * 5 + [anywhere] * count,
            out_specs=[block, fixed],
            scratch_shapes=[pltpu.VMEM((3 * width, width), BF), pltpu.SemaphoreType.DMA((count,))],
        ),
        compiler_params=pltpu.CompilerParams(vmem_limit_bytes=VMEM_LIMIT),
        cost_estimate=cost(6 * n * width * width, n * width * 14 + 6 * width * width),
        name="project_back",
    )(table, norms, dq, dk, dv, x, dx, *weight.arrays)


def gelu_both(values):
    phi = 0.5 + 0.5 * lax.erf(values * math.sqrt(0.5))
    bell = jnp.exp(values * values * -0.5) * (1.0 / math.sqrt(2.0 * math.pi))
    return values * phi, phi + values * bell


def down_copies(weight, refs, block, dst, sems, me):
    out = []
    for i, (ref, (slot, _)) in enumerate(zip(refs, weight.places)):
        src = ref.at[pl.ds(pl.multiple_of(block * weight.per, weight.per), weight.per), :]
        at = pl.multiple_of((me ^ slot) * weight.per, weight.per)
        out.append(pltpu.make_async_copy(src, dst.at[pl.ds(at, weight.per), :], sems.at[i]))
    return out


def middle_kernel(size, tb, sub, chunks, w_up, w_down, w_proj, tab, nrm_ref, att_ref, x_ref, cot_ref, *rest):
    ups, downs = len(w_up.arrays), len(w_down.arrays)
    up_refs, down_refs = rest[:ups], rest[ups : ups + downs]
    proj_refs = down_refs if size == 8 else rest[ups + downs : ups + downs + 1]
    outs = 1 if size == 8 else 2
    rest = rest[-(19 + outs) :]
    x1_ref, act_ref, dh_ref = rest[:3]
    g_refs = rest[3 : 3 + outs]
    h_sc, ht_sc, dy_sc, dyt_sc, dh_sc, gu_sc, gd_sc, wp_sc, wu_sc, wd_sc, su_sc, sd_sc, p_sem, u_sem, d_sem, g_sem = rest[3 + outs :]
    j = pl.program_id(0)
    t = pl.program_id(1)
    steps = pl.num_programs(1)
    me = tab[tab.shape[0] - 1]
    per = ROW_LEN // tb
    valid = tab[lax.div(t, per) * STRIDE + 33]
    ok = (lax.broadcasted_iota(jnp.int32, (tb, 1), 0) + lax.rem(t, per) * tb) < valid
    ts = pl.ds(pl.multiple_of(t * tb, tb), tb)
    width = x_ref.shape[1]
    gain = nrm_ref[2:3, :]
    shift = nrm_ref[3:4, :]
    parts = [pl.ds(pl.multiple_of(t * tb + i, sub), sub) for i in range(0, tb, sub)]
    pieces = [pl.ds(i, sub) for i in range(0, tb, sub)]

    def chunk_copies(m):
        b = m % 2
        if size != 8:
            piece = pl.ds(m * width, width)
            up = [pltpu.make_async_copy(up_refs[0].at[piece, :], wu_sc.at[b], u_sem.at[b, 0])]
            down = [pltpu.make_async_copy(down_refs[0].at[:, piece], wd_sc.at[b], d_sem.at[b, 0])]
            return up + down
        up = []
        for i, (ref, (slot, _)) in enumerate(zip(up_refs, w_up.places)):
            if slot // 2 == m:
                at = pl.multiple_of(((me & 1) ^ (slot & 1)) * w_up.per, w_up.per)
                into = wu_sc.at[b].at[pl.ds(at, w_up.per), :]
                up.append(pltpu.make_async_copy(ref, into, u_sem.at[b, len(up)]))
        return up + down_copies(w_down, down_refs, (me >> 1) ^ m, wd_sc.at[b], d_sem.at[b], me)

    def proj_copies():
        if size != 8:
            return [pltpu.make_async_copy(proj_refs[0], wp_sc, p_sem.at[0])]
        return down_copies(w_down, proj_refs, chunks, wp_sc, p_sem, me)

    def packed_copies(pair):
        fw, dw = w_up.per, w_down.per
        whole = fw + chunks * dw
        out = []
        for d in range(8):
            at = pl.multiple_of(d * whole + fw + pair * dw, dw)
            out.append(pltpu.make_async_copy(sd_sc.at[pl.ds(d * dw, dw), :], g_refs[0].at[pl.ds(at, dw), :], g_sem.at[d]))
        for k in range(2):
            at = pl.multiple_of((2 * pair + k) * whole, dw)
            out.append(pltpu.make_async_copy(su_sc.at[k], g_refs[0].at[pl.ds(at, fw), :], g_sem.at[8 + k]))
        return out

    @pl.when((j == 0) & (t == 0))
    def _():
        for c in proj_copies() + chunk_copies(0):
            c.start()
        for c in proj_copies():
            c.wait()

    for m in range(chunks):

        @pl.when((j == m) & (t == 0))
        def _():
            for c in chunk_copies(m):
                c.wait()
            if m + 1 < chunks:
                for c in chunk_copies(m + 1):
                    c.start()

    @pl.when(j == 0)
    def _():
        dy = jnp.where(ok, cot_ref[...], BF(0))
        dy_sc[ts, :] = dy
        x1s = [x_ref[p, :].astype(F32) + mm(att_ref[p, :], wp_sc[...], NT) for p in pieces]
        dyt_sc[:, ts] = dy.T
        for p, full, x1 in zip(pieces, parts, x1s):
            x1_ref[p, :] = x1
            unit, _ = norm_stats(x1)
            h = (unit * gain + shift).astype(BF)
            h_sc[full, :] = h
            ht_sc[:, full] = h.T
        dh_sc[ts, :] = jnp.zeros((tb, width), F32)

    @pl.when(t == 0)
    def _():
        gu_sc[...] = jnp.zeros_like(gu_sc)
        gd_sc[...] = jnp.zeros_like(gd_sc)

    wu = wu_sc[lax.rem(j, 2)]
    wd = wd_sc[lax.rem(j, 2)]
    uppers = [mm(h_sc[p, :], wu, NT) for p in parts]
    acts = []
    dups = []
    for p, upper in zip(parts, uppers):
        dact = mm(dy_sc[p, :], wd, NN)
        act, slope = gelu_both(upper)
        acts.append(act.astype(BF))
        dups.append((dact * slope).astype(BF))
    for p, dup in zip(parts, dups):
        dh_sc[p, :] += mm(dup, wu, NN)
    act = jnp.concatenate(acts, axis=0)
    act_ref[...] = act
    gd_sc[...] += mm(dyt_sc[:, ts], act, NN)
    gu_sc[...] += mm(ht_sc[:, ts], jnp.concatenate(dups, axis=0), NN)

    @pl.when(j == chunks - 1)
    def _():
        dh_ref[...] = dh_sc[ts, :]

    @pl.when(t == steps - 1)
    def _():
        if size == 8:
            pair = (me >> 1) ^ j

            @pl.when(j > 0)
            def _():
                for c in packed_copies((me >> 1) ^ (j - 1)):
                    c.wait()

            fw = w_up.per
            for k in range(2):
                for i in range(2):
                    su_sc[k, :, i * fw : (i + 1) * fw] = gu_sc[i * fw : (i + 1) * fw, k * fw : (k + 1) * fw].astype(BF)
            sd_sc[...] = gd_sc[...].astype(BF)
            for c in packed_copies(pair):
                c.start()

            @pl.when(j == chunks - 1)
            def _():
                for c in packed_copies(pair):
                    c.wait()
        else:
            g_refs[0][...] = gu_sc[...].astype(BF)
            g_refs[1][...] = gd_sc[...].astype(BF)


def middle(table, norms, att, x, cot, w_up, w_down, w_proj, hidden, size, tb=512, sub=512):
    n, width = x.shape
    chunks = hidden // width
    steps = n // tb
    dev = table.shape[0] - 1
    first = lambda j, t, tab: (jnp.where(j == 0, t, steps - 1), 0)
    final = lambda j, t, tab: (jnp.where(j == chunks - 1, t, 0), 0)
    fixed = lambda j, t, tab: (0, 0)
    anywhere = pl.BlockSpec(memory_space=pl.ANY)
    sds = jax.ShapeDtypeStruct
    if size == 8:
        fw, dw = w_up.per, w_down.per
        assert hidden == 8 * fw and width == 2 * fw == 8 * dw
        pair = lambda j, tab: lax.bitwise_xor(lax.shift_right_logical(tab[dev], 1), j)
        g_shapes = [sds((8 * (fw + chunks * dw), width), BF)]
        g_specs = [anywhere]
    else:
        pair = lambda j, tab: j
        g_shapes = [sds((width, hidden), BF)] * 2
        g_specs = [pl.BlockSpec((width, width), lambda j, t, tab: (0, j))] * 2
    block = lambda index: pl.BlockSpec((tb, width), index)
    weights = w_up.arrays + w_down.arrays + w_proj.arrays
    dma = pltpu.SemaphoreType.DMA
    return pl.pallas_call(
        partial(middle_kernel, size, tb, sub, chunks, w_up, w_down, w_proj),
        out_shape=[sds((n, width), F32), sds((n, hidden), BF), sds((n, width), F32)] + g_shapes,
        grid_spec=pltpu.PrefetchScalarGridSpec(
            num_scalar_prefetch=1,
            grid=(chunks, steps),
            in_specs=[pl.BlockSpec((8, width), fixed)] + [block(first)] * 3 + [anywhere] * len(weights),
            out_specs=[block(first), block(lambda j, t, tab: (t, pair(j, tab))), block(final)] + g_specs,
            scratch_shapes=[
                pltpu.VMEM((n, width), BF),
                pltpu.VMEM((width, n), BF),
                pltpu.VMEM((n, width), BF),
                pltpu.VMEM((width, n), BF),
                pltpu.VMEM((n, width), F32),
                pltpu.VMEM((width, width), F32),
                pltpu.VMEM((width, width), F32),
                pltpu.VMEM((width, width), BF),
                pltpu.VMEM((2, width, width), BF),
                pltpu.VMEM((2, width, width), BF),
                pltpu.VMEM((2, width // 2, width), BF),
                pltpu.VMEM((width, width), BF),
                dma((8,)),
                dma((2, 2)),
                dma((2, 8)),
                dma((10,)),
            ],
        ),
        compiler_params=pltpu.CompilerParams(vmem_limit_bytes=VMEM_LIMIT),
        cost_estimate=cost(n * width * (10 * hidden + 2 * width), n * (width * 22 + 2 * hidden) + 8 * hidden * width),
        name="middle",
    )(table, norms, att, x, cot, *weights)


def attended_back_kernel(size, tb, sub, block, w_down, w_proj, tab, nrm_ref, x1_ref, dh_ref, cot_ref, att_ref, *rest):
    count = len(w_down.arrays) if size == 8 else 1
    w_refs = rest[:count]
    dx_ref, da_ref, gn_ref, *g_refs, acc, wp_sc, sems = rest[count:]
    t = pl.program_id(0)
    me = tab[tab.shape[0] - 1]
    per = ROW_LEN // tb
    valid = tab[lax.div(t, per) * STRIDE + 33] - lax.rem(t, per) * tb
    width = x1_ref.shape[1]

    @pl.when(t == 0)
    def _():
        if size == 8:
            copies = down_copies(w_down, w_refs, block, wp_sc, sems, me)
        else:
            copies = [pltpu.make_async_copy(w_refs[0], wp_sc, sems.at[0])]
        for c in copies:
            c.start()
        acc[...] = jnp.zeros_like(acc)
        gn_ref[...] = jnp.zeros_like(gn_ref)
        for c in copies:
            c.wait()

    dgain = jnp.zeros((1, width), F32)
    dshift = jnp.zeros((1, width), F32)
    dbs = []
    for i in range(0, tb, sub):
        p = pl.ds(i, sub)
        unit, rate = norm_stats(x1_ref[p, :])
        dh = dh_ref[p, :]
        ok = lax.broadcasted_iota(jnp.int32, (sub, 1), 0) + i < valid
        dx = jnp.where(ok, cot_ref[p, :].astype(F32), 0.0) + norm_back(unit, rate, nrm_ref[2:3, :], dh)
        dx_ref[p, :] = dx
        dbs.append(dx.astype(BF))
        da_ref[p, :] = mm(dbs[-1], wp_sc[...], NN).astype(BF)
        dgain += jnp.sum(dh * unit, axis=0, keepdims=True)
        dshift += jnp.sum(dh, axis=0, keepdims=True)
    acc[...] += mm(jnp.concatenate(dbs, axis=0), att_ref[...], TN)
    gn_ref[0:1, :] += dgain
    gn_ref[1:2, :] += dshift

    @pl.when(t == pl.num_programs(0) - 1)
    def _():
        if size == 8:
            by_owner(acc, w_down.per, *g_refs, me)
        else:
            g_refs[0][...] = acc[...].astype(BF)


def attended_back(table, norms, x1, dh, cot, att, w_down, w_proj, size, tb=256, sub=256):
    n, width = x1.shape
    weights = w_down.arrays if size == 8 else w_proj.arrays
    block = pl.BlockSpec((tb, width), lambda t, tab: (t, 0))
    fixed = pl.BlockSpec((8, width), lambda t, tab: (0, 0))
    sds = jax.ShapeDtypeStruct
    g_shapes = [(4, w_down.per, width)] * 2 if size == 8 else [(width, width)]
    return pl.pallas_call(
        partial(attended_back_kernel, size, tb, sub, 4, w_down, w_proj),
        out_shape=[sds((n, width), F32), sds((n, width), BF), sds((8, width), F32)] + [sds(g, BF) for g in g_shapes],
        grid_spec=pltpu.PrefetchScalarGridSpec(
            num_scalar_prefetch=1,
            grid=(n // tb,),
            in_specs=[fixed] + [block] * 4 + [pl.BlockSpec(memory_space=pl.ANY)] * len(weights),
            out_specs=[block, block, fixed] + [pl.BlockSpec(g, lambda t, tab, k=len(g): (0,) * k) for g in g_shapes],
            scratch_shapes=[
                pltpu.VMEM((width, width), F32),
                pltpu.VMEM((width, width), BF),
                pltpu.SemaphoreType.DMA((8,)),
            ],
        ),
        compiler_params=pltpu.CompilerParams(vmem_limit_bytes=VMEM_LIMIT),
        cost_estimate=cost(4 * n * width * width, n * width * 18),
        name="attended_back",
    )(table, norms, x1, dh, cot, att, *weights)


def finish_kernel(size, blocks, w_down, tab, x1_ref, act_ref, *rest):
    w_refs = rest[: len(w_down.arrays)]
    out_ref, w_sc, sems = rest[-3:]
    t = pl.program_id(0)
    me = tab[tab.shape[0] - 1]
    tb, width = x1_ref.shape

    def copies(b):
        if size == 8:
            return down_copies(w_down, w_refs, b, w_sc.at[:, pl.ds(b * width, width)], sems.at[b], me)
        at = pl.ds(b * width, width)
        return [pltpu.make_async_copy(w_refs[0].at[:, at], w_sc.at[:, at], sems.at[b, 0])]

    @pl.when(t == 0)
    def _():
        for b in range(blocks):
            for c in copies(b):
                c.start()
        for b in range(blocks):
            for c in copies(b):
                c.wait()

    x2 = x1_ref[...] + mm(act_ref[...], w_sc[...], NT)
    per = ROW_LEN // tb
    valid = tab[lax.div(t, per) * STRIDE + 33] - lax.rem(t, per) * tb
    ok = lax.broadcasted_iota(jnp.int32, (tb, 1), 0) < valid
    out_ref[...] = jnp.where(ok, x2, 0.0).astype(BF)


def finish(table, x1, act, w_down, size, tb=256):
    n, width = x1.shape
    hidden = act.shape[1]
    blocks = hidden // width
    count = len(w_down.arrays)
    block = lambda w: pl.BlockSpec((tb, w), lambda t, tab: (t, 0))
    return pl.pallas_call(
        partial(finish_kernel, size, blocks, w_down),
        out_shape=jax.ShapeDtypeStruct((n, width), BF),
        grid_spec=pltpu.PrefetchScalarGridSpec(
            num_scalar_prefetch=1,
            grid=(n // tb,),
            in_specs=[block(width), block(hidden)] + [pl.BlockSpec(memory_space=pl.ANY)] * count,
            out_specs=block(width),
            scratch_shapes=[pltpu.VMEM((width, hidden), BF), pltpu.SemaphoreType.DMA((blocks, 8))],
        ),
        compiler_params=pltpu.CompilerParams(vmem_limit_bytes=VMEM_LIMIT),
        cost_estimate=cost(2 * n * width * hidden, n * (width * 6 + hidden * 2) + 2 * width * hidden),
        name="finish",
    )(table, x1, act, *w_down.arrays)


def per_device(
    size,
    replicas,
    tokens,
    segment_ids,
    cotangent,
    norm_params,
    qkv_weight,
    proj_weight,
    up_weight,
    down_weight,
    target_norms,
    target_qkv,
    target_proj,
    target_up,
    target_down,
):
    count, width = tokens.shape
    rows = count // ROW_LEN
    hidden = down_weight.shape[0]
    own = width // size
    blocks = hidden // width
    fast = size == 8 and replicas == 4
    size = size if fast else 0
    me = lax.axis_index("fsdp")
    table = job_table(segment_ids, rows, me)
    with jax.named_scope("gather_weights"):
        padded = jnp.pad(norm_params, ((0, 12), (0, width - own)))
        qkv_t, up_t, down_t, proj_t = qkv_weight.T, up_weight.T, down_weight.T, proj_weight.T
        if fast:
            half = qkv_t.shape[0] // 2
            first, second = gather_cross(jnp.concatenate([qkv_t[:half], padded], axis=0), qkv_t[half:])
            far = forward_cross(first, second)
            upper = both_cores([*first, far[0]])
            lower = both_cores([*second, far[1]])
            w_qkv = Weight([(a, s, 0) for a, s in upper] + [(a, s, half) for a, s in lower], 2 * half)
            norm_parts = []
            packed = jnp.concatenate([down_t[:, b * width : (b + 1) * width] for b in range(blocks)] + [proj_t], axis=0)
            up_1, down_1 = after((up_t, packed), first[1], second[2])
            up_x, down_y = hop(up_1, 2, 8), hop(down_1, 4, 8)
            up_2, down_2 = after((up_t, packed), *far)
            up_y, down_x = hop(up_2, 4, 8), hop(down_2, 2, 8)
        else:
            whole = lambda shard: lax.all_gather(shard, "fsdp", axis=0, tiled=True)
            w_qkv, w_up, w_down, w_proj = (Weight([(whole(w), None, 0)], 0) for w in (qkv_t, up_t, down_t, proj_t))
            placed = lax.dynamic_update_slice(jnp.zeros((16, width), F32), norm_params.astype(F32), (0, me * own))
            norm_parts = [lax.psum(placed, "fsdp").astype(BF)]

    keep_rate = 1.0 - ema_rate
    blend = lambda target, weight: ema_rate * target + keep_rate * weight.astype(F32)
    targets = (
        blend(target_norms, norm_params),
        blend(target_qkv, qkv_weight),
        blend(target_proj, proj_weight),
        blend(target_up, up_weight),
        blend(target_down, down_weight),
    )
    stage, *targets = lax.optimization_barrier((table, *targets))
    h1, qkv, norms = project(stage, norm_parts, tokens, w_qkv)
    stage = table
    if fast:
        with jax.named_scope("gather_weights"):
            up_x, down_y, up_t, packed = after((up_x, down_y, up_t, packed), qkv)
            up_far, down_far = hop(up_x, 4, 8), hop(down_y, 2, 8)
            near = both_cores([up_t, up_x]), both_cores([packed])
            stage = after(table, up_x, down_y)
    attended = attention_forward(qkv, stage, rows)
    if fast:
        with jax.named_scope("gather_weights"):
            up_y, down_x, down_y, up_far, down_far = after((up_y, down_x, down_y, up_far, down_far), attended)
            along = hop(up_y, 1, 8), hop(down_x, 1, 8), hop(down_y, 1, 8)
            ups = near[0] + [(up_y, 4), (along[0], 5), (up_far, 6), (hop(up_far, 1, 8), 7)]
            downs = near[1] + [(down_x, 2), (along[1], 3), (down_y, 4), (along[2], 5)]
            downs += [(down_far, 6), (hop(down_far, 1, 8), 7)]
            w_up = Weight([(a, s, 0) for a, s in ups], up_t.shape[0])
            w_down = Weight([(a, s, 0) for a, s in downs], own)
            w_proj = Weight([], own)
    x1, act, grad_second, *grads = middle(
        table, norms, attended, tokens, cotangent, w_up, w_down, w_proj, hidden, size
    )
    grad_middle, grad_attended, grad_norm2, *grad_proj = attended_back(
        table, norms, x1, grad_second, cotangent, attended, w_down, w_proj, size
    )

    after_table = lambda *values: after(table, *values)
    if fast:
        packed_own = lax.psum_scatter(grads[0], "fsdp", scatter_dimension=0, tiled=True)
    dqkv = attention_backward(qkv, grad_attended, table, rows)
    if fast:
        grad_qkv = project_grad(table, *dqkv, h1, grad_proj, size)
        qkv_sum = Scatter(*grad_qkv)
        fw = hidden // 8
        packed_own = after(packed_own, grad_qkv[0])
        packed_sum = lax.psum(packed_own, "rep")
        stage = after_table(packed_own, *qkv_sum.send())
        block_output = finish(stage, x1, act, w_down, size)
        qkv_own = qkv_sum.block(block_output)
        input_grad, grad_norm1 = project_back(after_table(qkv_own), norms, *dqkv, tokens, grad_middle, w_qkv)
        norm_sum = jnp.concatenate([grad_norm1[:2], grad_norm2[:2], jnp.zeros((4, width), F32)], axis=0)
        quarter = quarter_sum(qkv_own, grad_norm1)
        norm_sum = after(norm_sum, quarter)
        for bit in (1, 2):
            norm_sum = norm_sum + hop(norm_sum, bit, 8)
        quarter, norm_sum = after((quarter, norm_sum), packed_sum)
        for bit in (4,):
            norm_sum = norm_sum + hop(norm_sum, bit, 8)
        for bit in (1, 2):
            norm_sum = norm_sum + lax.ppermute(norm_sum, "rep", [(i, i ^ bit) for i in range(4)])
        qkv_own = all_quarters(quarter)
        packed_sum = packed_sum.astype(F32)
        up = jnp.concatenate([packed_sum[:fw, :fw], packed_sum[:fw, fw:]], axis=0)
        down = packed_sum[fw:].reshape(blocks, own, width).transpose(1, 0, 2).reshape(own, hidden)
        qkv_own, proj = qkv_own[: 3 * own], qkv_own[3 * own :]
    else:
        grad_qkv = project_grad(table, *dqkv, h1, [], size)
        input_grad, grad_norm1 = project_back(table, norms, *dqkv, tokens, grad_middle, w_qkv)
        block_output = finish(table, x1, act, w_down, size)
        sums = lambda g, dim: lax.psum(lax.psum_scatter(g, "fsdp", scatter_dimension=dim, tiled=True), "rep").astype(F32)
        up, down, proj, qkv_own = sums(grads[0], 1), sums(grads[1], 0), sums(grad_proj[0], 0), sums(grad_qkv[0], 0)
        norm_sum = jnp.concatenate([grad_norm1[:2], grad_norm2[:2]], axis=0)
        norm_sum = lax.psum(norm_sum, ("fsdp", "rep"))
    norm_grad = lax.dynamic_slice(norm_sum, (0, me * own), (4, own))
    return (block_output, input_grad, norm_grad, qkv_own.T, proj.T, up, down.T, *targets)


def solution(mesh):
    tokens = P(("fsdp", "rep"), None)
    columns = P(None, "fsdp")
    return jax.shard_map(
        partial(per_device, mesh.shape["fsdp"], mesh.shape["rep"]),
        mesh=mesh,
        in_specs=(tokens, P(("fsdp", "rep")), tokens) + (columns,) * 10,
        out_specs=(tokens, tokens) + (columns,) * 10,
        check_vma=False,
    )
```
